128 devices in a mesh: dp: 8 (over z, y_lo), neg: 16 (over x, y_hi, core).
Axes of the slice: x: 4, y: 4 (y_hi: 2, y_lo: 2; y = y_hi * 2 + y_lo), z: 4, core: 2. Of those that a mesh axis runs over, the one named last changes fastest.
Arguments:
- query_emb: bfloat16 [512, 32, 128], P(('dp', 'neg')), may hold values from -6 to 6
- positive: int32 [512], P(('dp', 'neg')), may hold values from 0 to 127
- passage_emb: bfloat16 [128, 512, 128], P(('dp', 'neg')), may hold values from -6 to 6
- lengths: int32 [128], P(('dp', 'neg')), may hold values from 256 to 512
- residual: bfloat16 [65536, 1024], P(('dp', 'neg')), may hold values from -6 to 6
- context: bfloat16 [65536, 1024], P(('dp', 'neg')), may hold values from -6 to 6
- out_proj: bfloat16 [1024, 1024], replicated, may hold values from -0.1875 to 0.1875
- norm_gain: float32 [1024], replicated, may hold values from 0.5 to 1.5
- colbert_proj: bfloat16 [1024, 128], replicated, may hold values from -0.1875 to 0.1875
Outputs:
- loss: float32 [], replicated
- query_grad: float32 [512, 32, 128], P(('dp', 'neg'))
- residual_grad: bfloat16 [65536, 1024], P(('dp', 'neg'))
- context_grad: bfloat16 [65536, 1024], P(('dp', 'neg'))
- out_proj_grad: float32 [1024, 1024], replicated
- colbert_grad: float32 [1024, 128], replicated
- gain_grad: float32 [1024], replicated
The draws below stay inside these ranges and needn't reach their ends.
Inputs may be any that keep to these rules, and one draw needn't show every extreme that they name: A passage's first lengths[p] token slots are real, the rest padding.
All inputs are finite; a program needn't handle non-finite values.
Results may differ from the reference program's by a relative error of at most 0.0065.
Values may be sent and summed in bfloat16 or wider, within the bound.
No kernel may reach another device: no remote copies, remote signals or barrier semaphores. Data moves between devices by JAX's collectives and lax.ppermute only.
A program may use at most 64 MiB of HBM per device.

```python
import jax
import jax.numpy as jnp
from jax import lax

D = 1024
DIM = 128
QLEN = 32
PLEN = 512
QUERIES = 512
PASSAGES = 128
ROWS = 65536


noise_level = 0.6


similar_gap = 9.5


def unit_rows(values):
    return values / jnp.sqrt(jnp.sum(values * values, axis=-1, keepdims=True))


def shared_parts(key):
    midpoint = DIM // 2
    first_half = (jnp.arange(DIM) < midpoint).astype(jnp.float32)
    second_half = 1.0 - first_half
    chosen = jax.random.randint(jax.random.fold_in(key, 101), (QUERIES,), 0, PASSAGES).astype(jnp.int32)
    directions = unit_rows(jax.random.normal(jax.random.fold_in(key, 102), (PASSAGES, DIM), jnp.float32) * first_half)
    query_common = unit_rows(jax.random.normal(jax.random.fold_in(key, 103), (DIM,), jnp.float32) * second_half)
    passage_common = unit_rows(jax.random.normal(jax.random.fold_in(key, 104), (DIM,), jnp.float32) * second_half)
    return (chosen, directions, query_common, passage_common, first_half, second_half)


def draw_positive(key, part):
    return shared_parts(key)[0]


def draw_query_emb(key, part):
    chosen, directions, query_common, passage_common, first_half, second_half = shared_parts(key)
    spread = noise_level * DIM ** (-0.25) * (second_half + 0.25 * first_half)
    noise_key = jax.random.fold_in(key, 201)
    noise = jax.random.normal(noise_key, (QUERIES, QLEN, DIM), jnp.float32)
    common = query_common
    aligned = similar_gap / QLEN * directions[chosen]
    values = noise * spread + common + aligned[:, None, :]
    return jnp.clip(values, -6.0, 6.0).astype(jnp.bfloat16)


def draw_passage_emb(key, part):
    chosen, directions, query_common, passage_common, first_half, second_half = shared_parts(key)
    spread = noise_level * DIM ** (-0.25)
    noise_key = jax.random.fold_in(key, 301)
    noise = jax.random.normal(noise_key, (PASSAGES, PLEN, DIM), jnp.float32)
    common = passage_common
    values = noise * spread + common + directions[:, None, :]
    return jnp.clip(values, -6.0, 6.0).astype(jnp.bfloat16)


def touch_ends(entries, key, least, high):
    index_at = [jax.random.randint(jax.random.fold_in(key, axis), (), 0, length) for axis, length in enumerate(entries.shape)]
    widest = entries.shape.index(max(entries.shape))
    beside = index_at[:widest] + [(index_at[widest] + 1) % entries.shape[widest]] + index_at[widest + 1:]
    return entries.at[tuple(index_at)].set(least).at[tuple(beside)].set(high)


def levels(key, extent, split, smallest, high):
    def one(position, parts):
        heights = jax.random.uniform(jax.random.fold_in(jax.random.fold_in(key, 6), position), (parts,), jnp.float32, smallest / len(split), high / len(split))
        return jnp.repeat(jnp.exp(heights), extent[position] // parts).reshape((-1,) + (1,) * (len(extent) - position - 1))

    loudness = one(*split[0])
    for cut in split[1:]:
        loudness = loudness * one(*cut)
    return loudness


def bell_draw(key, extent, scale, most, split=(), dtype=jnp.bfloat16):
    loudness = levels(key, extent, split, -0.22, 0.18) if split else 1.0
    entries = jax.random.normal(key, extent, jnp.float32) * scale * loudness
    return jnp.minimum(jnp.maximum(entries, -most), most).astype(dtype)


def setup_inputs(seed: int = 0) -> dict:
    key_list = jax.random.split(jax.random.key(seed), 10)
    query_emb = draw_query_emb(jax.random.fold_in(key_list[9], 71), 0)
    positive = draw_positive(jax.random.fold_in(key_list[9], 71), 0)
    passage_emb = draw_passage_emb(jax.random.fold_in(key_list[9], 71), 0)
    lengths = touch_ends(jax.random.randint(key_list[3], (PASSAGES,), PLEN // 2, PLEN + 1), jax.random.fold_in(key_list[3], 1), PLEN // 2, PLEN).astype(jnp.int32)
    residual = bell_draw(key_list[4], (ROWS, D), 1.0, 6.0, ((0, 128),))
    context = bell_draw(key_list[5], (ROWS, D), 1.0, 6.0, ((0, 128),))
    out_proj = bell_draw(key_list[6], (D, D), D ** -0.5, 0.1875)
    norm_gain = jnp.clip(1.0 + 0.1 * jax.random.normal(key_list[7], (D,), jnp.float32), 0.5, 1.5)
    colbert_proj = bell_draw(key_list[8], (D, DIM), D ** -0.5, 0.1875)
    return {"query_emb": query_emb, "positive": positive, "passage_emb": passage_emb, "lengths": lengths, "residual": residual, "context": context, "out_proj": out_proj, "norm_gain": norm_gain, "colbert_proj": colbert_proj}


def masked_scores(query_flat, passage_tokens, length):
    scores = jnp.dot(query_flat, passage_tokens.T, preferred_element_type=jnp.float32)
    usable = (jnp.arange(passage_tokens.shape[0]) < length)[None, :]
    return jnp.where(usable, scores, -1e+30)

def window_rows(running, inputs, out_proj, norm_gain, colbert_proj):
    resid_rows, context_rows, grad_rows = inputs
    hidden = resid_rows.astype(jnp.float32) + jnp.dot(context_rows, out_proj, preferred_element_type=jnp.float32)
    row_mean = lax.optimization_barrier(jnp.mean(hidden, axis=1, keepdims=True))
    centred = hidden - row_mean
    variance = lax.optimization_barrier(jnp.mean(centred * centred, axis=1, keepdims=True))
    inv_std = 1.0 / jnp.sqrt(variance + 1e-05)
    normed = centred * inv_std
    scaled = (normed * norm_gain).astype(jnp.bfloat16)
    colbert_part = jnp.dot(scaled.T, grad_rows, preferred_element_type=jnp.float32)
    scaled_grad = jnp.dot(grad_rows, colbert_proj.T, preferred_element_type=jnp.float32)
    gain_part = lax.optimization_barrier(jnp.sum(scaled_grad * normed, axis=0))
    gained = scaled_grad * norm_gain
    hidden_grad = (inv_std * (gained - lax.optimization_barrier(jnp.mean(gained, axis=1, keepdims=True)) - normed * lax.optimization_barrier(jnp.mean(gained * normed, axis=1, keepdims=True)))).astype(jnp.bfloat16)
    context_grad = jnp.dot(hidden_grad, out_proj.T, preferred_element_type=jnp.float32).astype(jnp.bfloat16)
    proj_part = jnp.dot(context_rows.T, hidden_grad, preferred_element_type=jnp.float32)
    running = (running[0] + proj_part, running[1] + colbert_part, running[2] + gain_part)
    return (running, (hidden_grad, context_grad))

def reference(query_emb, positive, passage_emb, lengths, residual, context, out_proj, norm_gain, colbert_proj):
    query_flat = query_emb.reshape(QUERIES * QLEN, DIM)

    def forward(inputs):
        passage_tokens, length = inputs
        masked = masked_scores(query_flat, passage_tokens, length)
        highest = lax.optimization_barrier(jnp.max(masked, axis=1, keepdims=True))
        inner_lse = highest[:, 0] + jnp.log(lax.optimization_barrier(jnp.sum(jnp.exp(masked - highest), axis=1)))
        shifted = inner_lse - jnp.log(length.astype(jnp.float32))
        return (inner_lse, lax.optimization_barrier(jnp.sum(shifted.reshape(QUERIES, QLEN), axis=1)))
    inner_all, similar = lax.map(forward, (passage_emb, lengths))
    similar = similar.T
    highest = lax.optimization_barrier(jnp.max(similar, axis=1, keepdims=True))
    log_total = highest[:, 0] + jnp.log(lax.optimization_barrier(jnp.sum(jnp.exp(similar - highest), axis=1)))
    is_positive = jnp.arange(PASSAGES).astype(jnp.int32)[None, :] == positive[:, None]
    positive_score = lax.optimization_barrier(jnp.sum(jnp.where(is_positive, similar, 0.0), axis=1))
    loss = jnp.mean(log_total - positive_score)
    coefficient = jnp.exp(similar - log_total[:, None]) - is_positive.astype(jnp.float32)

    def backward(running, inputs):
        passage_tokens, length, inner_lse, column = inputs
        masked = masked_scores(query_flat, passage_tokens, length)
        spread = jnp.exp(masked - inner_lse[:, None]).reshape(QUERIES, QLEN, PLEN)
        weight = (spread * column[:, None, None]).reshape(QUERIES * QLEN, PLEN).astype(jnp.bfloat16)
        running = running + jnp.dot(weight, passage_tokens, preferred_element_type=jnp.float32)
        passage_grad = jnp.dot(weight.T, query_flat, preferred_element_type=jnp.float32).astype(jnp.bfloat16)
        return (running, passage_grad)
    start = jnp.zeros((QUERIES * QLEN, DIM), jnp.float32)
    query_sum, emb_grad = lax.scan(backward, start, (passage_emb, lengths, inner_all, coefficient.T))
    query_grad = query_sum.reshape(QUERIES, QLEN, DIM)

    def window_step(running, inputs):
        return window_rows(running, inputs, out_proj, norm_gain, colbert_proj)
    begin = (jnp.zeros((D, D), jnp.float32), jnp.zeros((D, DIM), jnp.float32), jnp.zeros((D,), jnp.float32))
    sums, grads = lax.scan(window_step, begin, (residual.reshape(PASSAGES, PLEN, D), context.reshape(PASSAGES, PLEN, D), emb_grad))
    residual_grad = grads[0].reshape(ROWS, D)
    context_grad = grads[1].reshape(ROWS, D)
    return (loss, query_grad, residual_grad, context_grad, sums[0], sums[1], sums[2])
```

```python
import functools

import jax
import jax.numpy as jnp
from jax import lax
from jax.experimental import pallas as pl
from jax.experimental.pallas import tpu as pltpu
from jax.sharding import Mesh
from jax.sharding import PartitionSpec as P

DP = ("dp_0", "dp_1")
NEG = ("neg_0", "neg_1", "neg_2")
CROSS = ("neg_0", "neg_1")
CORE = "neg_2"
DP_NEG = DP + NEG
BF16 = jnp.bfloat16
F32 = jnp.float32
EXTRA = 8
LEAST = 256
MIB = 1 << 20


def dot(a, b, dims, precision=None):
    return lax.dot_general(a, b, (dims, ((), ())), precision=precision, preferred_element_type=F32)


def token_query(rows, queries, query_len, transposed=False):
    shape = (queries, rows) if transposed else (rows, queries)
    row = lax.broadcasted_iota(jnp.int32, shape, 1 if transposed else 0)
    query = lax.broadcasted_iota(jnp.int32, shape, 0 if transposed else 1)
    first = query * query_len
    return ((row >= first) & (row < first + query_len)).astype(F32)


def whole(shape):
    return pl.BlockSpec(shape, lambda *_: (0,) * len(shape))


def forward_kernel(
    query_len, group, q_ref, p_ref, ids_ref, exp_ref, mix_ref, inv_ref, sim_ref, stats_ref, lse_ref
):
    passage = pl.program_id(0)
    parts, q_rows, width = q_ref.shape[0], q_ref.shape[1] - EXTRA, q_ref.shape[2]
    slots = p_ref.shape[1] - EXTRA
    rows = parts * q_rows
    queries = rows // query_len
    tokens = p_ref[0, :slots, :]
    tokens_t = tokens.T
    length = p_ref[0, slots : slots + 1, :].astype(F32) + float(LEAST)
    chunk = group * q_rows
    wide = jnp.concatenate([length] * (chunk // width), axis=1)
    position = lax.broadcasted_iota(jnp.int32, (slots - LEAST, chunk), 0).astype(F32) + float(LEAST)
    usable = position < wide
    log_length = jnp.log(wide)

    steps = parts // group

    def scores(step):
        block = jnp.concatenate([q_ref[step * group + k, :q_rows, :] for k in range(group)], axis=0)
        return dot(tokens, block, ((1,), (1,)))

    ahead = scores(0)
    late = None
    for step in range(steps):
        now = ahead
        if step + 1 < steps:
            ahead = scores(step + 1)
        if late is not None:
            mix_ref[passage, :, pl.ds((step - 1) * chunk, chunk)] = dot(tokens_t, late, ((1,), (0,)))
        sure, rest = now[:LEAST], jnp.where(usable, now[LEAST:], -1e30)
        highest = jnp.max(sure, axis=0, keepdims=True)
        highest = jnp.maximum(highest, jnp.max(rest, axis=0, keepdims=True))
        sure = jnp.exp(sure - highest)
        rest = jnp.exp(rest - highest)
        total = jnp.sum(sure, axis=0, keepdims=True) + jnp.sum(rest, axis=0, keepdims=True)
        late = jnp.concatenate([sure.astype(BF16), rest.astype(BF16)], axis=0)
        at = pl.ds(step * chunk, chunk)
        exp_ref[passage, :, at] = late
        inv_ref[pl.ds(passage, 1), at] = 1.0 / total
        lse_ref[pl.ds(passage, 1), at] = highest + jnp.log(total) - log_length
    mix_ref[passage, :, pl.ds((steps - 1) * chunk, chunk)] = dot(tokens_t, late, ((1,), (0,)))

    @pl.when(passage == pl.num_programs(0) - 1)
    def _():
        similar = dot(
            lse_ref[...], token_query(rows, queries, query_len), ((1,), (0,)), lax.Precision.HIGHEST
        )
        wanted = jnp.sum(q_ref[:, q_rows, :].astype(F32), axis=0, keepdims=True)[:, :queries]
        hit = (wanted == ids_ref[:, :queries]).astype(F32)
        highest = jnp.max(similar, axis=0, keepdims=True)
        total = jnp.sum(jnp.exp(similar - highest), axis=0, keepdims=True)
        positive = jnp.sum(jnp.where(hit > 0.0, similar, 0.0), axis=0, keepdims=True)
        sim_ref[0] = similar
        sim_ref[1] = hit
        stats = jnp.concatenate(
            [highest, total, positive, jnp.zeros((5, queries), F32)], axis=0
        )
        stats = jnp.concatenate([stats, jnp.zeros((8, width - queries), F32)], axis=1)
        stats_ref[...] = jnp.broadcast_to(stats[None], stats_ref.shape)


def forward_tile(query_pack, passage_pack, ids, query_len, group=2):
    parts, q_rows, width = query_pack.shape
    q_rows -= EXTRA
    count, slots = passage_pack.shape[0], passage_pack.shape[1] - EXTRA
    rows = parts * q_rows
    queries = rows // query_len
    work = rows * slots * count
    return pl.pallas_call(
        functools.partial(forward_kernel, query_len, group),
        name="forward_tile",
        grid=(count,),
        in_specs=[
            whole(query_pack.shape),
            pl.BlockSpec((1, slots + EXTRA, width), lambda p: (p, 0, 0)),
            whole(ids.shape),
        ],
        out_specs=[
            pl.BlockSpec(memory_space=pltpu.VMEM),
            pl.BlockSpec(memory_space=pltpu.VMEM),
            whole((count, rows)),
            whole((2, count, queries)),
            whole((parts, 8, width)),
        ],
        out_shape=[
            pltpu.VMEM((count, slots, rows), BF16),
            pltpu.VMEM((count, width, rows), F32),
            jax.ShapeDtypeStruct((count, rows), F32),
            jax.ShapeDtypeStruct((2, count, queries), F32),
            jax.ShapeDtypeStruct((parts, 8, width), F32),
        ],
        scratch_shapes=[pltpu.VMEM((count, rows), F32)],
        compiler_params=pltpu.CompilerParams(vmem_limit_bytes=20 * MIB),
        cost_estimate=pl.CostEstimate(
            flops=4 * work * width, transcendentals=work, bytes_accessed=4 * work
        ),
    )(query_pack, passage_pack, ids)


def backward_kernel(
    query_len, q_ref, exp_ref, mix_ref, inv_ref, sim_ref, stats_ref, pg_ref, qg_ref, qt, scale, sums
):
    passage = pl.program_id(0)
    parts, q_rows, width = q_ref.shape[0], q_ref.shape[1] - EXTRA, q_ref.shape[2]
    slots = exp_ref.shape[1]
    rows = parts * q_rows
    queries = rows // query_len

    @pl.when(passage == 0)
    def _():
        highest_of = stats_ref[:, 0, :queries]
        highest = jnp.max(highest_of, axis=0, keepdims=True)
        total = jnp.sum(
            stats_ref[:, 1, :queries] * jnp.exp(highest_of - highest), axis=0, keepdims=True
        )
        positive = jnp.sum(stats_ref[:, 2, :queries], axis=0, keepdims=True)
        log_total = highest + jnp.log(total)
        coefficient = jnp.exp(sim_ref[0] - log_total) - sim_ref[1]
        spread = dot(
            coefficient,
            token_query(rows, queries, query_len, True),
            ((1,), (0,)),
            lax.Precision.HIGHEST,
        )
        scale[...] = spread * inv_ref[...]
        loss = jnp.broadcast_to(
            jnp.sum(log_total - positive, axis=1, keepdims=True), (EXTRA, width)
        )
        high = loss.astype(BF16).astype(F32)
        low = (loss - high).astype(BF16).astype(F32)
        last = loss - high - low
        row = lax.broadcasted_iota(jnp.int32, (EXTRA, width), 0)
        lines = jnp.where(row == 0, high, jnp.where(row == 1, low, jnp.where(row == 2, last, 0.0)))
        for k in range(pg_ref.shape[0]):
            pg_ref[k, slots:, :] = lines.astype(BF16)
        for k in range(parts):
            qt[:, k * q_rows : (k + 1) * q_rows] = q_ref[k, :q_rows, :].T
        sums[...] = jnp.zeros_like(sums)

    factor = scale[pl.ds(passage, 1), :]
    weighted = (qt[...].astype(F32) * factor).astype(BF16)
    grad_t = dot(weighted, exp_ref[passage], ((1,), (1,)))
    pg_ref[passage, :slots, :] = grad_t.T.astype(BF16)
    sums[...] += mix_ref[passage] * factor

    @pl.when(passage == pl.num_programs(0) - 1)
    def _():
        for k in range(parts):
            qg_ref[k % 2, k // 2] = sums[:, k * q_rows : (k + 1) * q_rows].T.astype(BF16)


def backward_tile(query_pack, spread, mixed, inverse, similar, stats, query_len):
    parts, q_rows, width = query_pack.shape
    q_rows -= EXTRA
    count, slots, rows = spread.shape
    work = rows * slots * count
    return pl.pallas_call(
        functools.partial(backward_kernel, query_len),
        name="backward_tile",
        grid=(count,),
        in_specs=[
            whole(query_pack.shape),
            pl.BlockSpec(memory_space=pltpu.VMEM),
            pl.BlockSpec(memory_space=pltpu.VMEM),
            whole(inverse.shape),
            whole(similar.shape),
            whole(stats.shape),
        ],
        out_specs=[whole((count, slots + EXTRA, width)), whole((2, parts // 2, q_rows, width))],
        out_shape=[
            jax.ShapeDtypeStruct((count, slots + EXTRA, width), BF16),
            jax.ShapeDtypeStruct((2, parts // 2, q_rows, width), BF16),
        ],
        scratch_shapes=[
            pltpu.VMEM((width, rows), BF16),
            pltpu.VMEM((count, rows), F32),
            pltpu.VMEM((width, rows), F32),
        ],
        compiler_params=pltpu.CompilerParams(vmem_limit_bytes=20 * MIB),
        cost_estimate=pl.CostEstimate(
            flops=2 * work * width, transcendentals=0, bytes_accessed=3 * work
        ),
    )(query_pack, spread, mixed, inverse, similar, stats)


def early_kernel(resid_ref, context_ref, proj_ref, normed_ref, inv_ref, context_t_ref):
    context = context_ref[...]
    hidden = resid_ref[...].astype(F32) + dot(context, proj_ref[...], ((1,), (0,)))
    centred = hidden - jnp.mean(hidden, axis=1, keepdims=True)
    variance = jnp.mean(centred * centred, axis=1, keepdims=True)
    inv_std = 1.0 / jnp.sqrt(variance + 1e-05)
    normed_ref[...] = centred * inv_std
    inv_ref[...] = jnp.broadcast_to(inv_std, inv_ref.shape)
    context_t_ref[...] = context.T


def early_rows(residual, context, out_proj, block=128):
    rows, width = residual.shape
    return pl.pallas_call(
        early_kernel,
        name="early_rows",
        grid=(rows // block,),
        in_specs=[
            pl.BlockSpec((block, width), lambda r: (r, 0)),
            pl.BlockSpec((block, width), lambda r: (r, 0)),
            whole(out_proj.shape),
        ],
        out_specs=[
            pl.BlockSpec((block, width), lambda r: (r, 0)),
            pl.BlockSpec((block, 128), lambda r: (r, 0)),
            pl.BlockSpec((width, block), lambda r: (0, r)),
        ],
        out_shape=[
            jax.ShapeDtypeStruct((rows, width), F32),
            jax.ShapeDtypeStruct((rows, 128), F32),
            jax.ShapeDtypeStruct((width, rows), BF16),
        ],
        compiler_params=pltpu.CompilerParams(vmem_limit_bytes=24 * MIB),
        cost_estimate=pl.CostEstimate(
            flops=2 * rows * width * width, transcendentals=0, bytes_accessed=10 * rows * width
        ),
    )(residual, context, out_proj)


def late_kernel(
    parts_ref, normed_ref, inv_ref, gain_ref, colbert_ref, context_t_ref, resid_ref, sums_ref, loss_ref
):
    slots = parts_ref.shape[1] - EXTRA
    count = parts_ref.shape[0]
    width = normed_ref.shape[1]
    total = parts_ref[0].astype(F32)
    for k in range(1, count):
        total = total + parts_ref[k].astype(F32)
    loss_ref[...] = jnp.broadcast_to(
        jnp.sum(total[slots:], axis=0, keepdims=True), loss_ref.shape
    )
    grad = total[:slots].astype(BF16)
    normed = normed_ref[...]
    gain = gain_ref[...]
    inv_std = inv_ref[:, :1]
    gained = dot(grad, colbert_ref[...], ((1,), (1,))) * gain
    resid = inv_std * (
        gained
        - jnp.mean(gained, axis=1, keepdims=True)
        - normed * jnp.mean(gained * normed, axis=1, keepdims=True)
    )
    resid = resid.astype(BF16)
    resid_ref[...] = resid
    scaled = (normed * gain).astype(BF16)
    sums_ref[width:, :] = dot(grad.T, scaled, ((1,), (0,))).astype(BF16)
    step = 256
    for k in range(width // step):
        sums_ref[k * step : (k + 1) * step, :] = dot(
            context_t_ref[k * step : (k + 1) * step, :], resid, ((1,), (0,))
        ).astype(BF16)


def late_rows(pieces, normed, inv_std, gain, colbert_proj, context_t):
    rows, width = normed.shape
    emb = colbert_proj.shape[1]
    return pl.pallas_call(
        late_kernel,
        name="late_rows",
        out_shape=[
            jax.ShapeDtypeStruct((rows, width), BF16),
            jax.ShapeDtypeStruct((width + emb, width), BF16),
            jax.ShapeDtypeStruct((8, emb), F32),
        ],
        compiler_params=pltpu.CompilerParams(vmem_limit_bytes=40 * MIB),
        cost_estimate=pl.CostEstimate(
            flops=2 * rows * width * (width + 2 * emb),
            transcendentals=0,
            bytes_accessed=14 * rows * width,
        ),
    )(pieces, normed, inv_std, gain, colbert_proj, context_t)


def exchange(pieces, axis):
    return lax.all_to_all(pieces, axis, 0, 0, tiled=True)


def to_everyone(array, axis):
    size = lax.axis_size(axis)
    return exchange(jnp.broadcast_to(array[None], (size, *array.shape)), axis)


def summed(pieces):
    return jnp.sum(pieces.astype(F32), axis=0).astype(BF16)


def finish_kernel(core_ref, half_ref, other_ref, colbert_ref, gain_ref, proj_ref, grad_ref, gain_grad_ref):
    rows = half_ref.shape[0]
    top = proj_ref.shape[0] - rows
    even = core_ref[0] == 0
    half, other = half_ref[...], other_ref[...]
    proj_ref[:rows, :] = jnp.where(even, half, other).astype(F32)
    second = jnp.where(even, other, half).astype(F32)
    proj_ref[rows:, :] = second[:top]
    colbert_grad = second[top:]
    colbert_t = colbert_ref[...].astype(F32).T
    gain_grad_ref[...] = (
        jnp.sum(colbert_grad * colbert_t, axis=0, keepdims=True) / gain_ref[...]
    )
    grad_ref[...] = colbert_grad.T


def finish(core, half, other, colbert_proj, gain, block=256):
    rows, width = half.shape
    emb = colbert_proj.shape[1]
    return pl.pallas_call(
        finish_kernel,
        name="finish",
        grid=(width // block,),
        in_specs=[
            pl.BlockSpec(memory_space=pltpu.SMEM),
            pl.BlockSpec((rows, block), lambda k: (0, k)),
            pl.BlockSpec((rows, block), lambda k: (0, k)),
            pl.BlockSpec((block, emb), lambda k: (k, 0)),
            pl.BlockSpec((1, block), lambda k: (0, k)),
        ],
        out_specs=[
            pl.BlockSpec((2 * rows - emb, block), lambda k: (0, k)),
            pl.BlockSpec((block, emb), lambda k: (k, 0)),
            pl.BlockSpec((1, block), lambda k: (0, k)),
        ],
        out_shape=[
            jax.ShapeDtypeStruct((2 * rows - emb, width), F32),
            jax.ShapeDtypeStruct((width, emb), F32),
            jax.ShapeDtypeStruct((1, width), F32),
        ],
        compiler_params=pltpu.CompilerParams(vmem_limit_bytes=24 * MIB),
        cost_estimate=pl.CostEstimate(
            flops=4 * rows * width, transcendentals=0, bytes_accessed=16 * rows * width
        ),
    )(core[None], half, other, colbert_proj, gain)


def core_halves(halves, core):
    given = lax.dynamic_index_in_dim(halves, 1 - core, 0, False)
    kept = lax.dynamic_index_in_dim(halves, core, 0, False)
    taken = lax.ppermute(given, CORE, [(0, 1), (1, 0)])
    return (kept.astype(F32) + taken.astype(F32)).astype(BF16)


def body(
    query_emb, positive, passage_emb, lengths, residual, context, out_proj, norm_gain, colbert_proj
):
    query_dev, query_len, emb = query_emb.shape
    neg_size, dp_size, cross_size = lax.axis_size(NEG), lax.axis_size(DP), lax.axis_size(CROSS)
    place, core = lax.axis_index(NEG), lax.axis_index(CORE)
    width = out_proj.shape[0]
    spot = jnp.arange(emb)[None] - place * query_dev
    wanted = jnp.sum(
        jnp.where(spot == jnp.arange(query_dev)[:, None], positive[:, None], 0), axis=0
    )
    query_own = jnp.concatenate(
        [
            query_emb.reshape(query_dev * query_len, emb),
            jnp.broadcast_to(wanted.astype(BF16)[None], (EXTRA, emb)),
        ]
    )
    passage_own = jnp.concatenate(
        [
            passage_emb.reshape(-1, emb),
            jnp.broadcast_to((lengths - LEAST).astype(BF16)[:, None], (EXTRA, emb)),
        ]
    )
    query_pack = lax.all_gather(query_own, NEG)
    passage_pack = to_everyone(passage_own, DP)
    ids = jnp.broadcast_to(
        (jnp.arange(dp_size) * neg_size + place).astype(F32)[:, None], (dp_size, emb)
    )
    early = early_rows(residual, context, out_proj)
    (query_pack, passage_pack), early = lax.optimization_barrier(
        ((query_pack, passage_pack), early)
    )
    normed, inv_std, context_t = early
    spread, mixed, inverse, similar, stats = forward_tile(query_pack, passage_pack, ids, query_len)
    stats = exchange(stats, NEG)
    passage_parts, query_parts = backward_tile(
        query_pack, spread, mixed, inverse, similar, stats, query_len
    )
    query_half = core_halves(query_parts, core)
    passage_parts = exchange(passage_parts, DP)
    passage_parts, query_half = lax.optimization_barrier((passage_parts, query_half))
    residual_grad, partial, loss_sum = late_rows(
        passage_parts, normed, inv_std, norm_gain[None], colbert_proj, context_t
    )
    half = core_halves(partial.reshape(2, -1, width), core)
    context_grad = jnp.dot(residual_grad, out_proj.T, preferred_element_type=F32).astype(BF16)
    slabs = exchange(half.reshape(dp_size, -1, width), DP)
    slabs, context_grad = lax.optimization_barrier((slabs, context_grad))
    slab = summed(slabs)
    lines = slab.shape[0]
    tiles = slab.reshape(lines, cross_size, -1).swapaxes(0, 1)
    tiles = exchange(jnp.concatenate([tiles, query_half], axis=1), CROSS)
    tile = jnp.sum(tiles.astype(F32), axis=0)
    query_grad = tile[lines:].reshape(query_dev, query_len, emb)
    slab = to_everyone(tile[:lines].astype(BF16), CROSS).swapaxes(0, 1).reshape(lines, width)
    half = to_everyone(slab, DP).reshape(-1, width)
    other = lax.ppermute(half, CORE, [(0, 1), (1, 0)])
    out_proj_grad, colbert_grad, gain_grad = finish(
        core, half, other, colbert_proj, norm_gain[None]
    )
    loss = loss_sum[0, 0] / (query_dev * dp_size * neg_size)
    return (
        loss,
        query_grad,
        residual_grad,
        context_grad,
        out_proj_grad,
        colbert_grad,
        gain_grad[0],
    )


def solution(mesh):
    split = Mesh(mesh.devices.reshape(mesh.shape["dp"] // 2, 2, 4, 2, 2), DP_NEG)
    placed = (
        P(DP_NEG, None, None),
        P(DP_NEG),
        P(DP_NEG, None, None),
        P(DP_NEG),
        P(DP_NEG, None),
        P(DP_NEG, None),
        P(),
        P(),
        P(),
    )
    return jax.shard_map(
        body,
        mesh=split,
        in_specs=placed,
        out_specs=(P(), P(DP_NEG, None, None), P(DP_NEG, None), P(DP_NEG, None), P(), P(), P()),
        check_vma=False,
    )
```

```python
import functools

import jax
import jax.numpy as jnp
from jax import lax
from jax.experimental import pallas as pl
from jax.experimental.pallas import tpu as pltpu
from jax.sharding import Mesh
from jax.sharding import PartitionSpec as P

DP = ("dp_0", "dp_1")
NEG = ("neg_0", "neg_1", "neg_2")
CROSS = ("neg_0", "neg_1")
CORE = "neg_2"
DP_NEG = DP + NEG
BF16 = jnp.bfloat16
F32 = jnp.float32
EXTRA = 8
LEAST = 256
MIB = 1 << 20


def dot(a, b, dims, precision=None):
    return lax.dot_general(a, b, (dims, ((), ())), precision=precision, preferred_element_type=F32)


def token_query(rows, queries, query_len, transposed=False):
    shape = (queries, rows) if transposed else (rows, queries)
    row = lax.broadcasted_iota(jnp.int32, shape, 1 if transposed else 0)
    query = lax.broadcasted_iota(jnp.int32, shape, 0 if transposed else 1)
    first = query * query_len
    return ((row >= first) & (row < first + query_len)).astype(F32)


def whole(shape):
    return pl.BlockSpec(shape, lambda *_: (0,) * len(shape))


def forward_kernel(
    query_len, group, flip_ref, q_ref, p_ref, ids_ref, exp_ref, mix_ref, inv_ref, sim_ref, stats_ref, lse_ref
):
    passage = pl.program_id(0)
    parts, q_rows, width = q_ref.shape[0], q_ref.shape[1] - EXTRA, q_ref.shape[2]
    slots = p_ref.shape[1] - EXTRA
    rows = parts * q_rows
    queries = rows // query_len
    flip = flip_ref[0]
    tokens = p_ref[0, :slots, :]
    tokens_t = tokens.T
    length = p_ref[0, slots : slots + 1, :].astype(F32) + float(LEAST)
    chunk = group * q_rows
    wide = jnp.concatenate([length] * (chunk // width), axis=1)
    position = lax.broadcasted_iota(jnp.int32, (slots - LEAST, chunk), 0).astype(F32) + float(LEAST)
    usable = position < wide
    log_length = jnp.log(wide)

    steps = parts // group

    def scores(step):
        block = jnp.concatenate([q_ref[(step * group + k) ^ flip, :q_rows, :] for k in range(group)], axis=0)
        return dot(tokens, block, ((1,), (1,)))

    ahead = scores(0)
    late = None
    for step in range(steps):
        now = ahead
        if step + 1 < steps:
            ahead = scores(step + 1)
        if late is not None:
            mix_ref[passage, :, pl.ds((step - 1) * chunk, chunk)] = dot(tokens_t, late, ((1,), (0,)))
        sure, rest = now[:LEAST], jnp.where(usable, now[LEAST:], -1e30)
        highest = jnp.max(sure, axis=0, keepdims=True)
        highest = jnp.maximum(highest, jnp.max(rest, axis=0, keepdims=True))
        sure = jnp.exp(sure - highest)
        rest = jnp.exp(rest - highest)
        total = jnp.sum(sure, axis=0, keepdims=True) + jnp.sum(rest, axis=0, keepdims=True)
        late = jnp.concatenate([sure.astype(BF16), rest.astype(BF16)], axis=0)
        at = pl.ds(step * chunk, chunk)
        exp_ref[passage, :, at] = late
        inv_ref[pl.ds(passage, 1), at] = 1.0 / total
        lse_ref[pl.ds(passage, 1), at] = highest + jnp.log(total) - log_length
    mix_ref[passage, :, pl.ds((steps - 1) * chunk, chunk)] = dot(tokens_t, late, ((1,), (0,)))

    @pl.when(passage == pl.num_programs(0) - 1)
    def _():
        similar = dot(
            lse_ref[...], token_query(rows, queries, query_len), ((1,), (0,)), lax.Precision.HIGHEST
        )
        wanted = jnp.sum(q_ref[:, q_rows, :].astype(F32), axis=0, keepdims=True)[:, :queries]
        hit = (wanted == ids_ref[:, :queries]).astype(F32)
        highest = jnp.max(similar, axis=0, keepdims=True)
        total = jnp.sum(jnp.exp(similar - highest), axis=0, keepdims=True)
        positive = jnp.sum(jnp.where(hit > 0.0, similar, 0.0), axis=0, keepdims=True)
        sim_ref[0] = similar
        sim_ref[1] = hit
        stats = jnp.concatenate(
            [highest, total, positive, jnp.zeros((5, queries), F32)], axis=0
        )
        stats = jnp.concatenate([stats, jnp.zeros((8, width - queries), F32)], axis=1)
        stats_ref[...] = jnp.broadcast_to(stats[None], stats_ref.shape)


def forward_tile(flip, query_pack, passage_pack, ids, query_len, group=4):
    parts, q_rows, width = query_pack.shape
    q_rows -= EXTRA
    count, slots = passage_pack.shape[0], passage_pack.shape[1] - EXTRA
    rows = parts * q_rows
    queries = rows // query_len
    work = rows * slots * count
    return pl.pallas_call(
        functools.partial(forward_kernel, query_len, group),
        name="forward_tile",
        grid=(count,),
        in_specs=[
            pl.BlockSpec(memory_space=pltpu.SMEM),
            whole(query_pack.shape),
            pl.BlockSpec((1, slots + EXTRA, width), lambda p: (p, 0, 0)),
            whole(ids.shape),
        ],
        out_specs=[
            pl.BlockSpec(memory_space=pltpu.VMEM),
            pl.BlockSpec(memory_space=pltpu.VMEM),
            whole((count, rows)),
            whole((2, count, queries)),
            whole((parts, 8, width)),
        ],
        out_shape=[
            pltpu.VMEM((count, slots, rows), BF16),
            pltpu.VMEM((count, width, rows), F32),
            jax.ShapeDtypeStruct((count, rows), F32),
            jax.ShapeDtypeStruct((2, count, queries), F32),
            jax.ShapeDtypeStruct((parts, 8, width), F32),
        ],
        scratch_shapes=[pltpu.VMEM((count, rows), F32)],
        compiler_params=pltpu.CompilerParams(vmem_limit_bytes=12 * MIB),
        cost_estimate=pl.CostEstimate(
            flops=4 * work * width, transcendentals=work, bytes_accessed=4 * work
        ),
    )(flip, query_pack, passage_pack, ids)


def backward_kernel(
    query_len, flip_ref, q_ref, exp_ref, mix_ref, inv_ref, sim_ref, stats_ref, pg_ref, qg_ref, qt, scale, sums
):
    passage = pl.program_id(0)
    parts, q_rows, width = q_ref.shape[0], q_ref.shape[1] - EXTRA, q_ref.shape[2]
    slots = exp_ref.shape[1]
    rows = parts * q_rows
    queries = rows // query_len

    @pl.when(passage == 0)
    def _():
        highest_of = stats_ref[:, 0, :queries]
        highest = jnp.max(highest_of, axis=0, keepdims=True)
        total = jnp.sum(
            stats_ref[:, 1, :queries] * jnp.exp(highest_of - highest), axis=0, keepdims=True
        )
        positive = jnp.sum(stats_ref[:, 2, :queries], axis=0, keepdims=True)
        log_total = highest + jnp.log(total)
        coefficient = jnp.exp(sim_ref[0] - log_total) - sim_ref[1]
        spread = dot(
            coefficient,
            token_query(rows, queries, query_len, True),
            ((1,), (0,)),
            lax.Precision.HIGHEST,
        )
        scale[...] = spread * inv_ref[...]
        loss = jnp.broadcast_to(
            jnp.sum(log_total - positive, axis=1, keepdims=True), (EXTRA, width)
        )
        high = loss.astype(BF16).astype(F32)
        low = (loss - high).astype(BF16).astype(F32)
        last = loss - high - low
        row = lax.broadcasted_iota(jnp.int32, (EXTRA, width), 0)
        lines = jnp.where(row == 0, high, jnp.where(row == 1, low, jnp.where(row == 2, last, 0.0)))
        for k in range(pg_ref.shape[0]):
            pg_ref[k, slots:, :] = lines.astype(BF16)
        for k in range(parts):
            qt[:, k * q_rows : (k + 1) * q_rows] = q_ref[k ^ flip_ref[0], :q_rows, :].T
        sums[...] = jnp.zeros_like(sums)

    factor = scale[pl.ds(passage, 1), :]
    weighted = (qt[...].astype(F32) * factor).astype(BF16)
    grad_t = dot(weighted, exp_ref[passage], ((1,), (1,)))
    pg_ref[passage, :slots, :] = grad_t.T.astype(BF16)
    sums[...] += mix_ref[passage] * factor

    @pl.when(passage == pl.num_programs(0) - 1)
    def _():
        for k in range(parts):
            qg_ref[k % 2, k // 2 % 2, k // 4] = sums[:, k * q_rows : (k + 1) * q_rows].T.astype(BF16)


def backward_tile(flip, query_pack, spread, mixed, inverse, similar, stats, query_len):
    parts, q_rows, width = query_pack.shape
    q_rows -= EXTRA
    count, slots, rows = spread.shape
    work = rows * slots * count
    return pl.pallas_call(
        functools.partial(backward_kernel, query_len),
        name="backward_tile",
        grid=(count,),
        in_specs=[
            pl.BlockSpec(memory_space=pltpu.SMEM),
            whole(query_pack.shape),
            pl.BlockSpec(memory_space=pltpu.VMEM),
            pl.BlockSpec(memory_space=pltpu.VMEM),
            whole(inverse.shape),
            whole(similar.shape),
            whole(stats.shape),
        ],
        out_specs=[whole((count, slots + EXTRA, width)), whole((2, 2, parts // 4, q_rows, width))],
        out_shape=[
            pltpu.HBM((count, slots + EXTRA, width), BF16),
            pltpu.HBM((2, 2, parts // 4, q_rows, width), BF16),
        ],
        scratch_shapes=[
            pltpu.VMEM((width, rows), BF16),
            pltpu.VMEM((count, rows), F32),
            pltpu.VMEM((width, rows), F32),
        ],
        compiler_params=pltpu.CompilerParams(vmem_limit_bytes=12 * MIB),
        cost_estimate=pl.CostEstimate(
            flops=2 * work * width, transcendentals=0, bytes_accessed=3 * work
        ),
    )(flip, query_pack, spread, mixed, inverse, similar, stats)


def early_kernel(resid_ref, context_ref, proj_ref, normed_ref, inv_ref, context_t_ref):
    context = context_ref[...]
    hidden = resid_ref[...].astype(F32) + dot(context, proj_ref[...], ((1,), (0,)))
    centred = hidden - jnp.mean(hidden, axis=1, keepdims=True)
    variance = jnp.mean(centred * centred, axis=1, keepdims=True)
    inv_std = 1.0 / jnp.sqrt(variance + 1e-05)
    normed_ref[...] = centred * inv_std
    inv_ref[...] = jnp.broadcast_to(inv_std, inv_ref.shape)
    context_t_ref[...] = context.T


def early_rows(residual, context, out_proj, block=128):
    rows, width = residual.shape
    return pl.pallas_call(
        early_kernel,
        name="early_rows",
        grid=(rows // block,),
        in_specs=[
            pl.BlockSpec((block, width), lambda r: (r, 0)),
            pl.BlockSpec((block, width), lambda r: (r, 0)),
            whole(out_proj.shape),
        ],
        out_specs=[
            pl.BlockSpec((block, width), lambda r: (r, 0)),
            pl.BlockSpec((block, 128), lambda r: (r, 0)),
            pl.BlockSpec((width, block), lambda r: (0, r)),
        ],
        out_shape=[
            pltpu.HBM((rows, width), F32),
            pltpu.HBM((rows, 128), F32),
            pltpu.HBM((width, rows), BF16),
        ],
        compiler_params=pltpu.CompilerParams(vmem_limit_bytes=10 * MIB),
        cost_estimate=pl.CostEstimate(
            flops=2 * rows * width * width, transcendentals=0, bytes_accessed=10 * rows * width
        ),
    )(residual, context, out_proj)


def late_kernel(
    parts_ref,
    normed_far,
    inv_far,
    gain_ref,
    colbert_ref,
    context_far,
    resid_ref,
    sums_ref,
    loss_ref,
    normed_ref,
    inv_ref,
    context_t_ref,
    sems,
):
    loads = [
        pltpu.make_async_copy(far, near, sems.at[k])
        for k, (far, near) in enumerate(
            ((normed_far, normed_ref), (inv_far, inv_ref), (context_far, context_t_ref))
        )
    ]
    for load in loads:
        load.start()
    slots = parts_ref.shape[1] - EXTRA
    count = parts_ref.shape[0]
    width = normed_ref.shape[1]
    total = parts_ref[0].astype(F32)
    for k in range(1, count):
        total = total + parts_ref[k].astype(F32)
    loss_ref[...] = jnp.broadcast_to(
        jnp.sum(total[slots:], axis=0, keepdims=True), loss_ref.shape
    )
    grad = total[:slots].astype(BF16)
    gain = gain_ref[...]
    gained = dot(grad, colbert_ref[...], ((1,), (1,))) * gain
    grad_t = grad.T
    for load in loads[:2]:
        load.wait()
    normed = normed_ref[...]
    inv_std = inv_ref[:, :1]
    resid = inv_std * (
        gained
        - jnp.mean(gained, axis=1, keepdims=True)
        - normed * jnp.mean(gained * normed, axis=1, keepdims=True)
    )
    resid = resid.astype(BF16)
    resid_ref[...] = resid
    scaled = (normed * gain).astype(BF16)
    blocks, lines = sums_ref.shape[1], sums_ref.shape[3]
    thin = grad.shape[1] // (2 * blocks)
    thick = lines - thin
    colbert = dot(grad_t, scaled, ((1,), (0,)))
    for k in range(2 * blocks):
        for j in range(width // 128):
            sums_ref[k // blocks, k % blocks, j, thick:, :] = colbert[
                k * thin : (k + 1) * thin, j * 128 : (j + 1) * 128
            ].astype(BF16)
    loads[2].wait()
    group = 4
    for first in range(0, 2 * blocks, group):
        part = dot(
            context_t_ref[first * thick : (first + group) * thick, :], resid, ((1,), (0,))
        ).astype(BF16)
        for k in range(first, first + group):
            at = (k - first) * thick
            for j in range(width // 128):
                sums_ref[k // blocks, k % blocks, j, :thick, :] = part[
                    at : at + thick, j * 128 : (j + 1) * 128
                ]


def far(array):
    return pltpu.with_memory_space_constraint(array, pltpu.HBM)


def late_rows(blocks, pieces, normed, inv_std, gain, colbert_proj, context_t):
    rows, width = normed.shape
    emb = colbert_proj.shape[1]
    return pl.pallas_call(
        late_kernel,
        name="late_rows",
        in_specs=[
            whole(pieces.shape),
            pl.BlockSpec(memory_space=pltpu.HBM),
            pl.BlockSpec(memory_space=pltpu.HBM),
            whole(gain.shape),
            whole(colbert_proj.shape),
            pl.BlockSpec(memory_space=pltpu.HBM),
        ],
        scratch_shapes=[
            pltpu.VMEM(normed.shape, F32),
            pltpu.VMEM(inv_std.shape, F32),
            pltpu.VMEM(context_t.shape, BF16),
            pltpu.SemaphoreType.DMA((3,)),
        ],
        out_shape=[
            jax.ShapeDtypeStruct((rows, width), BF16),
            jax.ShapeDtypeStruct(
                (2, blocks, width // 128, (width + emb) // (2 * blocks), 128), BF16
            ),
            jax.ShapeDtypeStruct((8, emb), F32),
        ],
        compiler_params=pltpu.CompilerParams(vmem_limit_bytes=24 * MIB),
        cost_estimate=pl.CostEstimate(
            flops=2 * rows * width * (width + 2 * emb),
            transcendentals=0,
            bytes_accessed=14 * rows * width,
        ),
    )(pieces, far(normed), far(inv_std), gain, colbert_proj, far(context_t))


def exchange(pieces, axis):
    return lax.all_to_all(pieces, axis, 0, 0, tiled=True)


def to_everyone(array, axis):
    size = lax.axis_size(axis)
    return exchange(jnp.broadcast_to(array[None], (size, *array.shape)), axis)


def summed(pieces):
    return jnp.sum(pieces.astype(F32), axis=0).astype(BF16)


def finish_kernel(core_ref, half_ref, other_ref, colbert_ref, gain_ref, proj_ref, grad_ref, gain_grad_ref):
    blocks, lines = half_ref.shape[0], half_ref.shape[2]
    thick = proj_ref.shape[0] // (2 * blocks)
    even = core_ref[0] == 0
    thin = []
    for part in range(2):
        for k in range(blocks):
            half, other = half_ref[k, 0].astype(F32), other_ref[k, 0].astype(F32)
            piece = jnp.where(even, half, other) if part == 0 else jnp.where(even, other, half)
            at = (part * blocks + k) * thick
            proj_ref[at : at + thick, :] = piece[:thick]
            thin.append(piece[thick:])
    colbert_grad = jnp.concatenate(thin, axis=0)
    colbert_t = colbert_ref[...].astype(F32).T
    gain_grad_ref[...] = (
        jnp.sum(colbert_grad * colbert_t, axis=0, keepdims=True) / gain_ref[...]
    )
    grad_ref[...] = colbert_grad.T


def finish(core, half, other, colbert_proj, gain):
    blocks, columns, lines, block = half.shape
    width, emb = colbert_proj.shape
    return pl.pallas_call(
        finish_kernel,
        name="finish",
        grid=(columns,),
        in_specs=[
            pl.BlockSpec(memory_space=pltpu.SMEM),
            pl.BlockSpec((blocks, 1, lines, block), lambda k: (0, k, 0, 0)),
            pl.BlockSpec((blocks, 1, lines, block), lambda k: (0, k, 0, 0)),
            pl.BlockSpec((block, emb), lambda k: (k, 0)),
            pl.BlockSpec((1, block), lambda k: (0, k)),
        ],
        out_specs=[
            pl.BlockSpec((width, block), lambda k: (0, k)),
            pl.BlockSpec((block, emb), lambda k: (k, 0)),
            pl.BlockSpec((1, block), lambda k: (0, k)),
        ],
        out_shape=[
            jax.ShapeDtypeStruct((width, width), F32),
            jax.ShapeDtypeStruct((width, emb), F32),
            jax.ShapeDtypeStruct((1, width), F32),
        ],
        compiler_params=pltpu.CompilerParams(vmem_limit_bytes=16 * MIB),
        cost_estimate=pl.CostEstimate(
            flops=4 * width * width, transcendentals=0, bytes_accessed=8 * width * width
        ),
    )(core, half, other, colbert_proj, gain)


SWAP = [(0, 1), (1, 0)]


def halves_summed(halves, axis, pairs, side, out_type):
    given = lax.dynamic_index_in_dim(halves, 1 - side, 0, False)
    kept = lax.dynamic_index_in_dim(halves, side, 0, False)
    taken = lax.ppermute(given, axis, pairs)
    return (kept.astype(F32) + taken.astype(F32)).astype(out_type)


def crossed(parts, row, column):
    parts = halves_summed(parts, "neg_1", SWAP, row, F32)
    far, near = column // 2, column % 2
    parts = parts.reshape(2, 2, *parts.shape[1:])
    parts = halves_summed(parts, "neg_0", [(k, k ^ 2) for k in range(4)], far, F32)
    return halves_summed(parts, "neg_0", [(k, k ^ 1) for k in range(4)], near, F32)


def query_gathered(own):
    pair = jnp.stack([own, lax.ppermute(own, CORE, SWAP)])
    four = jnp.stack([pair, lax.ppermute(pair, "neg_1", SWAP)])
    return lax.all_gather(four, "neg_0").reshape(-1, *own.shape)


def body(
    query_emb, positive, passage_emb, lengths, residual, context, out_proj, norm_gain, colbert_proj
):
    query_dev, query_len, emb = query_emb.shape
    neg_size, dp_size, cross_size = lax.axis_size(NEG), lax.axis_size(DP), lax.axis_size(CROSS)
    place, core = lax.axis_index(NEG), lax.axis_index(CORE)
    spot = jnp.arange(emb)[None] - place * query_dev
    wanted = jnp.sum(
        jnp.where(spot == jnp.arange(query_dev)[:, None], positive[:, None], 0), axis=0
    )
    query_own = jnp.concatenate(
        [
            query_emb.reshape(query_dev * query_len, emb),
            jnp.broadcast_to(wanted.astype(BF16)[None], (EXTRA, emb)),
        ]
    )
    passage_own = jnp.concatenate(
        [
            passage_emb.reshape(-1, emb),
            jnp.broadcast_to((lengths - LEAST).astype(BF16)[:, None], (EXTRA, emb)),
        ]
    )
    query_pack = query_gathered(query_own)
    passage_pack = to_everyone(passage_own, DP)
    ids = jnp.broadcast_to(
        (jnp.arange(dp_size) * neg_size + place).astype(F32)[:, None], (dp_size, emb)
    )
    row, column = lax.axis_index("neg_1"), lax.axis_index("neg_0")
    flip = (2 * row + core)[None]
    spread, mixed, inverse, similar, stats = forward_tile(
        flip, query_pack, passage_pack, ids, query_len
    )
    stats = exchange(stats, NEG)
    passage_parts, query_parts = backward_tile(
        flip, query_pack, spread, mixed, inverse, similar, stats, query_len
    )
    residual, query_parts = lax.optimization_barrier((residual, query_parts))
    early = early_rows(residual, context, out_proj)
    query_half = halves_summed(query_parts, CORE, SWAP, core, BF16)
    passage_parts = exchange(passage_parts, DP)
    passage_parts, query_half, early = lax.optimization_barrier((passage_parts, query_half, early))
    normed, inv_std, context_t = early
    residual_grad, partial, loss_sum = late_rows(
        dp_size, passage_parts, normed, inv_std, norm_gain[None], colbert_proj, context_t
    )
    half = halves_summed(partial, CORE, SWAP, core, BF16)
    context_grad = jnp.dot(residual_grad, out_proj.T, preferred_element_type=F32).astype(BF16)
    slabs = exchange(half.reshape(dp_size * cross_size, *half.shape[2:]), DP + CROSS)
    slabs, context_grad, query_half = lax.optimization_barrier((slabs, context_grad, query_half))
    tile = summed(slabs)
    half = to_everyone(tile, DP + CROSS).reshape(half.shape)
    query_grad = crossed(query_half, row, column)
    half, query_grad = lax.optimization_barrier((half, query_grad))
    query_grad = query_grad.reshape(query_dev, query_len, emb)
    other = lax.ppermute(half, CORE, SWAP)
    out_proj_grad, colbert_grad, gain_grad = finish(
        core[None], half, other, colbert_proj, norm_gain[None]
    )
    loss = loss_sum[0, 0] / (query_dev * dp_size * neg_size)
    return (
        loss,
        query_grad,
        residual_grad,
        context_grad,
        out_proj_grad,
        colbert_grad,
        gain_grad[0],
    )


def solution(mesh):
    split = Mesh(mesh.devices.reshape(mesh.shape["dp"] // 2, 2, 4, 2, 2), DP_NEG)
    placed = (
        P(DP_NEG, None, None),
        P(DP_NEG),
        P(DP_NEG, None, None),
        P(DP_NEG),
        P(DP_NEG, None),
        P(DP_NEG, None),
        P(),
        P(),
        P(),
    )
    return jax.shard_map(
        body,
        mesh=split,
        in_specs=placed,
        out_specs=(P(), P(DP_NEG, None, None), P(DP_NEG, None), P(DP_NEG, None), P(), P(), P()),
        check_vma=False,
    )
```

```python
import functools

import jax
import jax.numpy as jnp
from jax import lax
from jax.experimental import pallas as pl
from jax.experimental.pallas import tpu as pltpu
from jax.sharding import Mesh
from jax.sharding import PartitionSpec as P

DP = ("dp_0", "dp_1")
NEG = ("neg_0", "neg_1", "neg_2")
CROSS = ("neg_0", "neg_1")
CORE = "neg_2"
DP_NEG = DP + NEG
BF16 = jnp.bfloat16
F32 = jnp.float32
EXTRA = 8
LEAST = 256
MIB = 1 << 20


def dot(a, b, dims, precision=None):
    return lax.dot_general(a, b, (dims, ((), ())), precision=precision, preferred_element_type=F32)


def token_query(rows, queries, query_len, transposed=False):
    shape = (queries, rows) if transposed else (rows, queries)
    row = lax.broadcasted_iota(jnp.int32, shape, 1 if transposed else 0)
    query = lax.broadcasted_iota(jnp.int32, shape, 0 if transposed else 1)
    first = query * query_len
    return ((row >= first) & (row < first + query_len)).astype(F32)


def whole(shape):
    return pl.BlockSpec(shape, lambda *_: (0,) * len(shape))


def stored(k, parts, flip_ref):
    return ((k // 2 % 2) ^ flip_ref[0]) * (parts // 2) + k // 4 * 2 + ((k % 2) ^ flip_ref[1])


def forward_kernel(
    query_len, group, flip_ref, q_ref, p_ref, ids_ref, exp_ref, mix_ref, inv_ref, sim_ref, stats_ref, rows_ref
):
    passage = pl.program_id(0)
    parts, q_rows, width = q_ref.shape[0], q_ref.shape[1] - EXTRA, q_ref.shape[2]
    slots = p_ref.shape[1] - EXTRA
    count, rows = inv_ref.shape
    queries = rows // query_len
    chunk = group * q_rows
    steps = parts // group
    tokens = p_ref[0, :slots, :]
    length = p_ref[0, slots : slots + 1, :].astype(F32) + float(LEAST)
    log_length = jnp.log(length)[:, :1]
    wide = jnp.concatenate([length] * ((slots - LEAST) // width), axis=1)
    position = lax.broadcasted_iota(jnp.int32, wide.shape, 1).astype(F32) + float(LEAST)
    bias = jnp.where(position < wide, 0.0, -1e30)
    lane = lax.broadcasted_iota(jnp.int32, (chunk, width), 1)

    @pl.when(passage == 0)
    def _():
        rows_ref[...] = jnp.zeros_like(rows_ref)

    def scores(step):
        block = jnp.concatenate(
            [
                q_ref[stored(step * group + k, parts, flip_ref), :q_rows, :]
                for k in range(group)
            ],
            axis=0,
        )
        return dot(block, tokens, ((1,), (1,)))

    ahead = scores(0)
    late = None
    for step in range(steps):
        now = ahead
        if step + 1 < steps:
            ahead = scores(step + 1)
        if late is not None:
            mix_ref[passage, pl.ds((step - 1) * chunk, chunk), :] = dot(late, tokens, ((1,), (0,)))
        sure, rest = now[:, :LEAST], now[:, LEAST:] + bias
        highest = jnp.maximum(
            jnp.max(sure, axis=1, keepdims=True), jnp.max(rest, axis=1, keepdims=True)
        )
        sure = jnp.exp(sure - highest)
        rest = jnp.exp(rest - highest)
        total = jnp.sum(sure, axis=1, keepdims=True) + jnp.sum(rest, axis=1, keepdims=True)
        late = jnp.concatenate([sure.astype(BF16), rest.astype(BF16)], axis=1)
        at = pl.ds(step * chunk, chunk)
        exp_ref[passage, at, :] = late
        shifted = highest + jnp.log(total) - log_length
        rows_ref[at, :] = jnp.where(
            lane == passage,
            shifted,
            jnp.where(lane == passage + width // 2, total, rows_ref[at, :]),
        )
    mix_ref[passage, pl.ds((steps - 1) * chunk, chunk), :] = dot(late, tokens, ((1,), (0,)))

    @pl.when(passage == pl.num_programs(0) - 1)
    def _():
        turned = rows_ref[...].T
        inv_ref[...] = 1.0 / turned[width // 2 : width // 2 + count]
        similar = dot(
            turned[:count], token_query(rows, queries, query_len), ((1,), (0,)), lax.Precision.HIGHEST
        )
        wanted = jnp.sum(q_ref[:, q_rows, :].astype(F32), axis=0, keepdims=True)[:, :queries]
        hit = (wanted == ids_ref[:, :queries]).astype(F32)
        highest = jnp.max(similar, axis=0, keepdims=True)
        total = jnp.sum(jnp.exp(similar - highest), axis=0, keepdims=True)
        positive = jnp.sum(jnp.where(hit > 0.0, similar, 0.0), axis=0, keepdims=True)
        sim_ref[0] = similar
        sim_ref[1] = hit
        stats = jnp.concatenate([highest, total, positive, jnp.zeros((5, queries), F32)], axis=0)
        stats = jnp.concatenate([stats, jnp.zeros((8, width - queries), F32)], axis=1)
        stats_ref[...] = jnp.broadcast_to(stats[None], stats_ref.shape)


def forward_tile(flip, query_pack, passage_pack, ids, query_len, group=8):
    parts, q_rows, width = query_pack.shape
    q_rows -= EXTRA
    count, slots = passage_pack.shape[0], passage_pack.shape[1] - EXTRA
    rows = parts * q_rows
    queries = rows // query_len
    work = rows * slots * count
    return pl.pallas_call(
        functools.partial(forward_kernel, query_len, group),
        name="forward_tile",
        grid=(count,),
        in_specs=[
            pl.BlockSpec(memory_space=pltpu.SMEM),
            whole(query_pack.shape),
            pl.BlockSpec((1, slots + EXTRA, width), lambda p: (p, 0, 0)),
            whole(ids.shape),
        ],
        out_specs=[
            pl.BlockSpec(memory_space=pltpu.VMEM),
            pl.BlockSpec(memory_space=pltpu.VMEM),
            whole((count, rows)),
            whole((2, count, queries)),
            whole((parts, 8, width)),
        ],
        out_shape=[
            pltpu.VMEM((count, rows, slots), BF16),
            pltpu.VMEM((count, rows, width), F32),
            jax.ShapeDtypeStruct((count, rows), F32),
            jax.ShapeDtypeStruct((2, count, queries), F32),
            jax.ShapeDtypeStruct((parts, 8, width), F32),
        ],
        scratch_shapes=[pltpu.VMEM((rows, width), F32)],
        compiler_params=pltpu.CompilerParams(vmem_limit_bytes=16 * MIB),
        cost_estimate=pl.CostEstimate(
            flops=4 * work * width, transcendentals=work, bytes_accessed=4 * work
        ),
    )(flip, query_pack, passage_pack, ids)


def backward_kernel(
    query_len, flip_ref, q_ref, exp_ref, mix_ref, inv_ref, sim_ref, stats_ref, pg_ref, qg_ref, qt
):
    parts, q_rows, width = q_ref.shape[0], q_ref.shape[1] - EXTRA, q_ref.shape[2]
    count, rows, slots = exp_ref.shape
    queries = rows // query_len
    for k in range(parts):
        qt[:, k * q_rows : (k + 1) * q_rows] = q_ref[stored(k, parts, flip_ref), :q_rows, :].T
    highest_of = stats_ref[:, 0, :queries]
    highest = jnp.max(highest_of, axis=0, keepdims=True)
    total = jnp.sum(
        stats_ref[:, 1, :queries] * jnp.exp(highest_of - highest), axis=0, keepdims=True
    )
    positive = jnp.sum(stats_ref[:, 2, :queries], axis=0, keepdims=True)
    log_total = highest + jnp.log(total)
    coefficient = jnp.exp(sim_ref[0] - log_total) - sim_ref[1]
    scale = inv_ref[...] * dot(
        coefficient,
        token_query(rows, queries, query_len, True),
        ((1,), (0,)),
        lax.Precision.HIGHEST,
    )
    loss = jnp.broadcast_to(jnp.sum(log_total - positive, axis=1, keepdims=True), (EXTRA, width))
    high = loss.astype(BF16).astype(F32)
    low = (loss - high).astype(BF16).astype(F32)
    last = loss - high - low
    row = lax.broadcasted_iota(jnp.int32, (EXTRA, width), 0)
    lines = jnp.where(row == 0, high, jnp.where(row == 1, low, jnp.where(row == 2, last, 0.0)))
    for p in range(count):
        weighted = (qt[...].astype(F32) * scale[p : p + 1]).astype(BF16)
        pg_ref[p, :slots, :] = dot(weighted, exp_ref[p], ((1,), (0,))).T.astype(BF16)
        pg_ref[p, slots:, :] = lines.astype(BF16)
    turned = jnp.concatenate([scale, jnp.zeros((width - count, rows), F32)], axis=0).T
    for k in range(parts):
        at = slice(k * q_rows, (k + 1) * q_rows)
        sums = mix_ref[0, at, :] * turned[at, :1]
        for p in range(1, count):
            sums += mix_ref[p, at, :] * turned[at, p : p + 1]
        qg_ref[k % 2, k // 2 % 2, k // 4] = sums.astype(BF16)


def backward_tile(flip, query_pack, spread, mixed, inverse, similar, stats, query_len):
    parts, q_rows, width = query_pack.shape
    q_rows -= EXTRA
    count, rows, slots = spread.shape
    work = rows * slots * count
    return pl.pallas_call(
        functools.partial(backward_kernel, query_len),
        name="backward_tile",
        in_specs=[pl.BlockSpec(memory_space=pltpu.SMEM)]
        + [pl.BlockSpec(memory_space=pltpu.VMEM)] * 6,
        out_shape=[
            pltpu.HBM((count, slots + EXTRA, width), BF16),
            pltpu.HBM((2, 2, parts // 4, q_rows, width), BF16),
        ],
        out_specs=[whole((count, slots + EXTRA, width)), whole((2, 2, parts // 4, q_rows, width))],
        scratch_shapes=[pltpu.VMEM((width, rows), BF16)],
        compiler_params=pltpu.CompilerParams(vmem_limit_bytes=16 * MIB),
        cost_estimate=pl.CostEstimate(
            flops=2 * work * width, transcendentals=0, bytes_accessed=3 * work
        ),
    )(flip, query_pack, spread, mixed, inverse, similar, stats)


def early_kernel(resid_ref, context_ref, proj_ref, normed_ref, inv_ref, context_t_ref):
    context = context_ref[...]
    hidden = resid_ref[...].astype(F32) + dot(context, proj_ref[...], ((1,), (0,)))
    centred = hidden - jnp.mean(hidden, axis=1, keepdims=True)
    variance = jnp.mean(centred * centred, axis=1, keepdims=True)
    inv_std = 1.0 / jnp.sqrt(variance + 1e-05)
    normed_ref[...] = centred * inv_std
    inv_ref[...] = jnp.broadcast_to(inv_std, inv_ref.shape)
    context_t_ref[...] = context.T


def early_rows(residual, context, out_proj, block=128):
    rows, width = residual.shape
    return pl.pallas_call(
        early_kernel,
        name="early_rows",
        grid=(rows // block,),
        in_specs=[
            pl.BlockSpec((block, width), lambda r: (r, 0)),
            pl.BlockSpec((block, width), lambda r: (r, 0)),
            whole(out_proj.shape),
        ],
        out_specs=[
            pl.BlockSpec((block, width), lambda r: (r, 0)),
            pl.BlockSpec((block, 128), lambda r: (r, 0)),
            pl.BlockSpec((width, block), lambda r: (0, r)),
        ],
        out_shape=[
            pltpu.HBM((rows, width), F32),
            pltpu.HBM((rows, 128), F32),
            pltpu.HBM((width, rows), BF16),
        ],
        compiler_params=pltpu.CompilerParams(vmem_limit_bytes=10 * MIB),
        cost_estimate=pl.CostEstimate(
            flops=2 * rows * width * width, transcendentals=0, bytes_accessed=10 * rows * width
        ),
    )(residual, context, out_proj)


def late_kernel(
    parts_ref,
    normed_far,
    inv_far,
    gain_ref,
    colbert_ref,
    context_far,
    resid_ref,
    sums_ref,
    loss_ref,
    normed_ref,
    inv_ref,
    context_t_ref,
    sems,
):
    loads = [
        pltpu.make_async_copy(far, near, sems.at[k])
        for k, (far, near) in enumerate(
            ((normed_far, normed_ref), (inv_far, inv_ref), (context_far, context_t_ref))
        )
    ]
    for load in loads:
        load.start()
    slots = parts_ref.shape[1] - EXTRA
    count = parts_ref.shape[0]
    width = normed_ref.shape[1]
    total = parts_ref[0].astype(F32)
    for k in range(1, count):
        total = total + parts_ref[k].astype(F32)
    loss_ref[...] = jnp.broadcast_to(
        jnp.sum(total[slots:], axis=0, keepdims=True), loss_ref.shape
    )
    grad = total[:slots].astype(BF16)
    gain = gain_ref[...]
    gained = dot(grad, colbert_ref[...], ((1,), (1,))) * gain
    grad_t = grad.T
    for load in loads[:2]:
        load.wait()
    normed = normed_ref[...]
    inv_std = inv_ref[:, :1]
    resid = inv_std * (
        gained
        - jnp.mean(gained, axis=1, keepdims=True)
        - normed * jnp.mean(gained * normed, axis=1, keepdims=True)
    )
    resid = resid.astype(BF16)
    resid_ref[...] = resid
    scaled = (normed * gain).astype(BF16)
    blocks, lines = sums_ref.shape[1], sums_ref.shape[3]
    thin = grad.shape[1] // (2 * blocks)
    thick = lines - thin
    colbert = dot(grad_t, scaled, ((1,), (0,)))
    for k in range(2 * blocks):
        for j in range(width // 128):
            sums_ref[k // blocks, k % blocks, j, thick:, :] = colbert[
                k * thin : (k + 1) * thin, j * 128 : (j + 1) * 128
            ].astype(BF16)
    loads[2].wait()
    group = 4
    for first in range(0, 2 * blocks, group):
        part = dot(
            context_t_ref[first * thick : (first + group) * thick, :], resid, ((1,), (0,))
        ).astype(BF16)
        for k in range(first, first + group):
            at = (k - first) * thick
            for j in range(width // 128):
                sums_ref[k // blocks, k % blocks, j, :thick, :] = part[
                    at : at + thick, j * 128 : (j + 1) * 128
                ]


def far(array):
    return pltpu.with_memory_space_constraint(array, pltpu.HBM)


def late_rows(blocks, pieces, normed, inv_std, gain, colbert_proj, context_t):
    rows, width = normed.shape
    emb = colbert_proj.shape[1]
    return pl.pallas_call(
        late_kernel,
        name="late_rows",
        in_specs=[
            whole(pieces.shape),
            pl.BlockSpec(memory_space=pltpu.HBM),
            pl.BlockSpec(memory_space=pltpu.HBM),
            whole(gain.shape),
            whole(colbert_proj.shape),
            pl.BlockSpec(memory_space=pltpu.HBM),
        ],
        scratch_shapes=[
            pltpu.VMEM(normed.shape, F32),
            pltpu.VMEM(inv_std.shape, F32),
            pltpu.VMEM(context_t.shape, BF16),
            pltpu.SemaphoreType.DMA((3,)),
        ],
        out_shape=[
            jax.ShapeDtypeStruct((rows, width), BF16),
            jax.ShapeDtypeStruct(
                (2, blocks, width // 128, (width + emb) // (2 * blocks), 128), BF16
            ),
            jax.ShapeDtypeStruct((8, emb), F32),
        ],
        compiler_params=pltpu.CompilerParams(vmem_limit_bytes=24 * MIB),
        cost_estimate=pl.CostEstimate(
            flops=2 * rows * width * (width + 2 * emb),
            transcendentals=0,
            bytes_accessed=14 * rows * width,
        ),
    )(pieces, far(normed), far(inv_std), gain, colbert_proj, far(context_t))


def exchange(pieces, axis):
    return lax.all_to_all(pieces, axis, 0, 0, tiled=True)


def finish_kernel(core_ref, half_ref, other_ref, colbert_ref, gain_ref, proj_ref, grad_ref, gain_grad_ref):
    blocks, lines = half_ref.shape[0], half_ref.shape[2]
    thick = proj_ref.shape[0] // (2 * blocks)
    even = core_ref[0] == 0
    thin = []
    for part in range(2):
        for k in range(blocks):
            half, other = half_ref[k, 0].astype(F32), other_ref[k, 0].astype(F32)
            piece = jnp.where(even, half, other) if part == 0 else jnp.where(even, other, half)
            at = (part * blocks + k) * thick
            proj_ref[at : at + thick, :] = piece[:thick]
            thin.append(piece[thick:])
    colbert_grad = jnp.concatenate(thin, axis=0)
    colbert_t = colbert_ref[...].astype(F32).T
    gain_grad_ref[...] = (
        jnp.sum(colbert_grad * colbert_t, axis=0, keepdims=True) / gain_ref[...]
    )
    grad_ref[...] = colbert_grad.T


def finish(core, half, other, colbert_proj, gain):
    blocks, columns, lines, block = half.shape
    width, emb = colbert_proj.shape
    return pl.pallas_call(
        finish_kernel,
        name="finish",
        grid=(columns,),
        in_specs=[
            pl.BlockSpec(memory_space=pltpu.SMEM),
            pl.BlockSpec((blocks, 1, lines, block), lambda k: (0, k, 0, 0)),
            pl.BlockSpec((blocks, 1, lines, block), lambda k: (0, k, 0, 0)),
            pl.BlockSpec((block, emb), lambda k: (k, 0)),
            pl.BlockSpec((1, block), lambda k: (0, k)),
        ],
        out_specs=[
            pl.BlockSpec((width, block), lambda k: (0, k)),
            pl.BlockSpec((block, emb), lambda k: (k, 0)),
            pl.BlockSpec((1, block), lambda k: (0, k)),
        ],
        out_shape=[
            jax.ShapeDtypeStruct((width, width), F32),
            jax.ShapeDtypeStruct((width, emb), F32),
            jax.ShapeDtypeStruct((1, width), F32),
        ],
        compiler_params=pltpu.CompilerParams(vmem_limit_bytes=16 * MIB),
        cost_estimate=pl.CostEstimate(
            flops=4 * width * width, transcendentals=0, bytes_accessed=8 * width * width
        ),
    )(core, half, other, colbert_proj, gain)


SWAP = [(0, 1), (1, 0)]
FAR = [(k, k ^ 2) for k in range(4)]
NEAR = [(k, k ^ 1) for k in range(4)]


def halves_summed(halves, axis, pairs, side, out_type):
    keep, give = side
    given = lax.dynamic_index_in_dim(halves, give, 0, False)
    kept = lax.dynamic_index_in_dim(halves, keep, 0, False)
    taken = lax.ppermute(given, axis, pairs)
    return (kept.astype(F32) + taken.astype(F32)).astype(out_type)


def query_gathered(own):
    pair = jnp.stack([own, lax.ppermute(own, CORE, SWAP)])
    line = lax.all_gather(pair, "neg_0")
    both = jnp.stack([line, lax.ppermute(line, "neg_1", SWAP)])
    return both.reshape(-1, *own.shape)


def pack_kernel(length_ref, p_ref, out_ref):
    slots = p_ref.shape[1]
    extra = jnp.full((EXTRA, p_ref.shape[2]), (length_ref[0] - LEAST).astype(F32)).astype(BF16)
    for k in range(out_ref.shape[0]):
        out_ref[k, :slots, :] = p_ref[0]
        out_ref[k, slots:, :] = extra


def passage_copies(passage_emb, lengths, copies):
    _, slots, width = passage_emb.shape
    return pl.pallas_call(
        pack_kernel,
        name="passage_copies",
        in_specs=[
            pl.BlockSpec(memory_space=pltpu.SMEM),
            pl.BlockSpec(memory_space=pltpu.VMEM),
        ],
        out_specs=whole((copies, slots + EXTRA, width)),
        out_shape=pltpu.HBM((copies, slots + EXTRA, width), BF16),
    )(lengths, passage_emb)


def spread_kernel(parts_ref, out_ref):
    total = parts_ref[0].astype(F32)
    for k in range(1, parts_ref.shape[0]):
        total += parts_ref[k].astype(F32)
    out_ref[...] = jnp.broadcast_to(total.astype(BF16)[None], out_ref.shape)


def summed_copies(parts):
    return pl.pallas_call(
        spread_kernel,
        name="summed_copies",
        in_specs=[pl.BlockSpec(memory_space=pltpu.VMEM)],
        out_specs=whole(parts.shape),
        out_shape=pltpu.HBM(parts.shape, BF16),
    )(parts)


def body(
    query_emb, positive, passage_emb, lengths, residual, context, out_proj, norm_gain, colbert_proj
):
    query_dev, query_len, emb = query_emb.shape
    neg_size, dp_size, cross_size = lax.axis_size(NEG), lax.axis_size(DP), lax.axis_size(CROSS)
    place, core = lax.axis_index(NEG), lax.axis_index(CORE)
    spot = jnp.arange(emb)[None] - place * query_dev
    wanted = jnp.sum(
        jnp.where(spot == jnp.arange(query_dev)[:, None], positive[:, None], 0), axis=0
    )
    query_own = jnp.concatenate(
        [
            query_emb.reshape(query_dev * query_len, emb),
            jnp.broadcast_to(wanted.astype(BF16)[None], (EXTRA, emb)),
        ]
    )
    query_pack = query_gathered(query_own)
    passage_pack = exchange(passage_copies(passage_emb, lengths, dp_size), DP)
    ids = jnp.broadcast_to(
        (jnp.arange(dp_size) * neg_size + place).astype(F32)[:, None], (dp_size, emb)
    )
    row, column = lax.axis_index("neg_1"), lax.axis_index("neg_0")
    flip = jnp.stack([row, core])
    sides = [
        (own.astype(jnp.uint32), (1 - own).astype(jnp.uint32))
        for own in (core, row, column // 2, column % 2)
    ]
    query_pack, sides = lax.optimization_barrier((query_pack, sides))
    core_side, row_side, far_side, near_side = sides
    spread, mixed, inverse, similar, stats = forward_tile(
        flip, query_pack, passage_pack, ids, query_len
    )
    stats = exchange(stats, NEG)
    passage_parts, query_parts = backward_tile(
        flip, query_pack, spread, mixed, inverse, similar, stats, query_len
    )
    residual, query_parts = lax.optimization_barrier((residual, query_parts))
    early = early_rows(residual, context, out_proj)
    query_part = halves_summed(query_parts, CORE, SWAP, core_side, BF16)
    query_part = halves_summed(query_part, "neg_1", SWAP, row_side, F32)
    passage_parts = exchange(passage_parts, DP)
    passage_parts, query_part, early = lax.optimization_barrier((passage_parts, query_part, early))
    normed, inv_std, context_t = early
    residual_grad, partial, loss_sum = late_rows(
        dp_size, passage_parts, normed, inv_std, norm_gain[None], colbert_proj, context_t
    )
    half = halves_summed(partial, CORE, SWAP, core_side, BF16)
    context_grad = jnp.dot(residual_grad, out_proj.T, preferred_element_type=F32).astype(BF16)
    slabs = exchange(half.reshape(dp_size * cross_size, *half.shape[2:]), DP + CROSS)
    query_part = query_part.reshape(2, 2, *query_part.shape[1:])
    query_part = halves_summed(query_part, "neg_0", FAR, far_side, F32)
    slabs, context_grad, query_part = lax.optimization_barrier((slabs, context_grad, query_part))
    half = exchange(summed_copies(slabs), DP + CROSS).reshape(half.shape)
    query_grad = halves_summed(query_part, "neg_0", NEAR, near_side, F32)
    half, query_grad = lax.optimization_barrier((half, query_grad))
    query_grad = query_grad.reshape(query_dev, query_len, emb)
    other = lax.ppermute(half, CORE, SWAP)
    out_proj_grad, colbert_grad, gain_grad = finish(
        core[None], half, other, colbert_proj, norm_gain[None]
    )
    loss = loss_sum[0, 0] / (query_dev * dp_size * neg_size)
    return (
        loss,
        query_grad,
        residual_grad,
        context_grad,
        out_proj_grad,
        colbert_grad,
        gain_grad[0],
    )


def solution(mesh):
    split = Mesh(mesh.devices.reshape(mesh.shape["dp"] // 2, 2, 4, 2, 2), DP_NEG)
    placed = (
        P(DP_NEG, None, None),
        P(DP_NEG),
        P(DP_NEG, None, None),
        P(DP_NEG),
        P(DP_NEG, None),
        P(DP_NEG, None),
        P(),
        P(),
        P(),
    )
    return jax.shard_map(
        body,
        mesh=split,
        in_specs=placed,
        out_specs=(P(), P(DP_NEG, None, None), P(DP_NEG, None), P(DP_NEG, None), P(), P(), P()),
        check_vma=False,
    )
```

```python
import functools

import jax
import jax.numpy as jnp
from jax import lax
from jax.experimental import pallas as pl
from jax.experimental.pallas import tpu as pltpu
from jax.sharding import Mesh
from jax.sharding import PartitionSpec as P

DP = ("dp_0", "dp_1")
NEG = ("neg_0", "neg_1", "neg_2")
CROSS = ("neg_0", "neg_1")
CORE = "neg_2"
DP_NEG = DP + NEG
BF16 = jnp.bfloat16
F32 = jnp.float32
EXTRA = 8
LEAST = 256
MIB = 1 << 20


def dot(a, b, dims, precision=None):
    return lax.dot_general(a, b, (dims, ((), ())), precision=precision, preferred_element_type=F32)


def token_query(rows, queries, query_len, transposed=False):
    shape = (queries, rows) if transposed else (rows, queries)
    row = lax.broadcasted_iota(jnp.int32, shape, 1 if transposed else 0)
    query = lax.broadcasted_iota(jnp.int32, shape, 0 if transposed else 1)
    first = query * query_len
    return ((row >= first) & (row < first + query_len)).astype(F32)


def whole(shape):
    return pl.BlockSpec(shape, lambda *_: (0,) * len(shape))


def stored(k):
    core, row, near, far = k % 2, k // 2 % 2, k // 4 % 2, k // 8
    return row * 8 + far * 4 + near * 2 + core


def forward_kernel(
    query_len,
    group,
    flip_ref,
    near_ref,
    far_ref,
    p_ref,
    ids_ref,
    exp_ref,
    mix_ref,
    own_ref,
    inv_ref,
    sim_ref,
    stats_ref,
    rows_ref,
    length_ref,
):
    passage = pl.program_id(0)
    half, q_rows, width = near_ref.shape[0], near_ref.shape[1] - EXTRA, near_ref.shape[2]
    parts = 2 * half
    slots = p_ref.shape[1] - EXTRA
    count, rows = inv_ref.shape
    queries = rows // query_len
    chunk = group * q_rows
    steps = parts // group
    tokens = p_ref[0, :slots, :]
    length = p_ref[0, slots : slots + 1, :].astype(F32) + float(LEAST)
    length_ref[pl.ds(passage, 1), :] = length
    wide = jnp.concatenate([length] * ((slots - LEAST) // width), axis=1)
    position = lax.broadcasted_iota(jnp.int32, wide.shape, 1).astype(F32) + float(LEAST)
    bias = jnp.where(position < wide, 0.0, -1e30)
    lane = lax.broadcasted_iota(jnp.int32, (chunk, width), 1)

    @pl.when(passage == 0)
    def _():
        rows_ref[...] = jnp.zeros_like(rows_ref)
        for k in range(parts):
            at = stored(k) ^ flip_ref[0]
            spot = at % half
            own_ref[k * q_rows : (k + 1) * q_rows, :] = jnp.where(
                at < half, near_ref[spot, :q_rows, :], far_ref[spot, :q_rows, :]
            )

    def scores(step):
        block = own_ref[step * chunk : (step + 1) * chunk, :]
        return dot(block, tokens, ((1,), (1,)))

    ahead = scores(0)
    late = None
    for step in range(steps):
        now = ahead
        if step + 1 < steps:
            ahead = scores(step + 1)
        if late is not None:
            mix_ref[passage, pl.ds((step - 1) * chunk, chunk), :] = dot(late, tokens, ((1,), (0,)))
        sure, rest = now[:, :LEAST], now[:, LEAST:] + bias
        highest = jnp.maximum(
            jnp.max(sure, axis=1, keepdims=True), jnp.max(rest, axis=1, keepdims=True)
        )
        sure = jnp.exp(sure - highest)
        rest = jnp.exp(rest - highest)
        total = jnp.sum(sure, axis=1, keepdims=True) + jnp.sum(rest, axis=1, keepdims=True)
        late = jnp.concatenate([sure.astype(BF16), rest.astype(BF16)], axis=1)
        at = pl.ds(step * chunk, chunk)
        exp_ref[passage, at, :] = late
        rows_ref[at, :] = jnp.where(
            lane == passage,
            highest + jnp.log(total),
            jnp.where(lane == passage + width // 2, total, rows_ref[at, :]),
        )
    mix_ref[passage, pl.ds((steps - 1) * chunk, chunk), :] = dot(late, tokens, ((1,), (0,)))

    @pl.when(passage == pl.num_programs(0) - 1)
    def _():
        turned = rows_ref[...].T
        inv_ref[...] = 1.0 / turned[width // 2 : width // 2 + count]
        similar = dot(
            turned[:count], token_query(rows, queries, query_len), ((1,), (0,)), lax.Precision.HIGHEST
        )
        similar = similar - float(query_len) * jnp.log(length_ref[...])[:, :queries]
        wanted = jnp.sum(
            near_ref[:, q_rows, :].astype(F32) + far_ref[:, q_rows, :].astype(F32),
            axis=0,
            keepdims=True,
        )[:, :queries]
        hit = (wanted == ids_ref[:, :queries]).astype(F32)
        highest = jnp.max(similar, axis=0, keepdims=True)
        total = jnp.sum(jnp.exp(similar - highest), axis=0, keepdims=True)
        positive = jnp.sum(jnp.where(hit > 0.0, similar, 0.0), axis=0, keepdims=True)
        sim_ref[0] = similar
        sim_ref[1] = hit
        stats = jnp.concatenate([highest, total, positive, jnp.zeros((5, queries), F32)], axis=0)
        stats = jnp.concatenate([stats, jnp.zeros((8, width - queries), F32)], axis=1)
        stats_ref[...] = jnp.broadcast_to(stats[None], stats_ref.shape)


def forward_tile(flip, near, far, passage_pack, ids, query_len, group=8):
    half, q_rows, width = near.shape
    parts, q_rows = 2 * half, q_rows - EXTRA
    count, slots = passage_pack.shape[0], passage_pack.shape[1] - EXTRA
    rows = parts * q_rows
    queries = rows // query_len
    work = rows * slots * count
    return pl.pallas_call(
        functools.partial(forward_kernel, query_len, group),
        name="forward_tile",
        grid=(count,),
        in_specs=[
            pl.BlockSpec(memory_space=pltpu.SMEM),
            whole(near.shape),
            whole(far.shape),
            pl.BlockSpec((1, slots + EXTRA, width), lambda p: (p, 0, 0)),
            whole(ids.shape),
        ],
        out_specs=[
            pl.BlockSpec(memory_space=pltpu.VMEM),
            pl.BlockSpec(memory_space=pltpu.VMEM),
            pl.BlockSpec(memory_space=pltpu.VMEM),
            whole((count, rows)),
            whole((2, count, queries)),
            whole((parts, 8, width)),
        ],
        out_shape=[
            pltpu.VMEM((count, rows, slots), BF16),
            pltpu.VMEM((count, rows, width), F32),
            pltpu.VMEM((rows, width), BF16),
            jax.ShapeDtypeStruct((count, rows), F32),
            jax.ShapeDtypeStruct((2, count, queries), F32),
            jax.ShapeDtypeStruct((parts, 8, width), F32),
        ],
        scratch_shapes=[pltpu.VMEM((rows, width), F32), pltpu.VMEM((count, width), F32)],
        compiler_params=pltpu.CompilerParams(vmem_limit_bytes=16 * MIB),
        cost_estimate=pl.CostEstimate(
            flops=4 * work * width, transcendentals=work, bytes_accessed=4 * work
        ),
    )(flip, near, far, passage_pack, ids)


def backward_kernel(
    query_len, parts, own_ref, exp_ref, mix_ref, inv_ref, sim_ref, stats_ref, pg_ref, qg_ref, qt
):
    count, rows, slots = exp_ref.shape
    width, q_rows = own_ref.shape[1], rows // parts
    queries = rows // query_len
    for k in range(parts):
        qt[:, k * q_rows : (k + 1) * q_rows] = own_ref[k * q_rows : (k + 1) * q_rows, :].T
    highest_of = stats_ref[:, 0, :queries]
    highest = jnp.max(highest_of, axis=0, keepdims=True)
    total = jnp.sum(
        stats_ref[:, 1, :queries] * jnp.exp(highest_of - highest), axis=0, keepdims=True
    )
    positive = jnp.sum(stats_ref[:, 2, :queries], axis=0, keepdims=True)
    log_total = highest + jnp.log(total)
    coefficient = jnp.exp(sim_ref[0] - log_total) - sim_ref[1]
    scale = inv_ref[...] * dot(
        coefficient,
        token_query(rows, queries, query_len, True),
        ((1,), (0,)),
        lax.Precision.HIGHEST,
    )
    loss = jnp.broadcast_to(jnp.sum(log_total - positive, axis=1, keepdims=True), (EXTRA, width))
    high = loss.astype(BF16).astype(F32)
    low = (loss - high).astype(BF16).astype(F32)
    last = loss - high - low
    row = lax.broadcasted_iota(jnp.int32, (EXTRA, width), 0)
    lines = jnp.where(row == 0, high, jnp.where(row == 1, low, jnp.where(row == 2, last, 0.0)))
    for p in range(count):
        weighted = (qt[...].astype(F32) * scale[p : p + 1]).astype(BF16)
        pg_ref[p, :slots, :] = dot(weighted, exp_ref[p], ((1,), (0,))).T.astype(BF16)
        pg_ref[p, slots:, :] = lines.astype(BF16)
    turned = jnp.concatenate([scale, jnp.zeros((width - count, rows), F32)], axis=0).T
    for k in range(parts):
        at = slice(k * q_rows, (k + 1) * q_rows)
        sums = mix_ref[0, at, :] * turned[at, :1]
        for p in range(1, count):
            sums += mix_ref[p, at, :] * turned[at, p : p + 1]
        qg_ref[k % 2, k // 2 % 2, k // 4] = sums.astype(BF16)


def backward_tile(parts, own, spread, mixed, inverse, similar, stats, query_len):
    count, rows, slots = spread.shape
    q_rows, width = rows // parts, own.shape[1]
    work = rows * slots * count
    return pl.pallas_call(
        functools.partial(backward_kernel, query_len, parts),
        name="backward_tile",
        in_specs=[pl.BlockSpec(memory_space=pltpu.VMEM)] * 6,
        out_shape=[
            pltpu.HBM((count, slots + EXTRA, width), BF16),
            pltpu.HBM((2, 2, parts // 4, q_rows, width), BF16),
        ],
        out_specs=[whole((count, slots + EXTRA, width)), whole((2, 2, parts // 4, q_rows, width))],
        scratch_shapes=[pltpu.VMEM((width, rows), BF16)],
        compiler_params=pltpu.CompilerParams(vmem_limit_bytes=16 * MIB),
        cost_estimate=pl.CostEstimate(
            flops=2 * work * width, transcendentals=0, bytes_accessed=3 * work
        ),
    )(own, spread, mixed, inverse, similar, stats)


def early_kernel(resid_ref, context_ref, proj_ref, normed_ref, inv_ref, context_t_ref):
    context = context_ref[...]
    hidden = resid_ref[...].astype(F32) + dot(context, proj_ref[...], ((1,), (0,)))
    centred = hidden - jnp.mean(hidden, axis=1, keepdims=True)
    variance = jnp.mean(centred * centred, axis=1, keepdims=True)
    inv_std = 1.0 / jnp.sqrt(variance + 1e-05)
    normed_ref[...] = centred * inv_std
    inv_ref[...] = jnp.broadcast_to(inv_std, inv_ref.shape)
    context_t_ref[...] = context.T


def early_rows(residual, context, out_proj, block=128):
    rows, width = residual.shape
    return pl.pallas_call(
        early_kernel,
        name="early_rows",
        grid=(rows // block,),
        in_specs=[
            pl.BlockSpec((block, width), lambda r: (r, 0)),
            pl.BlockSpec((block, width), lambda r: (r, 0)),
            whole(out_proj.shape),
        ],
        out_specs=[
            pl.BlockSpec((block, width), lambda r: (r, 0)),
            pl.BlockSpec((block, 128), lambda r: (r, 0)),
            pl.BlockSpec((width, block), lambda r: (0, r)),
        ],
        out_shape=[
            pltpu.HBM((rows, width), F32),
            pltpu.HBM((rows, 128), F32),
            pltpu.HBM((width, rows), BF16),
        ],
        compiler_params=pltpu.CompilerParams(vmem_limit_bytes=10 * MIB),
        cost_estimate=pl.CostEstimate(
            flops=2 * rows * width * width, transcendentals=0, bytes_accessed=10 * rows * width
        ),
    )(residual, context, out_proj)


def late_kernel(
    parts_ref,
    normed_far,
    inv_far,
    gain_ref,
    colbert_ref,
    context_far,
    resid_ref,
    sums_ref,
    loss_ref,
    normed_ref,
    inv_ref,
    context_t_ref,
    sems,
):
    loads = [
        pltpu.make_async_copy(far, near, sems.at[k])
        for k, (far, near) in enumerate(
            ((normed_far, normed_ref), (inv_far, inv_ref), (context_far, context_t_ref))
        )
    ]
    for load in loads:
        load.start()
    slots = parts_ref.shape[1] - EXTRA
    count = parts_ref.shape[0]
    width = normed_ref.shape[1]
    total = parts_ref[0].astype(F32)
    for k in range(1, count):
        total = total + parts_ref[k].astype(F32)
    loss_ref[...] = jnp.broadcast_to(
        jnp.sum(total[slots:], axis=0, keepdims=True), loss_ref.shape
    )
    grad = total[:slots].astype(BF16)
    gain = gain_ref[...]
    gained = dot(grad, colbert_ref[...], ((1,), (1,))) * gain
    grad_t = grad.T
    for load in loads[:2]:
        load.wait()
    normed = normed_ref[...]
    inv_std = inv_ref[:, :1]
    resid = inv_std * (
        gained
        - jnp.mean(gained, axis=1, keepdims=True)
        - normed * jnp.mean(gained * normed, axis=1, keepdims=True)
    )
    resid = resid.astype(BF16)
    resid_ref[...] = resid
    scaled = (normed * gain).astype(BF16)
    blocks, lines = sums_ref.shape[1], sums_ref.shape[3]
    thin = grad.shape[1] // (2 * blocks)
    thick = lines - thin
    colbert = dot(grad_t, scaled, ((1,), (0,)))
    for k in range(2 * blocks):
        for j in range(width // 128):
            sums_ref[k // blocks, k % blocks, j, thick:, :] = colbert[
                k * thin : (k + 1) * thin, j * 128 : (j + 1) * 128
            ].astype(BF16)
    loads[2].wait()
    group = 4
    for first in range(0, 2 * blocks, group):
        part = dot(
            context_t_ref[first * thick : (first + group) * thick, :], resid, ((1,), (0,))
        ).astype(BF16)
        for k in range(first, first + group):
            at = (k - first) * thick
            for j in range(width // 128):
                sums_ref[k // blocks, k % blocks, j, :thick, :] = part[
                    at : at + thick, j * 128 : (j + 1) * 128
                ]


def far(array):
    return pltpu.with_memory_space_constraint(array, pltpu.HBM)


def late_rows(blocks, pieces, normed, inv_std, gain, colbert_proj, context_t):
    rows, width = normed.shape
    emb = colbert_proj.shape[1]
    return pl.pallas_call(
        late_kernel,
        name="late_rows",
        in_specs=[
            whole(pieces.shape),
            pl.BlockSpec(memory_space=pltpu.HBM),
            pl.BlockSpec(memory_space=pltpu.HBM),
            whole(gain.shape),
            whole(colbert_proj.shape),
            pl.BlockSpec(memory_space=pltpu.HBM),
        ],
        scratch_shapes=[
            pltpu.VMEM(normed.shape, F32),
            pltpu.VMEM(inv_std.shape, F32),
            pltpu.VMEM(context_t.shape, BF16),
            pltpu.SemaphoreType.DMA((3,)),
        ],
        out_shape=[
            jax.ShapeDtypeStruct((rows, width), BF16),
            jax.ShapeDtypeStruct(
                (2, blocks, width // 128, (width + emb) // (2 * blocks), 128), BF16
            ),
            jax.ShapeDtypeStruct((8, emb), F32),
        ],
        compiler_params=pltpu.CompilerParams(vmem_limit_bytes=24 * MIB),
        cost_estimate=pl.CostEstimate(
            flops=2 * rows * width * (width + 2 * emb),
            transcendentals=0,
            bytes_accessed=14 * rows * width,
        ),
    )(pieces, far(normed), far(inv_std), gain, colbert_proj, far(context_t))


def exchange(pieces, axis):
    return lax.all_to_all(pieces, axis, 0, 0, tiled=True)


def finish_kernel(core_ref, half_ref, other_ref, colbert_ref, gain_ref, proj_ref, grad_ref, gain_grad_ref):
    blocks, lines = half_ref.shape[0], half_ref.shape[2]
    thick = proj_ref.shape[0] // (2 * blocks)
    even = core_ref[0] == 0
    thin = []
    for part in range(2):
        for k in range(blocks):
            half, other = half_ref[k, 0].astype(F32), other_ref[k, 0].astype(F32)
            piece = jnp.where(even, half, other) if part == 0 else jnp.where(even, other, half)
            at = (part * blocks + k) * thick
            proj_ref[at : at + thick, :] = piece[:thick]
            thin.append(piece[thick:])
    colbert_grad = jnp.concatenate(thin, axis=0)
    colbert_t = colbert_ref[...].astype(F32).T
    gain_grad_ref[...] = (
        jnp.sum(colbert_grad * colbert_t, axis=0, keepdims=True) / gain_ref[...]
    )
    grad_ref[...] = colbert_grad.T


def finish(core, half, other, colbert_proj, gain):
    blocks, columns, lines, block = half.shape
    width, emb = colbert_proj.shape
    return pl.pallas_call(
        finish_kernel,
        name="finish",
        grid=(columns,),
        in_specs=[
            pl.BlockSpec(memory_space=pltpu.SMEM),
            pl.BlockSpec((blocks, 1, lines, block), lambda k: (0, k, 0, 0)),
            pl.BlockSpec((blocks, 1, lines, block), lambda k: (0, k, 0, 0)),
            pl.BlockSpec((block, emb), lambda k: (k, 0)),
            pl.BlockSpec((1, block), lambda k: (0, k)),
        ],
        out_specs=[
            pl.BlockSpec((width, block), lambda k: (0, k)),
            pl.BlockSpec((block, emb), lambda k: (k, 0)),
            pl.BlockSpec((1, block), lambda k: (0, k)),
        ],
        out_shape=[
            jax.ShapeDtypeStruct((width, width), F32),
            jax.ShapeDtypeStruct((width, emb), F32),
            jax.ShapeDtypeStruct((1, width), F32),
        ],
        compiler_params=pltpu.CompilerParams(vmem_limit_bytes=16 * MIB),
        cost_estimate=pl.CostEstimate(
            flops=4 * width * width, transcendentals=0, bytes_accessed=8 * width * width
        ),
    )(core, half, other, colbert_proj, gain)


SWAP = [(0, 1), (1, 0)]
FAR = [(k, k ^ 2) for k in range(4)]
NEAR = [(k, k ^ 1) for k in range(4)]


def halves_summed(halves, axis, pairs, side, out_type):
    keep, give = side
    given = lax.dynamic_index_in_dim(halves, give, 0, False)
    kept = lax.dynamic_index_in_dim(halves, keep, 0, False)
    taken = lax.ppermute(given, axis, pairs)
    return (kept.astype(F32) + taken.astype(F32)).astype(out_type)


def query_gathered(own):
    held = own[None]
    for axis, pairs in ((CORE, SWAP), ("neg_0", NEAR), ("neg_0", FAR)):
        held = jnp.concatenate([held, lax.ppermute(held, axis, pairs)])
    return held, lax.ppermute(held, "neg_1", SWAP)


def pack_kernel(length_ref, p_ref, out_ref):
    slots = p_ref.shape[1]
    extra = jnp.full((EXTRA, p_ref.shape[2]), (length_ref[0] - LEAST).astype(F32)).astype(BF16)
    for k in range(out_ref.shape[0]):
        out_ref[k, :slots, :] = p_ref[0]
        out_ref[k, slots:, :] = extra


def passage_copies(passage_emb, lengths, copies):
    _, slots, width = passage_emb.shape
    return pl.pallas_call(
        pack_kernel,
        name="passage_copies",
        in_specs=[
            pl.BlockSpec(memory_space=pltpu.SMEM),
            pl.BlockSpec(memory_space=pltpu.VMEM),
        ],
        out_specs=whole((copies, slots + EXTRA, width)),
        out_shape=pltpu.HBM((copies, slots + EXTRA, width), BF16),
    )(lengths, passage_emb)


def spread_kernel(parts_ref, out_ref):
    total = parts_ref[0].astype(F32)
    for k in range(1, parts_ref.shape[0]):
        total += parts_ref[k].astype(F32)
    out_ref[...] = jnp.broadcast_to(total.astype(BF16)[None], out_ref.shape)


def summed_copies(parts):
    return pl.pallas_call(
        spread_kernel,
        name="summed_copies",
        in_specs=[pl.BlockSpec(memory_space=pltpu.VMEM)],
        out_specs=whole(parts.shape),
        out_shape=pltpu.HBM(parts.shape, BF16),
    )(parts)


def body(
    query_emb, positive, passage_emb, lengths, residual, context, out_proj, norm_gain, colbert_proj
):
    query_dev, query_len, emb = query_emb.shape
    neg_size, dp_size, cross_size = lax.axis_size(NEG), lax.axis_size(DP), lax.axis_size(CROSS)
    place, core = lax.axis_index(NEG), lax.axis_index(CORE)
    spot = jnp.arange(emb)[None] - place * query_dev
    wanted = jnp.sum(
        jnp.where(spot == jnp.arange(query_dev)[:, None], positive[:, None], 0), axis=0
    )
    query_own = jnp.concatenate(
        [
            query_emb.reshape(query_dev * query_len, emb),
            jnp.broadcast_to(wanted.astype(BF16)[None], (EXTRA, emb)),
        ]
    )
    copies, query_own = lax.optimization_barrier(
        (passage_copies(passage_emb, lengths, dp_size), query_own)
    )
    passage_pack = exchange(copies, DP)
    queries = query_gathered(query_own)
    ids = jnp.broadcast_to(
        (jnp.arange(dp_size) * neg_size + place).astype(F32)[:, None], (dp_size, emb)
    )
    row, column = lax.axis_index("neg_1"), lax.axis_index("neg_0")
    flip = (row * 8 + column * 2 + core)[None]
    sides = [
        (own.astype(jnp.uint32), (1 - own).astype(jnp.uint32))
        for own in (core, row, column // 2, column % 2)
    ]
    queries, sides = lax.optimization_barrier((queries, sides))
    core_side, row_side, far_side, near_side = sides
    spread, mixed, query_rows, inverse, similar, stats = forward_tile(
        flip, *queries, passage_pack, ids, query_len
    )
    stats = exchange(stats, NEG)
    passage_parts, query_parts = backward_tile(
        neg_size, query_rows, spread, mixed, inverse, similar, stats, query_len
    )
    residual, query_parts = lax.optimization_barrier((residual, query_parts))
    early = early_rows(residual, context, out_proj)
    query_part = halves_summed(query_parts, CORE, SWAP, core_side, BF16)
    query_part = halves_summed(query_part, "neg_1", SWAP, row_side, F32)
    passage_parts = exchange(passage_parts, DP)
    passage_parts, query_part, early = lax.optimization_barrier((passage_parts, query_part, early))
    normed, inv_std, context_t = early
    residual_grad, partial, loss_sum = late_rows(
        dp_size, passage_parts, normed, inv_std, norm_gain[None], colbert_proj, context_t
    )
    half = halves_summed(partial, CORE, SWAP, core_side, BF16)
    context_grad = jnp.dot(residual_grad, out_proj.T, preferred_element_type=F32).astype(BF16)
    query_part = query_part.reshape(2, 2, *query_part.shape[1:])
    query_part = halves_summed(query_part, "neg_0", FAR, far_side, F32)
    half, context_grad, query_part = lax.optimization_barrier((half, context_grad, query_part))
    slabs = exchange(half.reshape(dp_size * cross_size, *half.shape[2:]), DP + CROSS)
    half = exchange(summed_copies(slabs), DP + CROSS).reshape(half.shape)
    half, query_part = lax.optimization_barrier((half, query_part))
    query_grad = halves_summed(query_part, "neg_0", NEAR, near_side, F32)
    query_grad = query_grad.reshape(query_dev, query_len, emb)
    other = lax.ppermute(half, CORE, SWAP)
    out_proj_grad, colbert_grad, gain_grad = finish(
        core[None], half, other, colbert_proj, norm_gain[None]
    )
    loss = loss_sum[0, 0] / (query_dev * dp_size * neg_size)
    return (
        loss,
        query_grad,
        residual_grad,
        context_grad,
        out_proj_grad,
        colbert_grad,
        gain_grad[0],
    )


def solution(mesh):
    split = Mesh(mesh.devices.reshape(mesh.shape["dp"] // 2, 2, 4, 2, 2), DP_NEG)
    placed = (
        P(DP_NEG, None, None),
        P(DP_NEG),
        P(DP_NEG, None, None),
        P(DP_NEG),
        P(DP_NEG, None),
        P(DP_NEG, None),
        P(),
        P(),
        P(),
    )
    return jax.shard_map(
        body,
        mesh=split,
        in_specs=placed,
        out_specs=(P(), P(DP_NEG, None, None), P(DP_NEG, None), P(DP_NEG, None), P(), P(), P()),
        check_vma=False,
    )
```

```python
import functools

import jax
import jax.numpy as jnp
from jax import lax
from jax.experimental import pallas as pl
from jax.experimental.pallas import tpu as pltpu
from jax.sharding import Mesh
from jax.sharding import PartitionSpec as P

DP = ("dp_0", "dp_1")
NEG = ("neg_0", "neg_1", "neg_2")
CROSS = ("neg_0", "neg_1")
CORE = "neg_2"
DP_NEG = DP + NEG
BF16 = jnp.bfloat16
F32 = jnp.float32
EXTRA = 8
LEAST = 256
MIB = 1 << 20


def dot(a, b, dims, precision=None):
    return lax.dot_general(a, b, (dims, ((), ())), precision=precision, preferred_element_type=F32)


def token_query(rows, queries, query_len, transposed=False):
    shape = (queries, rows) if transposed else (rows, queries)
    row = lax.broadcasted_iota(jnp.int32, shape, 1 if transposed else 0)
    query = lax.broadcasted_iota(jnp.int32, shape, 0 if transposed else 1)
    first = query * query_len
    return ((row >= first) & (row < first + query_len)).astype(F32)


def whole(shape):
    return pl.BlockSpec(shape, lambda *_: (0,) * len(shape))


def stored(k):
    core, row, near, far = k % 2, k // 2 % 2, k // 4 % 2, k // 8
    return row * 8 + far * 4 + near * 2 + core


def forward_kernel(
    query_len,
    group,
    flip_ref,
    near_ref,
    far_ref,
    p_ref,
    ids_ref,
    exp_ref,
    mix_ref,
    own_ref,
    inv_ref,
    sim_ref,
    stats_ref,
    rows_ref,
    length_ref,
):
    passage = pl.program_id(0)
    half, q_rows, width = near_ref.shape[0], near_ref.shape[1] - EXTRA, near_ref.shape[2]
    parts = 2 * half
    slots = p_ref.shape[1] - EXTRA
    count, rows = inv_ref.shape
    queries = rows // query_len
    chunk = group * q_rows
    steps = parts // group
    tokens = p_ref[0, :slots, :]
    length = p_ref[0, slots : slots + 1, :].astype(F32) + float(LEAST)
    length_ref[pl.ds(passage, 1), :] = length
    wide = jnp.concatenate([length] * ((slots - LEAST) // width), axis=1)
    position = lax.broadcasted_iota(jnp.int32, wide.shape, 1).astype(F32) + float(LEAST)
    bias = jnp.where(position < wide, 0.0, -1e30)
    lane = lax.broadcasted_iota(jnp.int32, (chunk, width), 1)

    @pl.when(passage == 0)
    def _():
        rows_ref[...] = jnp.zeros_like(rows_ref)
        for k in range(parts):
            at = stored(k) ^ flip_ref[0]
            spot = at % half
            own_ref[k * q_rows : (k + 1) * q_rows, :] = jnp.where(
                at < half, near_ref[spot, :q_rows, :], far_ref[spot, :q_rows, :]
            )

    def scores(step):
        block = own_ref[step * chunk : (step + 1) * chunk, :]
        return dot(block, tokens, ((1,), (1,)))

    ahead = scores(0)
    late = None
    for step in range(steps):
        now = ahead
        if step + 1 < steps:
            ahead = scores(step + 1)
        if late is not None:
            mix_ref[passage, pl.ds((step - 1) * chunk, chunk), :] = dot(late, tokens, ((1,), (0,)))
        sure, rest = now[:, :LEAST], now[:, LEAST:] + bias
        highest = jnp.maximum(
            jnp.max(sure, axis=1, keepdims=True), jnp.max(rest, axis=1, keepdims=True)
        )
        sure = jnp.exp(sure - highest)
        rest = jnp.exp(rest - highest)
        total = jnp.sum(sure, axis=1, keepdims=True) + jnp.sum(rest, axis=1, keepdims=True)
        late = jnp.concatenate([sure.astype(BF16), rest.astype(BF16)], axis=1)
        at = pl.ds(step * chunk, chunk)
        exp_ref[passage, at, :] = late
        rows_ref[at, :] = jnp.where(
            lane == passage,
            highest + jnp.log(total),
            jnp.where(lane == passage + width // 2, total, rows_ref[at, :]),
        )
    mix_ref[passage, pl.ds((steps - 1) * chunk, chunk), :] = dot(late, tokens, ((1,), (0,)))

    @pl.when(passage == pl.num_programs(0) - 1)
    def _():
        turned = rows_ref[...].T
        inv_ref[...] = 1.0 / turned[width // 2 : width // 2 + count]
        similar = dot(
            turned[:count], token_query(rows, queries, query_len), ((1,), (0,)), lax.Precision.HIGHEST
        )
        similar = similar - float(query_len) * jnp.log(length_ref[...])[:, :queries]
        wanted = jnp.sum(
            near_ref[:, q_rows, :].astype(F32) + far_ref[:, q_rows, :].astype(F32),
            axis=0,
            keepdims=True,
        )[:, :queries]
        hit = (wanted == ids_ref[:, :queries]).astype(F32)
        highest = jnp.max(similar, axis=0, keepdims=True)
        total = jnp.sum(jnp.exp(similar - highest), axis=0, keepdims=True)
        positive = jnp.sum(jnp.where(hit > 0.0, similar, 0.0), axis=0, keepdims=True)
        sim_ref[0] = similar
        sim_ref[1] = hit
        stats = jnp.concatenate([highest, total, positive, jnp.zeros((5, queries), F32)], axis=0)
        stats = jnp.concatenate([stats, jnp.zeros((8, width - queries), F32)], axis=1)
        stats_ref[...] = jnp.broadcast_to(stats[None], stats_ref.shape)


def forward_tile(flip, near, far, passage_pack, ids, query_len, group=8):
    half, q_rows, width = near.shape
    parts, q_rows = 2 * half, q_rows - EXTRA
    count, slots = passage_pack.shape[0], passage_pack.shape[1] - EXTRA
    rows = parts * q_rows
    queries = rows // query_len
    work = rows * slots * count
    return pl.pallas_call(
        functools.partial(forward_kernel, query_len, group),
        name="forward_tile",
        grid=(count,),
        in_specs=[
            pl.BlockSpec(memory_space=pltpu.SMEM),
            whole(near.shape),
            whole(far.shape),
            pl.BlockSpec((1, slots + EXTRA, width), lambda p: (p, 0, 0)),
            whole(ids.shape),
        ],
        out_specs=[
            pl.BlockSpec(memory_space=pltpu.VMEM),
            pl.BlockSpec(memory_space=pltpu.VMEM),
            pl.BlockSpec(memory_space=pltpu.VMEM),
            whole((count, rows)),
            whole((2, count, queries)),
            whole((parts, 8, width)),
        ],
        out_shape=[
            pltpu.VMEM((count, rows, slots), BF16),
            pltpu.VMEM((count, rows, width), F32),
            pltpu.VMEM((rows, width), BF16),
            jax.ShapeDtypeStruct((count, rows), F32),
            jax.ShapeDtypeStruct((2, count, queries), F32),
            jax.ShapeDtypeStruct((parts, 8, width), F32),
        ],
        scratch_shapes=[pltpu.VMEM((rows, width), F32), pltpu.VMEM((count, width), F32)],
        compiler_params=pltpu.CompilerParams(vmem_limit_bytes=16 * MIB),
        cost_estimate=pl.CostEstimate(
            flops=4 * work * width, transcendentals=work, bytes_accessed=4 * work
        ),
    )(flip, near, far, passage_pack, ids)


def split_lines(value):
    high = value.astype(BF16).astype(F32)
    low = (value - high).astype(BF16).astype(F32)
    last = value - high - low
    row = lax.broadcasted_iota(jnp.int32, value.shape, 0)
    lines = jnp.where(row == 0, high, jnp.where(row == 1, low, jnp.where(row == 2, last, 0.0)))
    return lines.astype(BF16)


def backward_kernel(
    query_len,
    parts,
    core_ref,
    own_ref,
    exp_ref,
    mix_ref,
    inv_ref,
    sim_ref,
    stats_ref,
    pg_ref,
    kept_ref,
    given_ref,
    qt,
    halves,
):
    count, rows, slots = exp_ref.shape
    width, q_rows = own_ref.shape[1], rows // parts
    queries = rows // query_len
    for k in range(parts):
        qt[:, k * q_rows : (k + 1) * q_rows] = own_ref[k * q_rows : (k + 1) * q_rows, :].T
    highest_of = stats_ref[:, 0, :queries]
    highest = jnp.max(highest_of, axis=0, keepdims=True)
    total = jnp.sum(
        stats_ref[:, 1, :queries] * jnp.exp(highest_of - highest), axis=0, keepdims=True
    )
    positive = jnp.sum(stats_ref[:, 2, :queries], axis=0, keepdims=True)
    log_total = highest + jnp.log(total)
    coefficient = jnp.exp(sim_ref[0] - log_total) - sim_ref[1]
    scale = inv_ref[...] * dot(
        coefficient,
        token_query(rows, queries, query_len, True),
        ((1,), (0,)),
        lax.Precision.HIGHEST,
    )
    lines = split_lines(
        jnp.broadcast_to(jnp.sum(log_total - positive, axis=1, keepdims=True), (EXTRA, width))
    )
    for p in range(count):
        weighted = (qt[...].astype(F32) * scale[p : p + 1]).astype(BF16)
        pg_ref[p, :slots, :] = dot(weighted, exp_ref[p], ((1,), (0,))).T.astype(BF16)
        pg_ref[p, slots:, :] = lines
    turned = jnp.concatenate([scale, jnp.zeros((width - count, rows), F32)], axis=0).T
    for k in range(parts):
        at = slice(k * q_rows, (k + 1) * q_rows)
        sums = mix_ref[0, at, :] * turned[at, :1]
        for p in range(1, count):
            sums += mix_ref[p, at, :] * turned[at, p : p + 1]
        halves[k % 2, k // 2 % 2, k // 4] = sums.astype(BF16)
    kept_ref[...] = halves[core_ref[0]]
    given_ref[...] = halves[1 - core_ref[0]]


def backward_tile(core, parts, own, spread, mixed, inverse, similar, stats, query_len):
    count, rows, slots = spread.shape
    q_rows, width = rows // parts, own.shape[1]
    work = rows * slots * count
    return pl.pallas_call(
        functools.partial(backward_kernel, query_len, parts),
        name="backward_tile",
        in_specs=[pl.BlockSpec(memory_space=pltpu.SMEM)]
        + [pl.BlockSpec(memory_space=pltpu.VMEM)] * 6,
        out_shape=[
            pltpu.HBM((count, slots + EXTRA, width), BF16),
            jax.ShapeDtypeStruct((2, parts // 4, q_rows, width), BF16),
            jax.ShapeDtypeStruct((2, parts // 4, q_rows, width), BF16),
        ],
        out_specs=[whole((count, slots + EXTRA, width))]
        + [whole((2, parts // 4, q_rows, width))] * 2,
        scratch_shapes=[
            pltpu.VMEM((width, rows), BF16),
            pltpu.VMEM((2, 2, parts // 4, q_rows, width), BF16),
        ],
        compiler_params=pltpu.CompilerParams(vmem_limit_bytes=16 * MIB),
        cost_estimate=pl.CostEstimate(
            flops=2 * work * width, transcendentals=0, bytes_accessed=3 * work
        ),
    )(core, own, spread, mixed, inverse, similar, stats)


def early_kernel(resid_ref, context_ref, proj_ref, normed_ref, inv_ref, context_t_ref):
    context = context_ref[...]
    hidden = resid_ref[...].astype(F32) + dot(context, proj_ref[...], ((1,), (0,)))
    centred = hidden - jnp.mean(hidden, axis=1, keepdims=True)
    variance = jnp.mean(centred * centred, axis=1, keepdims=True)
    inv_std = 1.0 / jnp.sqrt(variance + 1e-05)
    normed_ref[...] = centred * inv_std
    inv_ref[...] = jnp.broadcast_to(inv_std, inv_ref.shape)
    context_t_ref[...] = context.T


def early_rows(residual, context, out_proj, block=128):
    rows, width = residual.shape
    return pl.pallas_call(
        early_kernel,
        name="early_rows",
        grid=(rows // block,),
        in_specs=[
            pl.BlockSpec((block, width), lambda r: (r, 0)),
            pl.BlockSpec((block, width), lambda r: (r, 0)),
            whole(out_proj.shape),
        ],
        out_specs=[
            pl.BlockSpec((block, width), lambda r: (r, 0)),
            pl.BlockSpec((block, 128), lambda r: (r, 0)),
            pl.BlockSpec((width, block), lambda r: (0, r)),
        ],
        out_shape=[
            pltpu.HBM((rows, width), F32),
            pltpu.HBM((rows, 128), F32),
            pltpu.HBM((width, rows), BF16),
        ],
        compiler_params=pltpu.CompilerParams(vmem_limit_bytes=10 * MIB),
        cost_estimate=pl.CostEstimate(
            flops=2 * rows * width * width, transcendentals=0, bytes_accessed=10 * rows * width
        ),
    )(residual, context, out_proj)


def late_kernel(
    core_ref,
    own_ref,
    taken_ref,
    normed_far,
    inv_far,
    gain_ref,
    colbert_ref,
    context_far,
    resid_ref,
    kept_ref,
    given_ref,
    loss_ref,
    normed_ref,
    inv_ref,
    context_t_ref,
    sums_ref,
    sems,
):
    loads = [
        pltpu.make_async_copy(far, near, sems.at[k])
        for k, (far, near) in enumerate(
            ((normed_far, normed_ref), (inv_far, inv_ref), (context_far, context_t_ref))
        )
    ]
    for load in loads:
        load.start()
    slots = own_ref.shape[0] - EXTRA
    width = normed_ref.shape[1]
    total = own_ref[...] + taken_ref[...].astype(F32)
    loss_ref[...] = jnp.broadcast_to(
        jnp.sum(total[slots:], axis=0, keepdims=True), loss_ref.shape
    )
    grad = total[:slots].astype(BF16)
    gain = gain_ref[...]
    gained = dot(grad, colbert_ref[...], ((1,), (1,))) * gain
    grad_t = grad.T
    for load in loads[:2]:
        load.wait()
    normed = normed_ref[...]
    inv_std = inv_ref[:, :1]
    resid = inv_std * (
        gained
        - jnp.mean(gained, axis=1, keepdims=True)
        - normed * jnp.mean(gained * normed, axis=1, keepdims=True)
    )
    resid = resid.astype(BF16)
    resid_ref[...] = resid
    scaled = (normed * gain).astype(BF16)
    blocks, lines = sums_ref.shape[1], sums_ref.shape[3]
    thin = grad.shape[1] // (2 * blocks)
    thick = lines - thin
    colbert = dot(grad_t, scaled, ((1,), (0,)))
    for k in range(2 * blocks):
        for j in range(width // 128):
            sums_ref[k // blocks, k % blocks, j, thick:, :] = colbert[
                k * thin : (k + 1) * thin, j * 128 : (j + 1) * 128
            ].astype(BF16)
    loads[2].wait()
    group = 4
    for first in range(0, 2 * blocks, group):
        part = dot(
            context_t_ref[first * thick : (first + group) * thick, :], resid, ((1,), (0,))
        ).astype(BF16)
        for k in range(first, first + group):
            at = (k - first) * thick
            for j in range(width // 128):
                sums_ref[k // blocks, k % blocks, j, :thick, :] = part[
                    at : at + thick, j * 128 : (j + 1) * 128
                ]
    kept_ref[...] = sums_ref[core_ref[0]]
    given_ref[...] = sums_ref[1 - core_ref[0]]


def fold_kernel(parts_ref, kept_ref, given_ref):
    slots = parts_ref.shape[2] - EXTRA
    for side, out_ref in enumerate((kept_ref, given_ref)):
        total = parts_ref[0, side].astype(F32)
        for k in range(1, parts_ref.shape[0]):
            total += parts_ref[k, side].astype(F32)
        if side == 0:
            out_ref[...] = total
        else:
            out_ref[:slots, :] = total[:slots].astype(BF16)
            loss = jnp.sum(total[slots:], axis=0, keepdims=True)
            out_ref[slots:, :] = split_lines(jnp.broadcast_to(loss, (EXTRA, loss.shape[1])))


def folded(parts):
    shape = parts.shape[2:]
    return pl.pallas_call(
        fold_kernel,
        name="folded",
        out_shape=[jax.ShapeDtypeStruct(shape, F32), jax.ShapeDtypeStruct(shape, BF16)],
    )(parts)


def far(array):
    return pltpu.with_memory_space_constraint(array, pltpu.HBM)


def late_rows(core, blocks, own, taken, normed, inv_std, gain, colbert_proj, context_t):
    rows, width = normed.shape
    emb = colbert_proj.shape[1]
    shape = (blocks, width // 128, (width + emb) // (2 * blocks), 128)
    return pl.pallas_call(
        late_kernel,
        name="late_rows",
        in_specs=[
            pl.BlockSpec(memory_space=pltpu.SMEM),
            whole(own.shape),
            whole(taken.shape),
            pl.BlockSpec(memory_space=pltpu.HBM),
            pl.BlockSpec(memory_space=pltpu.HBM),
            whole(gain.shape),
            whole(colbert_proj.shape),
            pl.BlockSpec(memory_space=pltpu.HBM),
        ],
        scratch_shapes=[
            pltpu.VMEM(normed.shape, F32),
            pltpu.VMEM(inv_std.shape, F32),
            pltpu.VMEM(context_t.shape, BF16),
            pltpu.VMEM((2, *shape), BF16),
            pltpu.SemaphoreType.DMA((3,)),
        ],
        out_shape=[
            jax.ShapeDtypeStruct((rows, width), BF16),
            jax.ShapeDtypeStruct(shape, BF16),
            jax.ShapeDtypeStruct(shape, BF16),
            jax.ShapeDtypeStruct((8, emb), F32),
        ],
        compiler_params=pltpu.CompilerParams(vmem_limit_bytes=24 * MIB),
        cost_estimate=pl.CostEstimate(
            flops=2 * rows * width * (width + 2 * emb),
            transcendentals=0,
            bytes_accessed=14 * rows * width,
        ),
    )(core, own, taken, far(normed), far(inv_std), gain, colbert_proj, far(context_t))


def exchange(pieces, axis):
    return lax.all_to_all(pieces, axis, 0, 0, tiled=True)


def own_kernel(core_ref, half_ref, proj_ref):
    thick = proj_ref.shape[0] // half_ref.shape[0]
    for k in range(half_ref.shape[0]):
        proj_ref[k * thick : (k + 1) * thick, :] = half_ref[k, 0, :thick, :].astype(F32)


def own_rows(core, half, width):
    blocks, columns, lines, block = half.shape
    return pl.pallas_call(
        own_kernel,
        name="own_rows",
        grid_spec=pltpu.PrefetchScalarGridSpec(
            num_scalar_prefetch=1,
            grid=(columns,),
            in_specs=[pl.BlockSpec((blocks, 1, lines, block), lambda k, core: (0, k, 0, 0))],
            out_specs=pl.BlockSpec((width // 2, block), lambda k, core: (core[0], k)),
        ),
        out_shape=pltpu.HBM((width, width), F32),
        compiler_params=pltpu.CompilerParams(vmem_limit_bytes=8 * MIB),
        cost_estimate=pl.CostEstimate(
            flops=width * width, transcendentals=0, bytes_accessed=4 * width * width
        ),
    )(core, half)


def finish_kernel(
    core_ref, half_ref, other_ref, colbert_ref, gain_ref, _, proj_ref, grad_ref, gain_grad_ref
):
    blocks = half_ref.shape[0]
    thick = proj_ref.shape[0] // blocks
    even = core_ref[0] == 0
    own, others = [], []
    for k in range(blocks):
        piece = other_ref[k, 0].astype(F32)
        proj_ref[k * thick : (k + 1) * thick, :] = piece[:thick]
        others.append(piece[thick:])
        own.append(half_ref[k, 0].astype(F32)[thick:])
    own, others = jnp.concatenate(own, axis=0), jnp.concatenate(others, axis=0)
    colbert_grad = jnp.concatenate(
        [jnp.where(even, own, others), jnp.where(even, others, own)], axis=0
    )
    colbert_t = colbert_ref[...].astype(F32).T
    gain_grad_ref[...] = (
        jnp.sum(colbert_grad * colbert_t, axis=0, keepdims=True) / gain_ref[...]
    )
    grad_ref[...] = colbert_grad.T


def finish(core, half, other, colbert_proj, gain, proj):
    blocks, columns, lines, block = half.shape
    width, emb = colbert_proj.shape
    piece = pl.BlockSpec((blocks, 1, lines, block), lambda k, core: (0, k, 0, 0))
    return pl.pallas_call(
        finish_kernel,
        name="finish",
        grid_spec=pltpu.PrefetchScalarGridSpec(
            num_scalar_prefetch=1,
            grid=(columns,),
            in_specs=[
                piece,
                piece,
                pl.BlockSpec((block, emb), lambda k, core: (k, 0)),
                pl.BlockSpec((1, block), lambda k, core: (0, k)),
                pl.BlockSpec(memory_space=pl.ANY),
            ],
            out_specs=[
                pl.BlockSpec((width // 2, block), lambda k, core: (1 - core[0], k)),
                pl.BlockSpec((block, emb), lambda k, core: (k, 0)),
                pl.BlockSpec((1, block), lambda k, core: (0, k)),
            ],
        ),
        out_shape=[
            jax.ShapeDtypeStruct((width, width), F32),
            jax.ShapeDtypeStruct((width, emb), F32),
            jax.ShapeDtypeStruct((1, width), F32),
        ],
        input_output_aliases={5: 0},
        compiler_params=pltpu.CompilerParams(vmem_limit_bytes=8 * MIB),
        cost_estimate=pl.CostEstimate(
            flops=2 * width * width, transcendentals=0, bytes_accessed=4 * width * width
        ),
    )(core, half, other, colbert_proj, gain, proj)


SWAP = [(0, 1), (1, 0)]
FAR = [(k, k ^ 2) for k in range(4)]
NEAR = [(k, k ^ 1) for k in range(4)]


def pair_summed(kept, given, axis, pairs, out_type):
    taken = lax.ppermute(given, axis, pairs)
    return (kept.astype(F32) + taken.astype(F32)).astype(out_type)


def halves_summed(halves, axis, pairs, side, out_type):
    keep, give = side
    given = lax.dynamic_index_in_dim(halves, give, 0, False)
    kept = lax.dynamic_index_in_dim(halves, keep, 0, False)
    return pair_summed(kept, given, axis, pairs, out_type)


def query_gathered(own):
    held = own[None]
    for axis, pairs in ((CORE, SWAP), ("neg_0", NEAR), ("neg_0", FAR)):
        held = jnp.concatenate([held, lax.ppermute(held, axis, pairs)])
    return held, lax.ppermute(held, "neg_1", SWAP)


def pack_kernel(own_ref, taken_ref, out_ref):
    for k in range(out_ref.shape[0]):
        out_ref[k, 0] = own_ref[...]
        out_ref[k, 1] = taken_ref[...]


def passage_copies(own, taken, copies):
    shape = (copies, 2, *own.shape)
    return pl.pallas_call(
        pack_kernel,
        name="passage_copies",
        compiler_params=pltpu.CompilerParams(vmem_limit_bytes=8 * MIB),
        out_specs=whole(shape),
        out_shape=pltpu.HBM(shape, BF16),
    )(own, taken)


def spread_kernel(parts_ref, out_ref):
    total = parts_ref[0].astype(F32)
    for k in range(1, parts_ref.shape[0]):
        total += parts_ref[k].astype(F32)
    out_ref[...] = jnp.broadcast_to(total.astype(BF16)[None], out_ref.shape)


def summed_copies(parts):
    return pl.pallas_call(
        spread_kernel,
        name="summed_copies",
        in_specs=[pl.BlockSpec(memory_space=pltpu.VMEM)],
        out_specs=whole(parts.shape),
        out_shape=pltpu.HBM(parts.shape, BF16),
    )(parts)


def body(
    query_emb, positive, passage_emb, lengths, residual, context, out_proj, norm_gain, colbert_proj
):
    query_dev, query_len, emb = query_emb.shape
    neg_size, dp_size, cross_size = lax.axis_size(NEG), lax.axis_size(DP), lax.axis_size(CROSS)
    place, core = lax.axis_index(NEG), lax.axis_index(CORE)
    spot = jnp.arange(emb)[None] - place * query_dev
    wanted = jnp.sum(
        jnp.where(spot == jnp.arange(query_dev)[:, None], positive[:, None], 0), axis=0
    )
    query_own = jnp.concatenate(
        [
            query_emb.reshape(query_dev * query_len, emb),
            jnp.broadcast_to(wanted.astype(BF16)[None], (EXTRA, emb)),
        ]
    )
    passage_own = jnp.concatenate(
        [
            passage_emb.reshape(-1, emb),
            jnp.broadcast_to((lengths - LEAST).astype(BF16)[:, None], (EXTRA, emb)),
        ]
    )
    passage_pair = passage_copies(
        passage_own, lax.ppermute(passage_own, "dp_1", SWAP), lax.axis_size("dp_0")
    )
    passage_pack = exchange(passage_pair, "dp_0").reshape(dp_size, *passage_own.shape)
    queries = query_gathered(query_own)
    group = jnp.arange(dp_size) ^ lax.axis_index("dp_1")
    ids = jnp.broadcast_to((group * neg_size + place).astype(F32)[:, None], (dp_size, emb))
    row, column = lax.axis_index("neg_1"), lax.axis_index("neg_0")
    flip = (row * 8 + column * 2 + core)[None]
    sides = [
        (own.astype(jnp.uint32), (1 - own).astype(jnp.uint32))
        for own in (row, column // 2, column % 2)
    ]
    queries, sides = lax.optimization_barrier((queries, sides))
    row_side, far_side, near_side = sides
    spread, mixed, query_rows, inverse, similar, stats = forward_tile(
        flip, *queries, passage_pack, ids, query_len
    )
    stats = exchange(stats, NEG)
    passage_parts, kept, given = backward_tile(
        core[None], neg_size, query_rows, spread, mixed, inverse, similar, stats, query_len
    )
    residual, kept, given = lax.optimization_barrier((residual, kept, given))
    early = early_rows(residual, context, out_proj)
    query_part = pair_summed(kept, given, CORE, SWAP, BF16)
    query_part = halves_summed(query_part, "neg_1", SWAP, row_side, F32)
    passage_parts = exchange(passage_parts.reshape(passage_pair.shape), "dp_0")
    passage_parts, query_part, early = lax.optimization_barrier((passage_parts, query_part, early))
    normed, inv_std, context_t = early
    own_part, given_part = folded(passage_parts)
    taken_part = lax.ppermute(given_part, "dp_1", SWAP)
    query_part = query_part.reshape(2, 2, *query_part.shape[1:])
    query_part = halves_summed(query_part, "neg_0", FAR, far_side, F32)
    taken_part, query_part = lax.optimization_barrier((taken_part, query_part))
    residual_grad, kept, given, loss_sum = late_rows(
        core[None], dp_size, own_part, taken_part, normed, inv_std, norm_gain[None], colbert_proj, context_t
    )
    half = pair_summed(kept, given, CORE, SWAP, BF16)
    context_grad = jnp.dot(residual_grad, out_proj.T, preferred_element_type=F32).astype(BF16)
    query_grad = halves_summed(query_part, "neg_0", NEAR, near_side, F32)
    half, context_grad, query_grad = lax.optimization_barrier((half, context_grad, query_grad))
    query_grad = query_grad.reshape(query_dev, query_len, emb)
    slabs = exchange(half.reshape(dp_size * cross_size, *half.shape[2:]), DP + CROSS)
    half = exchange(summed_copies(slabs), DP + CROSS).reshape(half.shape)
    other = lax.ppermute(half, CORE, SWAP)
    proj = own_rows(core[None], half, out_proj.shape[0])
    out_proj_grad, colbert_grad, gain_grad = finish(
        core[None], half, other, colbert_proj, norm_gain[None], proj
    )
    loss = loss_sum[0, 0] / (query_dev * dp_size * neg_size)
    return (
        loss,
        query_grad,
        residual_grad,
        context_grad,
        out_proj_grad,
        colbert_grad,
        gain_grad[0],
    )


def solution(mesh):
    split = Mesh(mesh.devices.reshape(mesh.shape["dp"] // 2, 2, 4, 2, 2), DP_NEG)
    placed = (
        P(DP_NEG, None, None),
        P(DP_NEG),
        P(DP_NEG, None, None),
        P(DP_NEG),
        P(DP_NEG, None),
        P(DP_NEG, None),
        P(),
        P(),
        P(),
    )
    return jax.shard_map(
        body,
        mesh=split,
        in_specs=placed,
        out_specs=(P(), P(DP_NEG, None, None), P(DP_NEG, None), P(DP_NEG, None), P(), P(), P()),
        check_vma=False,
    )
```

```python
import functools

import jax
import jax.numpy as jnp
from jax import lax
from jax.experimental import pallas as pl
from jax.experimental.pallas import tpu as pltpu
from jax.sharding import Mesh
from jax.sharding import PartitionSpec as P

DP = ("dp_0", "dp_1")
NEG = ("neg_0", "neg_1", "neg_2")
CROSS = ("neg_0", "neg_1")
CORE = "neg_2"
DP_NEG = DP + NEG
BF16 = jnp.bfloat16
F32 = jnp.float32
EXTRA = 8
LEAST = 256
MIB = 1 << 20


def dot(a, b, dims, precision=None):
    return lax.dot_general(a, b, (dims, ((), ())), precision=precision, preferred_element_type=F32)


def token_query(rows, queries, query_len, transposed=False):
    shape = (queries, rows) if transposed else (rows, queries)
    row = lax.broadcasted_iota(jnp.int32, shape, 1 if transposed else 0)
    query = lax.broadcasted_iota(jnp.int32, shape, 0 if transposed else 1)
    first = query * query_len
    return ((row >= first) & (row < first + query_len)).astype(F32)


def whole(shape):
    return pl.BlockSpec(shape, lambda *_: (0,) * len(shape))


def stored(k):
    core, row, near, far = k % 2, k // 2 % 2, k // 4 % 2, k // 8
    return row * 8 + far * 4 + near * 2 + core


def forward_kernel(
    query_len,
    group,
    flip_ref,
    near_ref,
    far_ref,
    p_ref,
    ids_ref,
    exp_ref,
    mix_ref,
    own_ref,
    inv_ref,
    sim_ref,
    stats_ref,
    rows_ref,
    length_ref,
):
    passage = pl.program_id(0)
    half, q_rows, width = near_ref.shape[0], near_ref.shape[1] - EXTRA, near_ref.shape[2]
    parts = 2 * half
    slots = p_ref.shape[1] - EXTRA
    count, rows = inv_ref.shape
    queries = rows // query_len
    chunk = group * q_rows
    steps = parts // group
    tokens = p_ref[0, :slots, :]
    length = p_ref[0, slots : slots + 1, :].astype(F32) + float(LEAST)
    length_ref[pl.ds(passage, 1), :] = length
    wide = jnp.concatenate([length] * ((slots - LEAST) // width), axis=1)
    position = lax.broadcasted_iota(jnp.int32, wide.shape, 1).astype(F32) + float(LEAST)
    bias = jnp.where(position < wide, 0.0, -1e30)
    lane = lax.broadcasted_iota(jnp.int32, (chunk, width), 1)

    @pl.when(passage == 0)
    def _():
        rows_ref[...] = jnp.zeros_like(rows_ref)
        for k in range(parts):
            at = stored(k) ^ flip_ref[0]
            spot = at % half
            own_ref[k * q_rows : (k + 1) * q_rows, :] = jnp.where(
                at < half, near_ref[spot, :q_rows, :], far_ref[spot, :q_rows, :]
            )

    def scores(step):
        block = own_ref[step * chunk : (step + 1) * chunk, :]
        return dot(block, tokens, ((1,), (1,)))

    ahead = scores(0)
    late = None
    for step in range(steps):
        now = ahead
        if step + 1 < steps:
            ahead = scores(step + 1)
        if late is not None:
            mix_ref[passage, pl.ds((step - 1) * chunk, chunk), :] = dot(late, tokens, ((1,), (0,)))
        sure, rest = now[:, :LEAST], now[:, LEAST:] + bias
        highest = jnp.maximum(
            jnp.max(sure, axis=1, keepdims=True), jnp.max(rest, axis=1, keepdims=True)
        )
        sure = jnp.exp(sure - highest)
        rest = jnp.exp(rest - highest)
        total = jnp.sum(sure, axis=1, keepdims=True) + jnp.sum(rest, axis=1, keepdims=True)
        late = jnp.concatenate([sure.astype(BF16), rest.astype(BF16)], axis=1)
        at = pl.ds(step * chunk, chunk)
        exp_ref[passage, at, :] = late
        rows_ref[at, :] = jnp.where(
            lane == passage,
            highest + jnp.log(total),
            jnp.where(lane == passage + width // 2, total, rows_ref[at, :]),
        )
    mix_ref[passage, pl.ds((steps - 1) * chunk, chunk), :] = dot(late, tokens, ((1,), (0,)))

    @pl.when(passage == pl.num_programs(0) - 1)
    def _():
        turned = rows_ref[...].T
        inv_ref[...] = 1.0 / turned[width // 2 : width // 2 + count]
        similar = dot(
            turned[:count], token_query(rows, queries, query_len), ((1,), (0,)), lax.Precision.HIGHEST
        )
        similar = similar - float(query_len) * jnp.log(length_ref[...])[:, :queries]
        wanted = jnp.sum(
            near_ref[:, q_rows, :].astype(F32) + far_ref[:, q_rows, :].astype(F32),
            axis=0,
            keepdims=True,
        )[:, :queries]
        hit = (wanted == ids_ref[:, :queries]).astype(F32)
        highest = jnp.max(similar, axis=0, keepdims=True)
        total = jnp.sum(jnp.exp(similar - highest), axis=0, keepdims=True)
        positive = jnp.sum(jnp.where(hit > 0.0, similar, 0.0), axis=0, keepdims=True)
        sim_ref[0] = similar
        sim_ref[1] = hit
        stats = jnp.concatenate([highest, total, positive, jnp.zeros((5, queries), F32)], axis=0)
        stats = jnp.concatenate([stats, jnp.zeros((8, width - queries), F32)], axis=1)
        stats_ref[...] = stats


def forward_tile(flip, near, far, passage_pack, ids, query_len, group=8):
    half, q_rows, width = near.shape
    parts, q_rows = 2 * half, q_rows - EXTRA
    count, slots = passage_pack.shape[0], passage_pack.shape[1] - EXTRA
    rows = parts * q_rows
    queries = rows // query_len
    work = rows * slots * count
    return pl.pallas_call(
        functools.partial(forward_kernel, query_len, group),
        name="forward_tile",
        grid=(count,),
        in_specs=[
            pl.BlockSpec(memory_space=pltpu.SMEM),
            whole(near.shape),
            whole(far.shape),
            pl.BlockSpec((1, slots + EXTRA, width), lambda p: (p, 0, 0)),
            whole(ids.shape),
        ],
        out_specs=[
            pl.BlockSpec(memory_space=pltpu.VMEM),
            pl.BlockSpec(memory_space=pltpu.VMEM),
            pl.BlockSpec(memory_space=pltpu.VMEM),
            whole((count, rows)),
            whole((2, count, queries)),
            whole((8, width)),
        ],
        out_shape=[
            pltpu.VMEM((count, rows, slots), BF16),
            pltpu.VMEM((count, rows, width), F32),
            pltpu.VMEM((rows, width), BF16),
            jax.ShapeDtypeStruct((count, rows), F32),
            jax.ShapeDtypeStruct((2, count, queries), F32),
            jax.ShapeDtypeStruct((8, width), F32),
        ],
        scratch_shapes=[pltpu.VMEM((rows, width), F32), pltpu.VMEM((count, width), F32)],
        compiler_params=pltpu.CompilerParams(vmem_limit_bytes=16 * MIB),
        cost_estimate=pl.CostEstimate(
            flops=4 * work * width, transcendentals=work, bytes_accessed=4 * work
        ),
    )(flip, near, far, passage_pack, ids)


def split_lines(value):
    high = value.astype(BF16).astype(F32)
    low = (value - high).astype(BF16).astype(F32)
    last = value - high - low
    row = lax.broadcasted_iota(jnp.int32, value.shape, 0)
    lines = jnp.where(row == 0, high, jnp.where(row == 1, low, jnp.where(row == 2, last, 0.0)))
    return lines.astype(BF16)


def backward_kernel(
    query_len,
    parts,
    core_ref,
    flip_ref,
    own_ref,
    exp_ref,
    mix_ref,
    inv_ref,
    sim_ref,
    near_ref,
    far_ref,
    pg_ref,
    kept_ref,
    given_ref,
    qt,
    halves,
):
    count, rows, slots = exp_ref.shape
    width, q_rows = own_ref.shape[1], rows // parts
    queries = rows // query_len
    for k in range(parts):
        qt[:, k * q_rows : (k + 1) * q_rows] = own_ref[k * q_rows : (k + 1) * q_rows, :].T
    stats = []
    for k in range(parts):
        at = stored(k) ^ flip_ref[0]
        spot = at % (parts // 2)
        stats.append(jnp.where(at < parts // 2, near_ref[spot], far_ref[spot]))
    stats = jnp.stack(stats)
    highest_of = stats[:, 0, :queries]
    highest = jnp.max(highest_of, axis=0, keepdims=True)
    total = jnp.sum(
        stats[:, 1, :queries] * jnp.exp(highest_of - highest), axis=0, keepdims=True
    )
    positive = jnp.sum(stats[:, 2, :queries], axis=0, keepdims=True)
    log_total = highest + jnp.log(total)
    coefficient = jnp.exp(sim_ref[0] - log_total) - sim_ref[1]
    scale = inv_ref[...] * dot(
        coefficient,
        token_query(rows, queries, query_len, True),
        ((1,), (0,)),
        lax.Precision.HIGHEST,
    )
    lines = split_lines(
        jnp.broadcast_to(jnp.sum(log_total - positive, axis=1, keepdims=True), (EXTRA, width))
    )
    for p in range(count):
        weighted = (qt[...].astype(F32) * scale[p : p + 1]).astype(BF16)
        pg_ref[p, :slots, :] = dot(weighted, exp_ref[p], ((1,), (0,))).T.astype(BF16)
        pg_ref[p, slots:, :] = lines
    turned = jnp.concatenate([scale, jnp.zeros((width - count, rows), F32)], axis=0).T
    for k in range(parts):
        at = slice(k * q_rows, (k + 1) * q_rows)
        sums = mix_ref[0, at, :] * turned[at, :1]
        for p in range(1, count):
            sums += mix_ref[p, at, :] * turned[at, p : p + 1]
        halves[k % 2, k // 2 % 2, k // 4] = sums.astype(BF16)
    kept_ref[...] = halves[core_ref[0]]
    given_ref[...] = halves[1 - core_ref[0]]


def backward_tile(core, flip, parts, own, spread, mixed, inverse, similar, near, far, query_len):
    count, rows, slots = spread.shape
    q_rows, width = rows // parts, own.shape[1]
    work = rows * slots * count
    return pl.pallas_call(
        functools.partial(backward_kernel, query_len, parts),
        name="backward_tile",
        in_specs=[pl.BlockSpec(memory_space=pltpu.SMEM)] * 2
        + [pl.BlockSpec(memory_space=pltpu.VMEM)] * 7,
        out_shape=[
            pltpu.HBM((count, slots + EXTRA, width), BF16),
            jax.ShapeDtypeStruct((2, parts // 4, q_rows, width), BF16),
            jax.ShapeDtypeStruct((2, parts // 4, q_rows, width), BF16),
        ],
        out_specs=[whole((count, slots + EXTRA, width))]
        + [whole((2, parts // 4, q_rows, width))] * 2,
        scratch_shapes=[
            pltpu.VMEM((width, rows), BF16),
            pltpu.VMEM((2, 2, parts // 4, q_rows, width), BF16),
        ],
        compiler_params=pltpu.CompilerParams(vmem_limit_bytes=16 * MIB),
        cost_estimate=pl.CostEstimate(
            flops=2 * work * width, transcendentals=0, bytes_accessed=3 * work
        ),
    )(core, flip, own, spread, mixed, inverse, similar, near, far)


def early_kernel(resid_ref, context_ref, proj_ref, normed_ref, inv_ref, context_t_ref):
    context = context_ref[...]
    hidden = resid_ref[...].astype(F32) + dot(context, proj_ref[...], ((1,), (0,)))
    centred = hidden - jnp.mean(hidden, axis=1, keepdims=True)
    variance = jnp.mean(centred * centred, axis=1, keepdims=True)
    inv_std = 1.0 / jnp.sqrt(variance + 1e-05)
    normed_ref[...] = centred * inv_std
    inv_ref[...] = jnp.broadcast_to(inv_std, inv_ref.shape)
    context_t_ref[...] = context.T


def early_rows(residual, context, out_proj, block=128):
    rows, width = residual.shape
    return pl.pallas_call(
        early_kernel,
        name="early_rows",
        grid=(rows // block,),
        in_specs=[
            pl.BlockSpec((block, width), lambda r: (r, 0)),
            pl.BlockSpec((block, width), lambda r: (r, 0)),
            whole(out_proj.shape),
        ],
        out_specs=[
            pl.BlockSpec((block, width), lambda r: (r, 0)),
            pl.BlockSpec((block, 128), lambda r: (r, 0)),
            pl.BlockSpec((width, block), lambda r: (0, r)),
        ],
        out_shape=[
            pltpu.HBM((rows, width), F32),
            pltpu.HBM((rows, 128), F32),
            pltpu.HBM((width, rows), BF16),
        ],
        compiler_params=pltpu.CompilerParams(vmem_limit_bytes=10 * MIB),
        cost_estimate=pl.CostEstimate(
            flops=2 * rows * width * width, transcendentals=0, bytes_accessed=10 * rows * width
        ),
    )(residual, context, out_proj)


def late_kernel(
    core_ref,
    parts_ref,
    normed_far,
    inv_far,
    gain_ref,
    colbert_ref,
    context_far,
    resid_ref,
    kept_ref,
    given_ref,
    loss_ref,
    normed_ref,
    inv_ref,
    context_t_ref,
    sums_ref,
    sems,
):
    loads = [
        pltpu.make_async_copy(far, near, sems.at[k])
        for k, (far, near) in enumerate(
            ((normed_far, normed_ref), (inv_far, inv_ref), (context_far, context_t_ref))
        )
    ]
    for load in loads:
        load.start()
    slots = parts_ref.shape[1] - EXTRA
    width = normed_ref.shape[1]
    total = parts_ref[0].astype(F32)
    for k in range(1, parts_ref.shape[0]):
        total = total + parts_ref[k].astype(F32)
    loss_ref[...] = jnp.broadcast_to(
        jnp.sum(total[slots:], axis=0, keepdims=True), loss_ref.shape
    )
    grad = total[:slots].astype(BF16)
    gain = gain_ref[...]
    gained = dot(grad, colbert_ref[...], ((1,), (1,))) * gain
    grad_t = grad.T
    for load in loads[:2]:
        load.wait()
    normed = normed_ref[...]
    inv_std = inv_ref[:, :1]
    resid = inv_std * (
        gained
        - jnp.mean(gained, axis=1, keepdims=True)
        - normed * jnp.mean(gained * normed, axis=1, keepdims=True)
    )
    resid = resid.astype(BF16)
    resid_ref[...] = resid
    scaled = (normed * gain).astype(BF16)
    blocks, lines = sums_ref.shape[1], sums_ref.shape[3]
    thin = grad.shape[1] // (2 * blocks)
    thick = lines - thin
    colbert = dot(grad_t, scaled, ((1,), (0,)))
    for k in range(2 * blocks):
        for j in range(width // 128):
            sums_ref[k // blocks, k % blocks, j, thick:, :] = colbert[
                k * thin : (k + 1) * thin, j * 128 : (j + 1) * 128
            ].astype(BF16)
    loads[2].wait()
    group = 4
    for first in range(0, 2 * blocks, group):
        part = dot(
            context_t_ref[first * thick : (first + group) * thick, :], resid, ((1,), (0,))
        ).astype(BF16)
        for k in range(first, first + group):
            at = (k - first) * thick
            for j in range(width // 128):
                sums_ref[k // blocks, k % blocks, j, :thick, :] = part[
                    at : at + thick, j * 128 : (j + 1) * 128
                ]
    kept_ref[...] = sums_ref[core_ref[0]]
    given_ref[...] = sums_ref[1 - core_ref[0]]


def far(array):
    return pltpu.with_memory_space_constraint(array, pltpu.HBM)


def late_rows(core, blocks, pieces, normed, inv_std, gain, colbert_proj, context_t):
    rows, width = normed.shape
    emb = colbert_proj.shape[1]
    shape = (blocks, width // 128, (width + emb) // (2 * blocks), 128)
    return pl.pallas_call(
        late_kernel,
        name="late_rows",
        in_specs=[
            pl.BlockSpec(memory_space=pltpu.SMEM),
            whole(pieces.shape),
            pl.BlockSpec(memory_space=pltpu.HBM),
            pl.BlockSpec(memory_space=pltpu.HBM),
            whole(gain.shape),
            whole(colbert_proj.shape),
            pl.BlockSpec(memory_space=pltpu.HBM),
        ],
        scratch_shapes=[
            pltpu.VMEM(normed.shape, F32),
            pltpu.VMEM(inv_std.shape, F32),
            pltpu.VMEM(context_t.shape, BF16),
            pltpu.VMEM((2, *shape), BF16),
            pltpu.SemaphoreType.DMA((3,)),
        ],
        out_shape=[
            jax.ShapeDtypeStruct((rows, width), BF16),
            jax.ShapeDtypeStruct(shape, BF16),
            jax.ShapeDtypeStruct(shape, BF16),
            jax.ShapeDtypeStruct((8, emb), F32),
        ],
        compiler_params=pltpu.CompilerParams(vmem_limit_bytes=24 * MIB),
        cost_estimate=pl.CostEstimate(
            flops=2 * rows * width * (width + 2 * emb),
            transcendentals=0,
            bytes_accessed=14 * rows * width,
        ),
    )(core, pieces, far(normed), far(inv_std), gain, colbert_proj, far(context_t))


def exchange(pieces, axis):
    return lax.all_to_all(pieces, axis, 0, 0, tiled=True)


def own_kernel(core_ref, half_ref, proj_ref):
    blocks, columns, _, block = half_ref.shape
    thick = proj_ref.shape[0] // blocks
    for k in range(blocks):
        for j in range(columns):
            proj_ref[k * thick : (k + 1) * thick, j * block : (j + 1) * block] = half_ref[
                k, j, :thick, :
            ].astype(F32)


def own_rows(core, half, width, group=4):
    blocks, columns, lines, block = half.shape
    return pl.pallas_call(
        own_kernel,
        name="own_rows",
        grid_spec=pltpu.PrefetchScalarGridSpec(
            num_scalar_prefetch=1,
            grid=(columns // group,),
            in_specs=[pl.BlockSpec((blocks, group, lines, block), lambda k, core: (0, k, 0, 0))],
            out_specs=pl.BlockSpec((width // 2, group * block), lambda k, core: (core[0], k)),
        ),
        out_shape=pltpu.HBM((width, width), F32),
        compiler_params=pltpu.CompilerParams(vmem_limit_bytes=12 * MIB),
        cost_estimate=pl.CostEstimate(
            flops=width * width, transcendentals=0, bytes_accessed=4 * width * width
        ),
    )(core, half)


def finish_kernel(
    core_ref, half_ref, other_ref, colbert_ref, gain_ref, _, proj_ref, grad_ref, gain_grad_ref
):
    blocks, columns, _, block = half_ref.shape
    thick = proj_ref.shape[0] // blocks
    even = core_ref[0] == 0
    for j in range(columns):
        at = slice(j * block, (j + 1) * block)
        own, others = [], []
        for k in range(blocks):
            piece = other_ref[k, j].astype(F32)
            proj_ref[k * thick : (k + 1) * thick, at] = piece[:thick]
            others.append(piece[thick:])
            own.append(half_ref[k, j].astype(F32)[thick:])
        own, others = jnp.concatenate(own, axis=0), jnp.concatenate(others, axis=0)
        colbert_grad = jnp.concatenate(
            [jnp.where(even, own, others), jnp.where(even, others, own)], axis=0
        )
        colbert_t = colbert_ref[at, :].astype(F32).T
        gain_grad_ref[:, at] = (
            jnp.sum(colbert_grad * colbert_t, axis=0, keepdims=True) / gain_ref[:, at]
        )
        grad_ref[at, :] = colbert_grad.T


def finish(core, half, other, colbert_proj, gain, proj, group=4):
    blocks, columns, lines, block = half.shape
    width, emb = colbert_proj.shape
    piece = pl.BlockSpec((blocks, group, lines, block), lambda k, core: (0, k, 0, 0))
    span = group * block
    return pl.pallas_call(
        finish_kernel,
        name="finish",
        grid_spec=pltpu.PrefetchScalarGridSpec(
            num_scalar_prefetch=1,
            grid=(columns // group,),
            in_specs=[
                piece,
                piece,
                pl.BlockSpec((span, emb), lambda k, core: (k, 0)),
                pl.BlockSpec((1, span), lambda k, core: (0, k)),
                pl.BlockSpec(memory_space=pl.ANY),
            ],
            out_specs=[
                pl.BlockSpec((width // 2, span), lambda k, core: (1 - core[0], k)),
                pl.BlockSpec((span, emb), lambda k, core: (k, 0)),
                pl.BlockSpec((1, span), lambda k, core: (0, k)),
            ],
        ),
        out_shape=[
            jax.ShapeDtypeStruct((width, width), F32),
            jax.ShapeDtypeStruct((width, emb), F32),
            jax.ShapeDtypeStruct((1, width), F32),
        ],
        input_output_aliases={5: 0},
        compiler_params=pltpu.CompilerParams(vmem_limit_bytes=12 * MIB),
        cost_estimate=pl.CostEstimate(
            flops=2 * width * width, transcendentals=0, bytes_accessed=4 * width * width
        ),
    )(core, half, other, colbert_proj, gain, proj)


SWAP = [(0, 1), (1, 0)]
FAR = [(k, k ^ 2) for k in range(4)]
NEAR = [(k, k ^ 1) for k in range(4)]


def pair_summed(kept, given, axis, pairs, out_type):
    taken = lax.ppermute(given, axis, pairs)
    return (kept.astype(F32) + taken.astype(F32)).astype(out_type)


def halves_summed(halves, axis, pairs, side, out_type):
    keep, give = side
    given = lax.dynamic_index_in_dim(halves, give, 0, False)
    kept = lax.dynamic_index_in_dim(halves, keep, 0, False)
    return pair_summed(kept, given, axis, pairs, out_type)


def doubled(held, axis, pairs):
    return jnp.concatenate([held, lax.ppermute(held, axis, pairs)])


def fours_gathered(four):
    held = doubled(four, "neg_0", FAR)
    return held, lax.ppermute(held, "neg_1", SWAP)


def pack_kernel(length_ref, p_ref, out_ref):
    slots = p_ref.shape[1]
    extra = jnp.full((EXTRA, p_ref.shape[2]), (length_ref[0] - LEAST).astype(F32)).astype(BF16)
    for k in range(out_ref.shape[0]):
        out_ref[k, :slots, :] = p_ref[0]
        out_ref[k, slots:, :] = extra


def passage_copies(passage_emb, lengths, copies):
    _, slots, width = passage_emb.shape
    return pl.pallas_call(
        pack_kernel,
        name="passage_copies",
        in_specs=[
            pl.BlockSpec(memory_space=pltpu.SMEM),
            pl.BlockSpec(memory_space=pltpu.VMEM),
        ],
        out_specs=whole((copies, slots + EXTRA, width)),
        out_shape=pltpu.HBM((copies, slots + EXTRA, width), BF16),
    )(lengths, passage_emb)


def spread_kernel(parts_ref, out_ref):
    total = parts_ref[0].astype(F32)
    for k in range(1, parts_ref.shape[0]):
        total += parts_ref[k].astype(F32)
    out_ref[...] = jnp.broadcast_to(total.astype(BF16)[None], out_ref.shape)


def summed_copies(parts):
    return pl.pallas_call(
        spread_kernel,
        name="summed_copies",
        in_specs=[pl.BlockSpec(memory_space=pltpu.VMEM)],
        out_specs=whole(parts.shape),
        out_shape=pltpu.HBM(parts.shape, BF16),
    )(parts)


def body(
    query_emb, positive, passage_emb, lengths, residual, context, out_proj, norm_gain, colbert_proj
):
    query_dev, query_len, emb = query_emb.shape
    neg_size, dp_size, cross_size = lax.axis_size(NEG), lax.axis_size(DP), lax.axis_size(CROSS)
    place, core = lax.axis_index(NEG), lax.axis_index(CORE)
    spot = jnp.arange(emb)[None] - place * query_dev
    wanted = jnp.sum(
        jnp.where(spot == jnp.arange(query_dev)[:, None], positive[:, None], 0), axis=0
    )
    query_own = jnp.concatenate(
        [
            query_emb.reshape(query_dev * query_len, emb),
            jnp.broadcast_to(wanted.astype(BF16)[None], (EXTRA, emb)),
        ]
    )
    query_four = doubled(doubled(query_own[None], CORE, SWAP), "neg_0", NEAR)
    copies, query_four = lax.optimization_barrier(
        (passage_copies(passage_emb, lengths, dp_size), query_four)
    )
    passage_pack = exchange(copies, DP)
    queries = fours_gathered(query_four)
    ids = jnp.broadcast_to((jnp.arange(dp_size) * neg_size + place).astype(F32)[:, None], (dp_size, emb))
    row, column = lax.axis_index("neg_1"), lax.axis_index("neg_0")
    flip = (row * 8 + column * 2 + core)[None]
    sides = [
        (own.astype(jnp.uint32), (1 - own).astype(jnp.uint32))
        for own in (row, column // 2, column % 2)
    ]
    queries, sides = lax.optimization_barrier((queries, sides))
    row_side, far_side, near_side = sides
    spread, mixed, query_rows, inverse, similar, stats = forward_tile(
        flip, *queries, passage_pack, ids, query_len
    )
    stats = fours_gathered(doubled(doubled(stats[None], CORE, SWAP), "neg_0", NEAR))
    passage_parts, kept, given = backward_tile(
        core[None],
        flip,
        neg_size,
        query_rows,
        spread,
        mixed,
        inverse,
        similar,
        *stats,
        query_len,
    )
    residual, kept, given = lax.optimization_barrier((residual, kept, given))
    early = early_rows(residual, context, out_proj)
    query_part = pair_summed(kept, given, CORE, SWAP, BF16)
    query_part = halves_summed(query_part, "neg_1", SWAP, row_side, F32)
    passage_parts = exchange(passage_parts, DP)
    passage_parts, query_part, early = lax.optimization_barrier((passage_parts, query_part, early))
    normed, inv_std, context_t = early
    residual_grad, kept, given, loss_sum = late_rows(
        core[None], dp_size, passage_parts, normed, inv_std, norm_gain[None], colbert_proj, context_t
    )
    half = pair_summed(kept, given, CORE, SWAP, BF16)
    context_grad = jnp.dot(residual_grad, out_proj.T, preferred_element_type=F32).astype(BF16)
    query_part = query_part.reshape(2, 2, *query_part.shape[1:])
    query_part = halves_summed(query_part, "neg_0", FAR, far_side, F32)
    half, context_grad, query_part = lax.optimization_barrier((half, context_grad, query_part))
    slabs = exchange(half.reshape(dp_size * cross_size, *half.shape[2:]), DP + CROSS)
    half = exchange(summed_copies(slabs), DP + CROSS).reshape(half.shape)
    half, query_part = lax.optimization_barrier((half, query_part))
    query_grad = halves_summed(query_part, "neg_0", NEAR, near_side, F32)
    query_grad = query_grad.reshape(query_dev, query_len, emb)
    other = lax.ppermute(half, CORE, SWAP)
    proj = own_rows(core[None], half, out_proj.shape[0])
    out_proj_grad, colbert_grad, gain_grad = finish(
        core[None], half, other, colbert_proj, norm_gain[None], proj
    )
    loss = loss_sum[0, 0] / (query_dev * dp_size * neg_size)
    return (
        loss,
        query_grad,
        residual_grad,
        context_grad,
        out_proj_grad,
        colbert_grad,
        gain_grad[0],
    )


def solution(mesh):
    split = Mesh(mesh.devices.reshape(mesh.shape["dp"] // 2, 2, 4, 2, 2), DP_NEG)
    placed = (
        P(DP_NEG, None, None),
        P(DP_NEG),
        P(DP_NEG, None, None),
        P(DP_NEG),
        P(DP_NEG, None),
        P(DP_NEG, None),
        P(),
        P(),
        P(),
    )
    return jax.shard_map(
        body,
        mesh=split,
        in_specs=placed,
        out_specs=(P(), P(DP_NEG, None, None), P(DP_NEG, None), P(DP_NEG, None), P(), P(), P()),
        check_vma=False,
    )
```

```python
import functools

import jax
import jax.numpy as jnp
from jax import lax
from jax.experimental import pallas as pl
from jax.experimental.pallas import tpu as pltpu
from jax.sharding import Mesh
from jax.sharding import PartitionSpec as P

DP = ("dp_0", "dp_1")
NEG = ("neg_0", "neg_1", "neg_2")
CROSS = ("neg_0", "neg_1")
CORE = "neg_2"
DP_NEG = DP + NEG
BF16 = jnp.bfloat16
F32 = jnp.float32
EXTRA = 8
LEAST = 256
MIB = 1 << 20


def dot(a, b, dims, precision=None):
    return lax.dot_general(a, b, (dims, ((), ())), precision=precision, preferred_element_type=F32)


def token_query(rows, queries, query_len, transposed=False):
    shape = (queries, rows) if transposed else (rows, queries)
    row = lax.broadcasted_iota(jnp.int32, shape, 1 if transposed else 0)
    query = lax.broadcasted_iota(jnp.int32, shape, 0 if transposed else 1)
    first = query * query_len
    return ((row >= first) & (row < first + query_len)).astype(F32)


def whole(shape):
    return pl.BlockSpec(shape, lambda *_: (0,) * len(shape))


def stored(k):
    core, row, near, far = k % 2, k // 2 % 2, k // 4 % 2, k // 8
    return row * 8 + far * 4 + near * 2 + core


def forward_kernel(
    query_len,
    group,
    flip_ref,
    near_ref,
    far_ref,
    p_ref,
    ids_ref,
    exp_ref,
    mix_ref,
    own_ref,
    inv_ref,
    sim_ref,
    stats_ref,
    rows_ref,
    length_ref,
):
    passage = pl.program_id(0)
    half, q_rows, width = near_ref.shape[0], near_ref.shape[1] - EXTRA, near_ref.shape[2]
    parts = 2 * half
    slots = p_ref.shape[1] - EXTRA
    count, rows = inv_ref.shape
    queries = rows // query_len
    chunk = group * q_rows
    steps = parts // group
    tokens = p_ref[0, :slots, :]
    length = p_ref[0, slots : slots + 1, :].astype(F32) + float(LEAST)
    length_ref[pl.ds(passage, 1), :] = length
    wide = jnp.concatenate([length] * ((slots - LEAST) // width), axis=1)
    position = lax.broadcasted_iota(jnp.int32, wide.shape, 1).astype(F32) + float(LEAST)
    bias = jnp.where(position < wide, 0.0, -1e30)
    lane = lax.broadcasted_iota(jnp.int32, (chunk, width), 1)

    @pl.when(passage == 0)
    def _():
        rows_ref[...] = jnp.zeros_like(rows_ref)
        for k in range(parts):
            at = stored(k) ^ flip_ref[0]
            spot = at % half
            own_ref[k * q_rows : (k + 1) * q_rows, :] = jnp.where(
                at < half, near_ref[spot, :q_rows, :], far_ref[spot, :q_rows, :]
            )

    def scores(step):
        block = own_ref[step * chunk : (step + 1) * chunk, :]
        return dot(block, tokens, ((1,), (1,)))

    ahead = scores(0)
    late = None
    for step in range(steps):
        now = ahead
        if step + 1 < steps:
            ahead = scores(step + 1)
        if late is not None:
            mix_ref[passage, pl.ds((step - 1) * chunk, chunk), :] = dot(late, tokens, ((1,), (0,)))
        sure, rest = now[:, :LEAST], now[:, LEAST:] + bias
        highest = jnp.maximum(
            jnp.max(sure, axis=1, keepdims=True), jnp.max(rest, axis=1, keepdims=True)
        )
        sure = jnp.exp(sure - highest)
        rest = jnp.exp(rest - highest)
        total = jnp.sum(sure, axis=1, keepdims=True) + jnp.sum(rest, axis=1, keepdims=True)
        late = jnp.concatenate([sure.astype(BF16), rest.astype(BF16)], axis=1)
        at = pl.ds(step * chunk, chunk)
        exp_ref[passage, at, :] = late
        rows_ref[at, :] = jnp.where(
            lane == passage,
            highest + jnp.log(total),
            jnp.where(lane == passage + width // 2, total, rows_ref[at, :]),
        )
    mix_ref[passage, pl.ds((steps - 1) * chunk, chunk), :] = dot(late, tokens, ((1,), (0,)))

    @pl.when(passage == pl.num_programs(0) - 1)
    def _():
        turned = rows_ref[...].T
        inv_ref[...] = 1.0 / turned[width // 2 : width // 2 + count]
        similar = dot(
            turned[:count], token_query(rows, queries, query_len), ((1,), (0,)), lax.Precision.HIGHEST
        )
        similar = similar - float(query_len) * jnp.log(length_ref[...])[:, :queries]
        wanted = jnp.sum(
            near_ref[:, q_rows, :].astype(F32) + far_ref[:, q_rows, :].astype(F32),
            axis=0,
            keepdims=True,
        )[:, :queries]
        hit = (wanted == ids_ref[:, :queries]).astype(F32)
        highest = jnp.max(similar, axis=0, keepdims=True)
        total = jnp.sum(jnp.exp(similar - highest), axis=0, keepdims=True)
        positive = jnp.sum(jnp.where(hit > 0.0, similar, 0.0), axis=0, keepdims=True)
        sim_ref[0] = similar
        sim_ref[1] = hit
        stats = jnp.concatenate([highest, total, positive, jnp.zeros((5, queries), F32)], axis=0)
        stats = jnp.concatenate([stats, jnp.zeros((8, width - queries), F32)], axis=1)
        stats_ref[...] = jnp.broadcast_to(stats[None], stats_ref.shape)


def forward_tile(flip, near, far, passage_pack, ids, query_len, group=8):
    half, q_rows, width = near.shape
    parts, q_rows = 2 * half, q_rows - EXTRA
    count, slots = passage_pack.shape[0], passage_pack.shape[1] - EXTRA
    rows = parts * q_rows
    queries = rows // query_len
    work = rows * slots * count
    return pl.pallas_call(
        functools.partial(forward_kernel, query_len, group),
        name="forward_tile",
        grid=(count,),
        in_specs=[
            pl.BlockSpec(memory_space=pltpu.SMEM),
            whole(near.shape),
            whole(far.shape),
            pl.BlockSpec((1, slots + EXTRA, width), lambda p: (p, 0, 0)),
            whole(ids.shape),
        ],
        out_specs=[
            pl.BlockSpec(memory_space=pltpu.VMEM),
            pl.BlockSpec(memory_space=pltpu.VMEM),
            pl.BlockSpec(memory_space=pltpu.VMEM),
            whole((count, rows)),
            whole((2, count, queries)),
            whole((parts, 8, width)),
        ],
        out_shape=[
            pltpu.VMEM((count, rows, slots), BF16),
            pltpu.VMEM((count, rows, width), F32),
            pltpu.VMEM((rows, width), BF16),
            jax.ShapeDtypeStruct((count, rows), F32),
            jax.ShapeDtypeStruct((2, count, queries), F32),
            jax.ShapeDtypeStruct((parts, 8, width), F32),
        ],
        scratch_shapes=[pltpu.VMEM((rows, width), F32), pltpu.VMEM((count, width), F32)],
        compiler_params=pltpu.CompilerParams(vmem_limit_bytes=16 * MIB),
        cost_estimate=pl.CostEstimate(
            flops=4 * work * width, transcendentals=work, bytes_accessed=4 * work
        ),
    )(flip, near, far, passage_pack, ids)


def split_lines(value):
    high = value.astype(BF16).astype(F32)
    low = (value - high).astype(BF16).astype(F32)
    last = value - high - low
    row = lax.broadcasted_iota(jnp.int32, value.shape, 0)
    lines = jnp.where(row == 0, high, jnp.where(row == 1, low, jnp.where(row == 2, last, 0.0)))
    return lines.astype(BF16)


def backward_kernel(
    query_len,
    parts,
    core_ref,
    own_ref,
    exp_ref,
    mix_ref,
    inv_ref,
    sim_ref,
    stats_ref,
    pg_ref,
    kept_ref,
    given_ref,
    qt,
    halves,
):
    count, rows, slots = exp_ref.shape
    width, q_rows = own_ref.shape[1], rows // parts
    queries = rows // query_len
    for k in range(parts):
        qt[:, k * q_rows : (k + 1) * q_rows] = own_ref[k * q_rows : (k + 1) * q_rows, :].T
    highest_of = stats_ref[:, 0, :queries]
    highest = jnp.max(highest_of, axis=0, keepdims=True)
    total = jnp.sum(
        stats_ref[:, 1, :queries] * jnp.exp(highest_of - highest), axis=0, keepdims=True
    )
    positive = jnp.sum(stats_ref[:, 2, :queries], axis=0, keepdims=True)
    log_total = highest + jnp.log(total)
    coefficient = jnp.exp(sim_ref[0] - log_total) - sim_ref[1]
    scale = inv_ref[...] * dot(
        coefficient,
        token_query(rows, queries, query_len, True),
        ((1,), (0,)),
        lax.Precision.HIGHEST,
    )
    lines = split_lines(
        jnp.broadcast_to(jnp.sum(log_total - positive, axis=1, keepdims=True), (EXTRA, width))
    )
    for p in range(count):
        weighted = (qt[...].astype(F32) * scale[p : p + 1]).astype(BF16)
        pg_ref[p, :slots, :] = dot(weighted, exp_ref[p], ((1,), (0,))).T.astype(BF16)
        pg_ref[p, slots:, :] = lines
    turned = jnp.concatenate([scale, jnp.zeros((width - count, rows), F32)], axis=0).T
    for k in range(parts):
        at = slice(k * q_rows, (k + 1) * q_rows)
        sums = mix_ref[0, at, :] * turned[at, :1]
        for p in range(1, count):
            sums += mix_ref[p, at, :] * turned[at, p : p + 1]
        halves[k % 2, k // 2 % 2, k // 4] = sums.astype(BF16)
    kept_ref[...] = halves[core_ref[0]]
    given_ref[...] = halves[1 - core_ref[0]]


def backward_tile(core, parts, own, spread, mixed, inverse, similar, stats, query_len):
    count, rows, slots = spread.shape
    q_rows, width = rows // parts, own.shape[1]
    work = rows * slots * count
    return pl.pallas_call(
        functools.partial(backward_kernel, query_len, parts),
        name="backward_tile",
        in_specs=[pl.BlockSpec(memory_space=pltpu.SMEM)]
        + [pl.BlockSpec(memory_space=pltpu.VMEM)] * 6,
        out_shape=[
            pltpu.HBM((count, slots + EXTRA, width), BF16),
            jax.ShapeDtypeStruct((2, parts // 4, q_rows, width), BF16),
            jax.ShapeDtypeStruct((2, parts // 4, q_rows, width), BF16),
        ],
        out_specs=[whole((count, slots + EXTRA, width))]
        + [whole((2, parts // 4, q_rows, width))] * 2,
        scratch_shapes=[
            pltpu.VMEM((width, rows), BF16),
            pltpu.VMEM((2, 2, parts // 4, q_rows, width), BF16),
        ],
        compiler_params=pltpu.CompilerParams(vmem_limit_bytes=16 * MIB),
        cost_estimate=pl.CostEstimate(
            flops=2 * work * width, transcendentals=0, bytes_accessed=3 * work
        ),
    )(core, own, spread, mixed, inverse, similar, stats)


def early_kernel(resid_ref, context_ref, proj_ref, normed_ref, inv_ref, context_t_ref):
    context = context_ref[...]
    hidden = resid_ref[...].astype(F32) + dot(context, proj_ref[...], ((1,), (0,)))
    centred = hidden - jnp.mean(hidden, axis=1, keepdims=True)
    variance = jnp.mean(centred * centred, axis=1, keepdims=True)
    inv_std = 1.0 / jnp.sqrt(variance + 1e-05)
    normed_ref[...] = centred * inv_std
    inv_ref[...] = jnp.broadcast_to(inv_std, inv_ref.shape)
    context_t_ref[...] = context.T


def early_rows(residual, context, out_proj, block=128):
    rows, width = residual.shape
    return pl.pallas_call(
        early_kernel,
        name="early_rows",
        grid=(rows // block,),
        in_specs=[
            pl.BlockSpec((block, width), lambda r: (r, 0)),
            pl.BlockSpec((block, width), lambda r: (r, 0)),
            whole(out_proj.shape),
        ],
        out_specs=[
            pl.BlockSpec((block, width), lambda r: (r, 0)),
            pl.BlockSpec((block, 128), lambda r: (r, 0)),
            pl.BlockSpec((width, block), lambda r: (0, r)),
        ],
        out_shape=[
            pltpu.HBM((rows, width), F32),
            pltpu.HBM((rows, 128), F32),
            pltpu.HBM((width, rows), BF16),
        ],
        compiler_params=pltpu.CompilerParams(vmem_limit_bytes=10 * MIB),
        cost_estimate=pl.CostEstimate(
            flops=2 * rows * width * width, transcendentals=0, bytes_accessed=10 * rows * width
        ),
    )(residual, context, out_proj)


def late_kernel(
    core_ref,
    parts_ref,
    normed_far,
    inv_far,
    gain_ref,
    colbert_ref,
    context_far,
    resid_ref,
    kept_ref,
    given_ref,
    loss_ref,
    normed_ref,
    inv_ref,
    context_t_ref,
    sums_ref,
    sems,
):
    loads = [
        pltpu.make_async_copy(far, near, sems.at[k])
        for k, (far, near) in enumerate(
            ((normed_far, normed_ref), (inv_far, inv_ref), (context_far, context_t_ref))
        )
    ]
    for load in loads:
        load.start()
    slots = parts_ref.shape[1] - EXTRA
    width = normed_ref.shape[1]
    total = parts_ref[0].astype(F32)
    for k in range(1, parts_ref.shape[0]):
        total = total + parts_ref[k].astype(F32)
    loss_ref[...] = jnp.broadcast_to(
        jnp.sum(total[slots:], axis=0, keepdims=True), loss_ref.shape
    )
    grad = total[:slots].astype(BF16)
    gain = gain_ref[...]
    gained = dot(grad, colbert_ref[...], ((1,), (1,))) * gain
    grad_t = grad.T
    for load in loads[:2]:
        load.wait()
    normed = normed_ref[...]
    inv_std = inv_ref[:, :1]
    resid = inv_std * (
        gained
        - jnp.mean(gained, axis=1, keepdims=True)
        - normed * jnp.mean(gained * normed, axis=1, keepdims=True)
    )
    resid = resid.astype(BF16)
    resid_ref[...] = resid
    scaled = (normed * gain).astype(BF16)
    blocks, lines = sums_ref.shape[1], sums_ref.shape[3]
    thin = grad.shape[1] // (2 * blocks)
    thick = lines - thin
    colbert = dot(grad_t, scaled, ((1,), (0,)))
    for k in range(2 * blocks):
        for j in range(width // 128):
            sums_ref[k // blocks, k % blocks, j, thick:, :] = colbert[
                k * thin : (k + 1) * thin, j * 128 : (j + 1) * 128
            ].astype(BF16)
    loads[2].wait()
    group = 4
    for first in range(0, 2 * blocks, group):
        part = dot(
            context_t_ref[first * thick : (first + group) * thick, :], resid, ((1,), (0,))
        ).astype(BF16)
        for k in range(first, first + group):
            at = (k - first) * thick
            for j in range(width // 128):
                sums_ref[k // blocks, k % blocks, j, :thick, :] = part[
                    at : at + thick, j * 128 : (j + 1) * 128
                ]
    kept_ref[...] = sums_ref[core_ref[0]]
    given_ref[...] = sums_ref[1 - core_ref[0]]


def far(array):
    return pltpu.with_memory_space_constraint(array, pltpu.HBM)


def late_rows(core, blocks, pieces, normed, inv_std, gain, colbert_proj, context_t):
    rows, width = normed.shape
    emb = colbert_proj.shape[1]
    shape = (blocks, width // 128, (width + emb) // (2 * blocks), 128)
    return pl.pallas_call(
        late_kernel,
        name="late_rows",
        in_specs=[
            pl.BlockSpec(memory_space=pltpu.SMEM),
            whole(pieces.shape),
            pl.BlockSpec(memory_space=pltpu.HBM),
            pl.BlockSpec(memory_space=pltpu.HBM),
            whole(gain.shape),
            whole(colbert_proj.shape),
            pl.BlockSpec(memory_space=pltpu.HBM),
        ],
        scratch_shapes=[
            pltpu.VMEM(normed.shape, F32),
            pltpu.VMEM(inv_std.shape, F32),
            pltpu.VMEM(context_t.shape, BF16),
            pltpu.VMEM((2, *shape), BF16),
            pltpu.SemaphoreType.DMA((3,)),
        ],
        out_shape=[
            jax.ShapeDtypeStruct((rows, width), BF16),
            jax.ShapeDtypeStruct(shape, BF16),
            jax.ShapeDtypeStruct(shape, BF16),
            jax.ShapeDtypeStruct((8, emb), F32),
        ],
        compiler_params=pltpu.CompilerParams(vmem_limit_bytes=24 * MIB),
        cost_estimate=pl.CostEstimate(
            flops=2 * rows * width * (width + 2 * emb),
            transcendentals=0,
            bytes_accessed=14 * rows * width,
        ),
    )(core, pieces, far(normed), far(inv_std), gain, colbert_proj, far(context_t))


def exchange(pieces, axis):
    return lax.all_to_all(pieces, axis, 0, 0, tiled=True)


def own_kernel(core_ref, half_ref, proj_ref):
    blocks, columns, _, block = half_ref.shape
    thick = proj_ref.shape[0] // blocks
    for k in range(blocks):
        for j in range(columns):
            proj_ref[k * thick : (k + 1) * thick, j * block : (j + 1) * block] = half_ref[
                k, j, :thick, :
            ].astype(F32)


def own_rows(core, half, width, group=4):
    blocks, columns, lines, block = half.shape
    return pl.pallas_call(
        own_kernel,
        name="own_rows",
        grid_spec=pltpu.PrefetchScalarGridSpec(
            num_scalar_prefetch=1,
            grid=(columns // group,),
            in_specs=[pl.BlockSpec((blocks, group, lines, block), lambda k, core: (0, k, 0, 0))],
            out_specs=pl.BlockSpec((width // 2, group * block), lambda k, core: (core[0], k)),
        ),
        out_shape=pltpu.HBM((width, width), F32),
        compiler_params=pltpu.CompilerParams(vmem_limit_bytes=12 * MIB),
        cost_estimate=pl.CostEstimate(
            flops=width * width, transcendentals=0, bytes_accessed=4 * width * width
        ),
    )(core, half)


def finish_kernel(
    core_ref, half_ref, other_ref, colbert_ref, gain_ref, _, proj_ref, grad_ref, gain_grad_ref
):
    blocks, columns, _, block = half_ref.shape
    thick = proj_ref.shape[0] // blocks
    even = core_ref[0] == 0
    for j in range(columns):
        at = slice(j * block, (j + 1) * block)
        own, others = [], []
        for k in range(blocks):
            piece = other_ref[k, j].astype(F32)
            proj_ref[k * thick : (k + 1) * thick, at] = piece[:thick]
            others.append(piece[thick:])
            own.append(half_ref[k, j].astype(F32)[thick:])
        own, others = jnp.concatenate(own, axis=0), jnp.concatenate(others, axis=0)
        colbert_grad = jnp.concatenate(
            [jnp.where(even, own, others), jnp.where(even, others, own)], axis=0
        )
        colbert_t = colbert_ref[at, :].astype(F32).T
        gain_grad_ref[:, at] = (
            jnp.sum(colbert_grad * colbert_t, axis=0, keepdims=True) / gain_ref[:, at]
        )
        grad_ref[at, :] = colbert_grad.T


def finish(core, half, other, colbert_proj, gain, proj, group=4):
    blocks, columns, lines, block = half.shape
    width, emb = colbert_proj.shape
    piece = pl.BlockSpec((blocks, group, lines, block), lambda k, core: (0, k, 0, 0))
    span = group * block
    return pl.pallas_call(
        finish_kernel,
        name="finish",
        grid_spec=pltpu.PrefetchScalarGridSpec(
            num_scalar_prefetch=1,
            grid=(columns // group,),
            in_specs=[
                piece,
                piece,
                pl.BlockSpec((span, emb), lambda k, core: (k, 0)),
                pl.BlockSpec((1, span), lambda k, core: (0, k)),
                pl.BlockSpec(memory_space=pl.ANY),
            ],
            out_specs=[
                pl.BlockSpec((width // 2, span), lambda k, core: (1 - core[0], k)),
                pl.BlockSpec((span, emb), lambda k, core: (k, 0)),
                pl.BlockSpec((1, span), lambda k, core: (0, k)),
            ],
        ),
        out_shape=[
            jax.ShapeDtypeStruct((width, width), F32),
            jax.ShapeDtypeStruct((width, emb), F32),
            jax.ShapeDtypeStruct((1, width), F32),
        ],
        input_output_aliases={5: 0},
        compiler_params=pltpu.CompilerParams(vmem_limit_bytes=12 * MIB),
        cost_estimate=pl.CostEstimate(
            flops=2 * width * width, transcendentals=0, bytes_accessed=4 * width * width
        ),
    )(core, half, other, colbert_proj, gain, proj)


SWAP = [(0, 1), (1, 0)]
FAR = [(k, k ^ 2) for k in range(4)]
NEAR = [(k, k ^ 1) for k in range(4)]


def pair_summed(kept, given, axis, pairs, out_type):
    taken = lax.ppermute(given, axis, pairs)
    return (kept.astype(F32) + taken.astype(F32)).astype(out_type)


def halves_summed(halves, axis, pairs, side, out_type):
    keep, give = side
    given = lax.dynamic_index_in_dim(halves, give, 0, False)
    kept = lax.dynamic_index_in_dim(halves, keep, 0, False)
    return pair_summed(kept, given, axis, pairs, out_type)


def query_gathered(own):
    held = own[None]
    for axis, pairs in ((CORE, SWAP), ("neg_0", NEAR), ("neg_0", FAR)):
        held = jnp.concatenate([held, lax.ppermute(held, axis, pairs)])
    return held, lax.ppermute(held, "neg_1", SWAP)


def sent_out(tile_ref, out_ref, sems):
    copies = [
        pltpu.make_async_copy(tile_ref, out_ref.at[k], sems.at[k]) for k in range(out_ref.shape[0])
    ]
    for copy in copies:
        copy.start()
    for copy in copies:
        copy.wait()


def pack_kernel(length_ref, p_ref, out_ref, tile_ref, sems):
    slots = p_ref.shape[1]
    tile_ref[:slots, :] = p_ref[0]
    tile_ref[slots:, :] = jnp.full(
        (EXTRA, p_ref.shape[2]), (length_ref[0] - LEAST).astype(F32)
    ).astype(BF16)
    sent_out(tile_ref, out_ref, sems)


def passage_copies(passage_emb, lengths, copies):
    _, slots, width = passage_emb.shape
    tile = (slots + EXTRA, width)
    return pl.pallas_call(
        pack_kernel,
        name="passage_copies",
        in_specs=[
            pl.BlockSpec(memory_space=pltpu.SMEM),
            pl.BlockSpec(memory_space=pltpu.VMEM),
        ],
        out_specs=pl.BlockSpec(memory_space=pltpu.HBM),
        out_shape=pltpu.HBM((copies, *tile), BF16),
        scratch_shapes=[pltpu.VMEM(tile, BF16), pltpu.SemaphoreType.DMA((copies,))],
    )(lengths, passage_emb)


def spread_kernel(parts_ref, out_ref, tile_ref, sems):
    total = parts_ref[0].astype(F32)
    for k in range(1, parts_ref.shape[0]):
        total += parts_ref[k].astype(F32)
    tile_ref[...] = total.astype(BF16)
    sent_out(tile_ref, out_ref, sems)


def summed_copies(parts):
    return pl.pallas_call(
        spread_kernel,
        name="summed_copies",
        in_specs=[pl.BlockSpec(memory_space=pltpu.VMEM)],
        out_specs=pl.BlockSpec(memory_space=pltpu.HBM),
        out_shape=pltpu.HBM(parts.shape, BF16),
        scratch_shapes=[
            pltpu.VMEM(parts.shape[1:], BF16),
            pltpu.SemaphoreType.DMA((parts.shape[0],)),
        ],
    )(parts)


def body(
    query_emb, positive, passage_emb, lengths, residual, context, out_proj, norm_gain, colbert_proj
):
    query_dev, query_len, emb = query_emb.shape
    neg_size, dp_size, cross_size = lax.axis_size(NEG), lax.axis_size(DP), lax.axis_size(CROSS)
    place, core = lax.axis_index(NEG), lax.axis_index(CORE)
    spot = jnp.arange(emb)[None] - place * query_dev
    wanted = jnp.sum(
        jnp.where(spot == jnp.arange(query_dev)[:, None], positive[:, None], 0), axis=0
    )
    query_own = jnp.concatenate(
        [
            query_emb.reshape(query_dev * query_len, emb),
            jnp.broadcast_to(wanted.astype(BF16)[None], (EXTRA, emb)),
        ]
    )
    copies, query_own = lax.optimization_barrier(
        (passage_copies(passage_emb, lengths, dp_size), query_own)
    )
    passage_pack = exchange(copies, DP)
    queries = query_gathered(query_own)
    ids = jnp.broadcast_to((jnp.arange(dp_size) * neg_size + place).astype(F32)[:, None], (dp_size, emb))
    row, column = lax.axis_index("neg_1"), lax.axis_index("neg_0")
    flip = (row * 8 + column * 2 + core)[None]
    sides = [
        (own.astype(jnp.uint32), (1 - own).astype(jnp.uint32))
        for own in (row, column // 2, column % 2)
    ]
    queries, sides = lax.optimization_barrier((queries, sides))
    row_side, far_side, near_side = sides
    spread, mixed, query_rows, inverse, similar, stats = forward_tile(
        flip, *queries, passage_pack, ids, query_len
    )
    stats = exchange(stats, NEG)
    passage_parts, kept, given = backward_tile(
        core[None], neg_size, query_rows, spread, mixed, inverse, similar, stats, query_len
    )
    residual, kept, given = lax.optimization_barrier((residual, kept, given))
    early = early_rows(residual, context, out_proj)
    query_part = pair_summed(kept, given, CORE, SWAP, BF16)
    query_part = halves_summed(query_part, "neg_1", SWAP, row_side, F32)
    passage_parts = exchange(passage_parts, DP)
    passage_parts, query_part, early = lax.optimization_barrier((passage_parts, query_part, early))
    normed, inv_std, context_t = early
    residual_grad, kept, given, loss_sum = late_rows(
        core[None], dp_size, passage_parts, normed, inv_std, norm_gain[None], colbert_proj, context_t
    )
    half = pair_summed(kept, given, CORE, SWAP, BF16)
    context_grad = jnp.dot(residual_grad, out_proj.T, preferred_element_type=F32).astype(BF16)
    query_part = query_part.reshape(2, 2, *query_part.shape[1:])
    query_part = halves_summed(query_part, "neg_0", FAR, far_side, F32)
    half, context_grad, query_part = lax.optimization_barrier((half, context_grad, query_part))
    slabs = exchange(half.reshape(dp_size * cross_size, *half.shape[2:]), DP + CROSS)
    half = exchange(summed_copies(slabs), DP + CROSS).reshape(half.shape)
    half, query_part = lax.optimization_barrier((half, query_part))
    query_grad = halves_summed(query_part, "neg_0", NEAR, near_side, F32)
    query_grad = query_grad.reshape(query_dev, query_len, emb)
    other = lax.ppermute(half, CORE, SWAP)
    proj = own_rows(core[None], half, out_proj.shape[0])
    out_proj_grad, colbert_grad, gain_grad = finish(
        core[None], half, other, colbert_proj, norm_gain[None], proj
    )
    loss = loss_sum[0, 0] / (query_dev * dp_size * neg_size)
    return (
        loss,
        query_grad,
        residual_grad,
        context_grad,
        out_proj_grad,
        colbert_grad,
        gain_grad[0],
    )


def solution(mesh):
    split = Mesh(mesh.devices.reshape(mesh.shape["dp"] // 2, 2, 4, 2, 2), DP_NEG)
    placed = (
        P(DP_NEG, None, None),
        P(DP_NEG),
        P(DP_NEG, None, None),
        P(DP_NEG),
        P(DP_NEG, None),
        P(DP_NEG, None),
        P(),
        P(),
        P(),
    )
    return jax.shard_map(
        body,
        mesh=split,
        in_specs=placed,
        out_specs=(P(), P(DP_NEG, None, None), P(DP_NEG, None), P(DP_NEG, None), P(), P(), P()),
        check_vma=False,
    )
```

```python
import functools

import jax
import jax.numpy as jnp
from jax import lax
from jax.experimental import pallas as pl
from jax.experimental.pallas import tpu as pltpu
from jax.sharding import Mesh
from jax.sharding import PartitionSpec as P

DP = ("dp_0", "dp_1")
NEG = ("neg_0", "neg_1", "neg_2")
CROSS = ("neg_0", "neg_1")
CORE = "neg_2"
DP_NEG = DP + NEG
BF16 = jnp.bfloat16
F32 = jnp.float32
EXTRA = 8
LEAST = 256
MIB = 1 << 20


def dot(a, b, dims, precision=None):
    return lax.dot_general(a, b, (dims, ((), ())), precision=precision, preferred_element_type=F32)


def token_query(rows, queries, query_len, transposed=False):
    shape = (queries, rows) if transposed else (rows, queries)
    row = lax.broadcasted_iota(jnp.int32, shape, 1 if transposed else 0)
    query = lax.broadcasted_iota(jnp.int32, shape, 0 if transposed else 1)
    first = query * query_len
    return ((row >= first) & (row < first + query_len)).astype(F32)


def whole(shape):
    return pl.BlockSpec(shape, lambda *_: (0,) * len(shape))


def stored(k):
    core, row, near, far = k % 2, k // 2 % 2, k // 4 % 2, k // 8
    return row * 8 + far * 4 + near * 2 + core


def forward_kernel(
    query_len,
    group,
    flip_ref,
    near_ref,
    far_ref,
    p_ref,
    ids_ref,
    exp_ref,
    mix_ref,
    own_ref,
    inv_ref,
    sim_ref,
    stats_ref,
    rows_ref,
    length_ref,
):
    passage = pl.program_id(0)
    half, q_rows, width = near_ref.shape[0], near_ref.shape[1] - EXTRA, near_ref.shape[2]
    parts = 2 * half
    slots = p_ref.shape[1] - EXTRA
    count, rows = inv_ref.shape
    queries = rows // query_len
    chunk = group * q_rows
    steps = parts // group
    tokens = p_ref[0, :slots, :]
    length = p_ref[0, slots : slots + 1, :].astype(F32) + float(LEAST)
    length_ref[pl.ds(passage, 1), :] = length
    wide = jnp.concatenate([length] * ((slots - LEAST) // width), axis=1)
    position = lax.broadcasted_iota(jnp.int32, wide.shape, 1).astype(F32) + float(LEAST)
    bias = jnp.where(position < wide, 0.0, -1e30)
    lane = lax.broadcasted_iota(jnp.int32, (chunk, width), 1)

    @pl.when(passage == 0)
    def _():
        rows_ref[...] = jnp.zeros_like(rows_ref)
        for k in range(parts):
            at = stored(k) ^ flip_ref[0]
            spot = at % half
            own_ref[k * q_rows : (k + 1) * q_rows, :] = jnp.where(
                at < half, near_ref[spot, :q_rows, :], far_ref[spot, :q_rows, :]
            )

    def scores(step):
        block = own_ref[step * chunk : (step + 1) * chunk, :]
        return dot(block, tokens, ((1,), (1,)))

    ahead = scores(0)
    late = None
    for step in range(steps):
        now = ahead
        if step + 1 < steps:
            ahead = scores(step + 1)
        if late is not None:
            mix_ref[passage, pl.ds((step - 1) * chunk, chunk), :] = dot(late, tokens, ((1,), (0,)))
        sure, rest = now[:, :LEAST], now[:, LEAST:] + bias
        highest = jnp.maximum(
            jnp.max(sure, axis=1, keepdims=True), jnp.max(rest, axis=1, keepdims=True)
        )
        sure = jnp.exp(sure - highest)
        rest = jnp.exp(rest - highest)
        total = jnp.sum(sure, axis=1, keepdims=True) + jnp.sum(rest, axis=1, keepdims=True)
        late = jnp.concatenate([sure.astype(BF16), rest.astype(BF16)], axis=1)
        at = pl.ds(step * chunk, chunk)
        exp_ref[passage, at, :] = late
        rows_ref[at, :] = jnp.where(
            lane == passage,
            highest + jnp.log(total),
            jnp.where(lane == passage + width // 2, total, rows_ref[at, :]),
        )
    mix_ref[passage, pl.ds((steps - 1) * chunk, chunk), :] = dot(late, tokens, ((1,), (0,)))

    @pl.when(passage == pl.num_programs(0) - 1)
    def _():
        turned = rows_ref[...].T
        inv_ref[...] = 1.0 / turned[width // 2 : width // 2 + count]
        similar = dot(
            turned[:count], token_query(rows, queries, query_len), ((1,), (0,)), lax.Precision.HIGHEST
        )
        similar = similar - float(query_len) * jnp.log(length_ref[...])[:, :queries]
        wanted = jnp.sum(
            near_ref[:, q_rows, :].astype(F32) + far_ref[:, q_rows, :].astype(F32),
            axis=0,
            keepdims=True,
        )[:, :queries]
        hit = (wanted == ids_ref[:, :queries]).astype(F32)
        highest = jnp.max(similar, axis=0, keepdims=True)
        total = jnp.sum(jnp.exp(similar - highest), axis=0, keepdims=True)
        positive = jnp.sum(jnp.where(hit > 0.0, similar, 0.0), axis=0, keepdims=True)
        sim_ref[0] = similar
        sim_ref[1] = hit
        stats = jnp.concatenate([highest, total, positive, jnp.zeros((5, queries), F32)], axis=0)
        stats = jnp.concatenate([stats, jnp.zeros((8, width - queries), F32)], axis=1)
        stats_ref[...] = jnp.broadcast_to(stats[None], stats_ref.shape)


def forward_tile(flip, near, far, passage_pack, ids, query_len, group=8):
    half, q_rows, width = near.shape
    parts, q_rows = 2 * half, q_rows - EXTRA
    count, slots = passage_pack.shape[0], passage_pack.shape[1] - EXTRA
    rows = parts * q_rows
    queries = rows // query_len
    work = rows * slots * count
    return pl.pallas_call(
        functools.partial(forward_kernel, query_len, group),
        name="forward_tile",
        grid=(count,),
        in_specs=[
            pl.BlockSpec(memory_space=pltpu.SMEM),
            whole(near.shape),
            whole(far.shape),
            pl.BlockSpec((1, slots + EXTRA, width), lambda p: (p, 0, 0)),
            whole(ids.shape),
        ],
        out_specs=[
            pl.BlockSpec(memory_space=pltpu.VMEM),
            pl.BlockSpec(memory_space=pltpu.VMEM),
            pl.BlockSpec(memory_space=pltpu.VMEM),
            whole((count, rows)),
            whole((2, count, queries)),
            whole((parts, 8, width)),
        ],
        out_shape=[
            pltpu.VMEM((count, rows, slots), BF16),
            pltpu.VMEM((count, rows, width), F32),
            pltpu.VMEM((rows, width), BF16),
            jax.ShapeDtypeStruct((count, rows), F32),
            jax.ShapeDtypeStruct((2, count, queries), F32),
            jax.ShapeDtypeStruct((parts, 8, width), F32),
        ],
        scratch_shapes=[pltpu.VMEM((rows, width), F32), pltpu.VMEM((count, width), F32)],
        compiler_params=pltpu.CompilerParams(vmem_limit_bytes=16 * MIB),
        cost_estimate=pl.CostEstimate(
            flops=4 * work * width, transcendentals=work, bytes_accessed=4 * work
        ),
    )(flip, near, far, passage_pack, ids)


def split_lines(value):
    high = value.astype(BF16).astype(F32)
    low = (value - high).astype(BF16).astype(F32)
    last = value - high - low
    row = lax.broadcasted_iota(jnp.int32, value.shape, 0)
    lines = jnp.where(row == 0, high, jnp.where(row == 1, low, jnp.where(row == 2, last, 0.0)))
    return lines.astype(BF16)


def backward_kernel(
    query_len,
    parts,
    core_ref,
    own_ref,
    exp_ref,
    mix_ref,
    inv_ref,
    sim_ref,
    stats_ref,
    pg_ref,
    kept_ref,
    given_ref,
    qt,
    halves,
):
    count, rows, slots = exp_ref.shape
    width, q_rows = own_ref.shape[1], rows // parts
    queries = rows // query_len
    for k in range(parts):
        qt[:, k * q_rows : (k + 1) * q_rows] = own_ref[k * q_rows : (k + 1) * q_rows, :].T
    highest_of = stats_ref[:, 0, :queries]
    highest = jnp.max(highest_of, axis=0, keepdims=True)
    total = jnp.sum(
        stats_ref[:, 1, :queries] * jnp.exp(highest_of - highest), axis=0, keepdims=True
    )
    positive = jnp.sum(stats_ref[:, 2, :queries], axis=0, keepdims=True)
    log_total = highest + jnp.log(total)
    coefficient = jnp.exp(sim_ref[0] - log_total) - sim_ref[1]
    scale = inv_ref[...] * dot(
        coefficient,
        token_query(rows, queries, query_len, True),
        ((1,), (0,)),
        lax.Precision.HIGHEST,
    )
    lines = split_lines(
        jnp.broadcast_to(jnp.sum(log_total - positive, axis=1, keepdims=True), (EXTRA, width))
    )
    for p in range(count):
        weighted = (qt[...].astype(F32) * scale[p : p + 1]).astype(BF16)
        pg_ref[p, :slots, :] = dot(weighted, exp_ref[p], ((1,), (0,))).T.astype(BF16)
        pg_ref[p, slots:, :] = lines
    turned = jnp.concatenate([scale, jnp.zeros((width - count, rows), F32)], axis=0).T
    for k in range(parts):
        at = slice(k * q_rows, (k + 1) * q_rows)
        sums = mix_ref[0, at, :] * turned[at, :1]
        for p in range(1, count):
            sums += mix_ref[p, at, :] * turned[at, p : p + 1]
        halves[k % 2, k // 2 % 2, k // 4] = sums.astype(BF16)
    kept_ref[...] = halves[core_ref[0]]
    given_ref[...] = halves[1 - core_ref[0]]


def backward_tile(core, parts, own, spread, mixed, inverse, similar, stats, query_len):
    count, rows, slots = spread.shape
    q_rows, width = rows // parts, own.shape[1]
    work = rows * slots * count
    return pl.pallas_call(
        functools.partial(backward_kernel, query_len, parts),
        name="backward_tile",
        in_specs=[pl.BlockSpec(memory_space=pltpu.SMEM)]
        + [pl.BlockSpec(memory_space=pltpu.VMEM)] * 6,
        out_shape=[
            pltpu.HBM((count, slots + EXTRA, width), BF16),
            jax.ShapeDtypeStruct((2, parts // 4, q_rows, width), BF16),
            jax.ShapeDtypeStruct((2, parts // 4, q_rows, width), BF16),
        ],
        out_specs=[whole((count, slots + EXTRA, width))]
        + [whole((2, parts // 4, q_rows, width))] * 2,
        scratch_shapes=[
            pltpu.VMEM((width, rows), BF16),
            pltpu.VMEM((2, 2, parts // 4, q_rows, width), BF16),
        ],
        compiler_params=pltpu.CompilerParams(vmem_limit_bytes=16 * MIB),
        cost_estimate=pl.CostEstimate(
            flops=2 * work * width, transcendentals=0, bytes_accessed=3 * work
        ),
    )(core, own, spread, mixed, inverse, similar, stats)


def early_kernel(resid_ref, context_ref, proj_ref, normed_ref, inv_ref, context_t_ref):
    context = context_ref[...]
    hidden = resid_ref[...].astype(F32) + dot(context, proj_ref[...], ((1,), (0,)))
    centred = hidden - jnp.mean(hidden, axis=1, keepdims=True)
    variance = jnp.mean(centred * centred, axis=1, keepdims=True)
    inv_std = 1.0 / jnp.sqrt(variance + 1e-05)
    normed_ref[...] = centred * inv_std
    inv_ref[...] = jnp.broadcast_to(inv_std, inv_ref.shape)
    context_t_ref[...] = context.T


def early_rows(residual, context, out_proj, block=128):
    rows, width = residual.shape
    return pl.pallas_call(
        early_kernel,
        name="early_rows",
        grid=(rows // block,),
        in_specs=[
            pl.BlockSpec((block, width), lambda r: (r, 0)),
            pl.BlockSpec((block, width), lambda r: (r, 0)),
            whole(out_proj.shape),
        ],
        out_specs=[
            pl.BlockSpec((block, width), lambda r: (r, 0)),
            pl.BlockSpec((block, 128), lambda r: (r, 0)),
            pl.BlockSpec((width, block), lambda r: (0, r)),
        ],
        out_shape=[
            pltpu.HBM((rows, width), F32),
            pltpu.HBM((rows, 128), F32),
            pltpu.HBM((width, rows), BF16),
        ],
        compiler_params=pltpu.CompilerParams(vmem_limit_bytes=10 * MIB),
        cost_estimate=pl.CostEstimate(
            flops=2 * rows * width * width, transcendentals=0, bytes_accessed=10 * rows * width
        ),
    )(residual, context, out_proj)


def late_kernel(
    core_ref,
    parts_ref,
    normed_far,
    inv_far,
    gain_ref,
    colbert_ref,
    context_far,
    resid_ref,
    kept_ref,
    given_ref,
    loss_ref,
    normed_ref,
    inv_ref,
    context_t_ref,
    sums_ref,
    sems,
):
    loads = [
        pltpu.make_async_copy(far, near, sems.at[k])
        for k, (far, near) in enumerate(
            ((normed_far, normed_ref), (inv_far, inv_ref), (context_far, context_t_ref))
        )
    ]
    for load in loads:
        load.start()
    slots = parts_ref.shape[1] - EXTRA
    width = normed_ref.shape[1]
    total = parts_ref[0].astype(F32)
    for k in range(1, parts_ref.shape[0]):
        total = total + parts_ref[k].astype(F32)
    loss_ref[...] = jnp.broadcast_to(
        jnp.sum(total[slots:], axis=0, keepdims=True), loss_ref.shape
    )
    grad = total[:slots].astype(BF16)
    gain = gain_ref[...]
    gained = dot(grad, colbert_ref[...], ((1,), (1,))) * gain
    grad_t = grad.T
    for load in loads[:2]:
        load.wait()
    normed = normed_ref[...]
    inv_std = inv_ref[:, :1]
    resid = inv_std * (
        gained
        - jnp.mean(gained, axis=1, keepdims=True)
        - normed * jnp.mean(gained * normed, axis=1, keepdims=True)
    )
    resid = resid.astype(BF16)
    resid_ref[...] = resid
    scaled = (normed * gain).astype(BF16)
    blocks, lines = sums_ref.shape[1], sums_ref.shape[3]
    thin = grad.shape[1] // (2 * blocks)
    thick = lines - thin
    colbert = dot(grad_t, scaled, ((1,), (0,)))
    for k in range(2 * blocks):
        for j in range(width // 128):
            sums_ref[k // blocks, k % blocks, j, thick:, :] = colbert[
                k * thin : (k + 1) * thin, j * 128 : (j + 1) * 128
            ].astype(BF16)
    loads[2].wait()
    group = 4
    for first in range(0, 2 * blocks, group):
        part = dot(
            context_t_ref[first * thick : (first + group) * thick, :], resid, ((1,), (0,))
        ).astype(BF16)
        for k in range(first, first + group):
            at = (k - first) * thick
            for j in range(width // 128):
                sums_ref[k // blocks, k % blocks, j, :thick, :] = part[
                    at : at + thick, j * 128 : (j + 1) * 128
                ]
    kept_ref[...] = sums_ref[core_ref[0]]
    given_ref[...] = sums_ref[1 - core_ref[0]]


def far(array):
    return pltpu.with_memory_space_constraint(array, pltpu.HBM)


def late_rows(core, blocks, pieces, normed, inv_std, gain, colbert_proj, context_t):
    rows, width = normed.shape
    emb = colbert_proj.shape[1]
    shape = (blocks, width // 128, (width + emb) // (2 * blocks), 128)
    return pl.pallas_call(
        late_kernel,
        name="late_rows",
        in_specs=[
            pl.BlockSpec(memory_space=pltpu.SMEM),
            whole(pieces.shape),
            pl.BlockSpec(memory_space=pltpu.HBM),
            pl.BlockSpec(memory_space=pltpu.HBM),
            whole(gain.shape),
            whole(colbert_proj.shape),
            pl.BlockSpec(memory_space=pltpu.HBM),
        ],
        scratch_shapes=[
            pltpu.VMEM(normed.shape, F32),
            pltpu.VMEM(inv_std.shape, F32),
            pltpu.VMEM(context_t.shape, BF16),
            pltpu.VMEM((2, *shape), BF16),
            pltpu.SemaphoreType.DMA((3,)),
        ],
        out_shape=[
            jax.ShapeDtypeStruct((rows, width), BF16),
            jax.ShapeDtypeStruct(shape, BF16),
            jax.ShapeDtypeStruct(shape, BF16),
            jax.ShapeDtypeStruct((8, emb), F32),
        ],
        compiler_params=pltpu.CompilerParams(vmem_limit_bytes=24 * MIB),
        cost_estimate=pl.CostEstimate(
            flops=2 * rows * width * (width + 2 * emb),
            transcendentals=0,
            bytes_accessed=14 * rows * width,
        ),
    )(core, pieces, far(normed), far(inv_std), gain, colbert_proj, far(context_t))


def exchange(pieces, axis):
    return lax.all_to_all(pieces, axis, 0, 0, tiled=True)


def own_kernel(core_ref, half_ref, proj_ref):
    blocks, columns, _, block = half_ref.shape
    thick = proj_ref.shape[0] // blocks
    for k in range(blocks):
        for j in range(columns):
            proj_ref[k * thick : (k + 1) * thick, j * block : (j + 1) * block] = half_ref[
                k, j, :thick, :
            ].astype(F32)


def own_rows(core, half, width, group=4):
    blocks, columns, lines, block = half.shape
    return pl.pallas_call(
        own_kernel,
        name="own_rows",
        grid_spec=pltpu.PrefetchScalarGridSpec(
            num_scalar_prefetch=1,
            grid=(columns // group,),
            in_specs=[pl.BlockSpec((blocks, group, lines, block), lambda k, core: (0, k, 0, 0))],
            out_specs=pl.BlockSpec((width // 2, group * block), lambda k, core: (core[0], k)),
        ),
        out_shape=pltpu.HBM((width, width), F32),
        compiler_params=pltpu.CompilerParams(vmem_limit_bytes=12 * MIB),
        cost_estimate=pl.CostEstimate(
            flops=width * width, transcendentals=0, bytes_accessed=4 * width * width
        ),
    )(core, half)


def finish_kernel(
    core_ref, half_ref, other_ref, colbert_ref, gain_ref, _, proj_ref, grad_ref, gain_grad_ref
):
    blocks, columns, _, block = half_ref.shape
    thick = proj_ref.shape[0] // blocks
    even = core_ref[0] == 0
    for j in range(columns):
        at = slice(j * block, (j + 1) * block)
        own, others = [], []
        for k in range(blocks):
            piece = other_ref[k, j].astype(F32)
            proj_ref[k * thick : (k + 1) * thick, at] = piece[:thick]
            others.append(piece[thick:])
            own.append(half_ref[k, j].astype(F32)[thick:])
        own, others = jnp.concatenate(own, axis=0), jnp.concatenate(others, axis=0)
        colbert_grad = jnp.concatenate(
            [jnp.where(even, own, others), jnp.where(even, others, own)], axis=0
        )
        colbert_t = colbert_ref[at, :].astype(F32).T
        gain_grad_ref[:, at] = (
            jnp.sum(colbert_grad * colbert_t, axis=0, keepdims=True) / gain_ref[:, at]
        )
        grad_ref[at, :] = colbert_grad.T


def finish(core, half, other, colbert_proj, gain, proj, group=4):
    blocks, columns, lines, block = half.shape
    width, emb = colbert_proj.shape
    piece = pl.BlockSpec((blocks, group, lines, block), lambda k, core: (0, k, 0, 0))
    span = group * block
    return pl.pallas_call(
        finish_kernel,
        name="finish",
        grid_spec=pltpu.PrefetchScalarGridSpec(
            num_scalar_prefetch=1,
            grid=(columns // group,),
            in_specs=[
                piece,
                piece,
                pl.BlockSpec((span, emb), lambda k, core: (k, 0)),
                pl.BlockSpec((1, span), lambda k, core: (0, k)),
                pl.BlockSpec(memory_space=pl.ANY),
            ],
            out_specs=[
                pl.BlockSpec((width // 2, span), lambda k, core: (1 - core[0], k)),
                pl.BlockSpec((span, emb), lambda k, core: (k, 0)),
                pl.BlockSpec((1, span), lambda k, core: (0, k)),
            ],
        ),
        out_shape=[
            jax.ShapeDtypeStruct((width, width), F32),
            jax.ShapeDtypeStruct((width, emb), F32),
            jax.ShapeDtypeStruct((1, width), F32),
        ],
        input_output_aliases={5: 0},
        compiler_params=pltpu.CompilerParams(vmem_limit_bytes=12 * MIB),
        cost_estimate=pl.CostEstimate(
            flops=2 * width * width, transcendentals=0, bytes_accessed=4 * width * width
        ),
    )(core, half, other, colbert_proj, gain, proj)


SWAP = [(0, 1), (1, 0)]
FAR = [(k, k ^ 2) for k in range(4)]
NEAR = [(k, k ^ 1) for k in range(4)]


def pair_summed(kept, given, axis, pairs, out_type):
    taken = lax.ppermute(given, axis, pairs)
    return (kept.astype(F32) + taken.astype(F32)).astype(out_type)


def halves_summed(halves, axis, pairs, side, out_type):
    keep, give = side
    given = lax.dynamic_index_in_dim(halves, give, 0, False)
    kept = lax.dynamic_index_in_dim(halves, keep, 0, False)
    return pair_summed(kept, given, axis, pairs, out_type)


def query_gathered(own):
    held = own[None]
    for axis, pairs in ((CORE, SWAP), ("neg_0", NEAR), ("neg_0", FAR)):
        held = jnp.concatenate([held, lax.ppermute(held, axis, pairs)])
    return held, lax.ppermute(held, "neg_1", SWAP)


def sent_out(tile_ref, out_ref, sems):
    copies = [
        pltpu.make_async_copy(tile_ref, out_ref.at[k], sems.at[k]) for k in range(out_ref.shape[0])
    ]
    for copy in copies:
        copy.start()
    for copy in copies:
        copy.wait()


def pack_kernel(length_ref, p_ref, out_ref, tile_ref, sems):
    slots = p_ref.shape[1]
    tile_ref[:slots, :] = p_ref[0]
    tile_ref[slots:, :] = jnp.full(
        (EXTRA, p_ref.shape[2]), (length_ref[0] - LEAST).astype(F32)
    ).astype(BF16)
    sent_out(tile_ref, out_ref, sems)


def passage_copies(passage_emb, lengths, copies):
    _, slots, width = passage_emb.shape
    tile = (slots + EXTRA, width)
    return pl.pallas_call(
        pack_kernel,
        name="passage_copies",
        in_specs=[
            pl.BlockSpec(memory_space=pltpu.SMEM),
            pl.BlockSpec(memory_space=pltpu.VMEM),
        ],
        out_specs=pl.BlockSpec(memory_space=pltpu.HBM),
        out_shape=pltpu.HBM((copies, *tile), BF16),
        scratch_shapes=[pltpu.VMEM(tile, BF16), pltpu.SemaphoreType.DMA((copies,))],
    )(lengths, passage_emb)


def spread_kernel(parts_ref, out_ref):
    total = parts_ref[0].astype(F32)
    for k in range(1, parts_ref.shape[0]):
        total += parts_ref[k].astype(F32)
    out_ref[...] = jnp.broadcast_to(total.astype(BF16)[None], out_ref.shape)


def summed_copies(parts):
    return pl.pallas_call(
        spread_kernel,
        name="summed_copies",
        in_specs=[pl.BlockSpec(memory_space=pltpu.VMEM)],
        out_specs=pl.BlockSpec(memory_space=pltpu.VMEM),
        out_shape=pltpu.VMEM(parts.shape, BF16),
        compiler_params=pltpu.CompilerParams(vmem_limit_bytes=6 * MIB),
    )(parts)


def body(
    query_emb, positive, passage_emb, lengths, residual, context, out_proj, norm_gain, colbert_proj
):
    query_dev, query_len, emb = query_emb.shape
    neg_size, dp_size, cross_size = lax.axis_size(NEG), lax.axis_size(DP), lax.axis_size(CROSS)
    place, core = lax.axis_index(NEG), lax.axis_index(CORE)
    spot = jnp.arange(emb)[None] - place * query_dev
    wanted = jnp.sum(
        jnp.where(spot == jnp.arange(query_dev)[:, None], positive[:, None], 0), axis=0
    )
    query_own = jnp.concatenate(
        [
            query_emb.reshape(query_dev * query_len, emb),
            jnp.broadcast_to(wanted.astype(BF16)[None], (EXTRA, emb)),
        ]
    )
    copies, query_own = lax.optimization_barrier(
        (passage_copies(passage_emb, lengths, dp_size), query_own)
    )
    passage_pack = exchange(copies, DP)
    queries = query_gathered(query_own)
    ids = jnp.broadcast_to((jnp.arange(dp_size) * neg_size + place).astype(F32)[:, None], (dp_size, emb))
    row, column = lax.axis_index("neg_1"), lax.axis_index("neg_0")
    flip = (row * 8 + column * 2 + core)[None]
    sides = [
        (own.astype(jnp.uint32), (1 - own).astype(jnp.uint32))
        for own in (row, column // 2, column % 2)
    ]
    queries, sides = lax.optimization_barrier((queries, sides))
    row_side, far_side, near_side = sides
    spread, mixed, query_rows, inverse, similar, stats = forward_tile(
        flip, *queries, passage_pack, ids, query_len
    )
    stats = exchange(stats, NEG)
    passage_parts, kept, given = backward_tile(
        core[None], neg_size, query_rows, spread, mixed, inverse, similar, stats, query_len
    )
    residual, kept, given = lax.optimization_barrier((residual, kept, given))
    early = early_rows(residual, context, out_proj)
    query_part = pair_summed(kept, given, CORE, SWAP, BF16)
    query_part = halves_summed(query_part, "neg_1", SWAP, row_side, F32)
    passage_parts = exchange(passage_parts, DP)
    passage_parts, query_part, early = lax.optimization_barrier((passage_parts, query_part, early))
    normed, inv_std, context_t = early
    residual_grad, kept, given, loss_sum = late_rows(
        core[None], dp_size, passage_parts, normed, inv_std, norm_gain[None], colbert_proj, context_t
    )
    half = pair_summed(kept, given, CORE, SWAP, BF16)
    context_grad = jnp.dot(residual_grad, out_proj.T, preferred_element_type=F32).astype(BF16)
    query_part = query_part.reshape(2, 2, *query_part.shape[1:])
    query_part = halves_summed(query_part, "neg_0", FAR, far_side, F32)
    half, context_grad, query_part = lax.optimization_barrier((half, context_grad, query_part))
    slabs = exchange(half.reshape(dp_size * cross_size, *half.shape[2:]), DP + CROSS)
    half = exchange(summed_copies(slabs), DP + CROSS).reshape(half.shape)
    half, query_part = lax.optimization_barrier((half, query_part))
    query_grad = halves_summed(query_part, "neg_0", NEAR, near_side, F32)
    query_grad = query_grad.reshape(query_dev, query_len, emb)
    other = lax.ppermute(half, CORE, SWAP)
    proj = own_rows(core[None], half, out_proj.shape[0])
    out_proj_grad, colbert_grad, gain_grad = finish(
        core[None], half, other, colbert_proj, norm_gain[None], proj
    )
    loss = loss_sum[0, 0] / (query_dev * dp_size * neg_size)
    return (
        loss,
        query_grad,
        residual_grad,
        context_grad,
        out_proj_grad,
        colbert_grad,
        gain_grad[0],
    )


def solution(mesh):
    split = Mesh(mesh.devices.reshape(mesh.shape["dp"] // 2, 2, 4, 2, 2), DP_NEG)
    placed = (
        P(DP_NEG, None, None),
        P(DP_NEG),
        P(DP_NEG, None, None),
        P(DP_NEG),
        P(DP_NEG, None),
        P(DP_NEG, None),
        P(),
        P(),
        P(),
    )
    return jax.shard_map(
        body,
        mesh=split,
        in_specs=placed,
        out_specs=(P(), P(DP_NEG, None, None), P(DP_NEG, None), P(DP_NEG, None), P(), P(), P()),
        check_vma=False,
    )
```

```python
import functools

import jax
import jax.numpy as jnp
from jax import lax
from jax.experimental import pallas as pl
from jax.experimental.pallas import tpu as pltpu
from jax.sharding import Mesh
from jax.sharding import PartitionSpec as P

DP = ("dp_0", "dp_1")
NEG = ("neg_0", "neg_1", "neg_2")
CROSS = ("neg_0", "neg_1")
CORE = "neg_2"
DP_NEG = DP + NEG
BF16 = jnp.bfloat16
F32 = jnp.float32
EXTRA = 8
LEAST = 256
MIB = 1 << 20


def dot(a, b, dims, precision=None):
    return lax.dot_general(a, b, (dims, ((), ())), precision=precision, preferred_element_type=F32)


def token_query(rows, queries, query_len, transposed=False):
    shape = (queries, rows) if transposed else (rows, queries)
    row = lax.broadcasted_iota(jnp.int32, shape, 1 if transposed else 0)
    query = lax.broadcasted_iota(jnp.int32, shape, 0 if transposed else 1)
    first = query * query_len
    return ((row >= first) & (row < first + query_len)).astype(F32)


def whole(shape):
    return pl.BlockSpec(shape, lambda *_: (0,) * len(shape))


def stored(k):
    core, row, near, far = k % 2, k // 2 % 2, k // 4 % 2, k // 8
    return row * 8 + far * 4 + near * 2 + core


def forward_kernel(
    query_len,
    group,
    flip_ref,
    near_ref,
    far_ref,
    p_ref,
    ids_ref,
    exp_ref,
    mix_ref,
    own_ref,
    inv_ref,
    sim_ref,
    stats_ref,
    rows_ref,
    length_ref,
):
    passage = pl.program_id(0)
    half, q_rows, width = near_ref.shape[0], near_ref.shape[1] - EXTRA, near_ref.shape[2]
    parts = 2 * half
    slots = p_ref.shape[1] - EXTRA
    count, rows = inv_ref.shape
    queries = rows // query_len
    chunk = group * q_rows
    steps = parts // group
    tokens = p_ref[0, :slots, :]
    length = p_ref[0, slots : slots + 1, :].astype(F32) + float(LEAST)
    length_ref[pl.ds(passage, 1), :] = length
    wide = jnp.concatenate([length] * ((slots - LEAST) // width), axis=1)
    position = lax.broadcasted_iota(jnp.int32, wide.shape, 1).astype(F32) + float(LEAST)
    bias = jnp.where(position < wide, 0.0, -1e30)
    lane = lax.broadcasted_iota(jnp.int32, (chunk, width), 1)

    @pl.when(passage == 0)
    def _():
        rows_ref[...] = jnp.zeros_like(rows_ref)
        for k in range(parts):
            at = stored(k) ^ flip_ref[0]
            spot = at % half
            own_ref[k * q_rows : (k + 1) * q_rows, :] = jnp.where(
                at < half, near_ref[spot, :q_rows, :], far_ref[spot, :q_rows, :]
            )

    def scores(step):
        block = own_ref[step * chunk : (step + 1) * chunk, :]
        return dot(block, tokens, ((1,), (1,)))

    ahead = scores(0)
    late = None
    for step in range(steps):
        now = ahead
        if step + 1 < steps:
            ahead = scores(step + 1)
        if late is not None:
            mix_ref[passage, pl.ds((step - 1) * chunk, chunk), :] = dot(late, tokens, ((1,), (0,)))
        sure, rest = now[:, :LEAST], now[:, LEAST:] + bias
        highest = jnp.maximum(
            jnp.max(sure, axis=1, keepdims=True), jnp.max(rest, axis=1, keepdims=True)
        )
        sure = jnp.exp(sure - highest)
        rest = jnp.exp(rest - highest)
        total = jnp.sum(sure, axis=1, keepdims=True) + jnp.sum(rest, axis=1, keepdims=True)
        late = jnp.concatenate([sure.astype(BF16), rest.astype(BF16)], axis=1)
        at = pl.ds(step * chunk, chunk)
        exp_ref[passage, at, :] = late
        rows_ref[at, :] = jnp.where(
            lane == passage,
            highest + jnp.log(total),
            jnp.where(lane == passage + width // 2, total, rows_ref[at, :]),
        )
    mix_ref[passage, pl.ds((steps - 1) * chunk, chunk), :] = dot(late, tokens, ((1,), (0,)))

    @pl.when(passage == pl.num_programs(0) - 1)
    def _():
        turned = rows_ref[...].T
        inv_ref[...] = 1.0 / turned[width // 2 : width // 2 + count]
        similar = dot(
            turned[:count], token_query(rows, queries, query_len), ((1,), (0,)), lax.Precision.HIGHEST
        )
        similar = similar - float(query_len) * jnp.log(length_ref[...])[:, :queries]
        wanted = jnp.sum(
            near_ref[:, q_rows, :].astype(F32) + far_ref[:, q_rows, :].astype(F32),
            axis=0,
            keepdims=True,
        )[:, :queries]
        hit = (wanted == ids_ref[:, :queries]).astype(F32)
        highest = jnp.max(similar, axis=0, keepdims=True)
        total = jnp.sum(jnp.exp(similar - highest), axis=0, keepdims=True)
        positive = jnp.sum(jnp.where(hit > 0.0, similar, 0.0), axis=0, keepdims=True)
        sim_ref[0] = similar
        sim_ref[1] = hit
        stats = jnp.concatenate([highest, total, positive, jnp.zeros((5, queries), F32)], axis=0)
        stats = jnp.concatenate([stats, jnp.zeros((8, width - queries), F32)], axis=1)
        stats_ref[...] = jnp.broadcast_to(stats[None], stats_ref.shape)


def forward_tile(flip, near, far, passage_pack, ids, query_len, group=8):
    half, q_rows, width = near.shape
    parts, q_rows = 2 * half, q_rows - EXTRA
    count, slots = passage_pack.shape[0], passage_pack.shape[1] - EXTRA
    rows = parts * q_rows
    queries = rows // query_len
    work = rows * slots * count
    return pl.pallas_call(
        functools.partial(forward_kernel, query_len, group),
        name="forward_tile",
        grid=(count,),
        in_specs=[
            pl.BlockSpec(memory_space=pltpu.SMEM),
            whole(near.shape),
            whole(far.shape),
            pl.BlockSpec((1, slots + EXTRA, width), lambda p: (p, 0, 0)),
            whole(ids.shape),
        ],
        out_specs=[
            pl.BlockSpec(memory_space=pltpu.VMEM),
            pl.BlockSpec(memory_space=pltpu.VMEM),
            pl.BlockSpec(memory_space=pltpu.VMEM),
            whole((count, rows)),
            whole((2, count, queries)),
            whole((parts, 8, width)),
        ],
        out_shape=[
            pltpu.VMEM((count, rows, slots), BF16),
            pltpu.VMEM((count, rows, width), F32),
            pltpu.VMEM((rows, width), BF16),
            jax.ShapeDtypeStruct((count, rows), F32),
            jax.ShapeDtypeStruct((2, count, queries), F32),
            jax.ShapeDtypeStruct((parts, 8, width), F32),
        ],
        scratch_shapes=[pltpu.VMEM((rows, width), F32), pltpu.VMEM((count, width), F32)],
        compiler_params=pltpu.CompilerParams(vmem_limit_bytes=16 * MIB),
        cost_estimate=pl.CostEstimate(
            flops=4 * work * width, transcendentals=work, bytes_accessed=4 * work
        ),
    )(flip, near, far, passage_pack, ids)


def split_lines(value):
    high = value.astype(BF16).astype(F32)
    low = (value - high).astype(BF16).astype(F32)
    last = value - high - low
    row = lax.broadcasted_iota(jnp.int32, value.shape, 0)
    lines = jnp.where(row == 0, high, jnp.where(row == 1, low, jnp.where(row == 2, last, 0.0)))
    return lines.astype(BF16)


def backward_kernel(
    query_len,
    parts,
    core_ref,
    own_ref,
    exp_ref,
    mix_ref,
    inv_ref,
    sim_ref,
    stats_ref,
    pg_ref,
    kept_ref,
    given_ref,
    qt,
    halves,
):
    count, rows, slots = exp_ref.shape
    width, q_rows = own_ref.shape[1], rows // parts
    queries = rows // query_len
    for k in range(parts):
        qt[:, k * q_rows : (k + 1) * q_rows] = own_ref[k * q_rows : (k + 1) * q_rows, :].T
    highest_of = stats_ref[:, 0, :queries]
    highest = jnp.max(highest_of, axis=0, keepdims=True)
    total = jnp.sum(
        stats_ref[:, 1, :queries] * jnp.exp(highest_of - highest), axis=0, keepdims=True
    )
    positive = jnp.sum(stats_ref[:, 2, :queries], axis=0, keepdims=True)
    log_total = highest + jnp.log(total)
    coefficient = jnp.exp(sim_ref[0] - log_total) - sim_ref[1]
    scale = inv_ref[...] * dot(
        coefficient,
        token_query(rows, queries, query_len, True),
        ((1,), (0,)),
        lax.Precision.HIGHEST,
    )
    lines = split_lines(
        jnp.broadcast_to(jnp.sum(log_total - positive, axis=1, keepdims=True), (EXTRA, width))
    )
    for p in range(count):
        weighted = (qt[...].astype(F32) * scale[p : p + 1]).astype(BF16)
        pg_ref[p, :slots, :] = dot(weighted, exp_ref[p], ((1,), (0,))).T.astype(BF16)
        pg_ref[p, slots:, :] = lines
    turned = jnp.concatenate([scale, jnp.zeros((width - count, rows), F32)], axis=0).T
    for k in range(parts):
        at = slice(k * q_rows, (k + 1) * q_rows)
        sums = mix_ref[0, at, :] * turned[at, :1]
        for p in range(1, count):
            sums += mix_ref[p, at, :] * turned[at, p : p + 1]
        halves[k % 2, k // 2 % 2, k // 4] = sums.astype(BF16)
    kept_ref[...] = halves[core_ref[0]]
    given_ref[...] = halves[1 - core_ref[0]]


def backward_tile(core, parts, own, spread, mixed, inverse, similar, stats, query_len):
    count, rows, slots = spread.shape
    q_rows, width = rows // parts, own.shape[1]
    work = rows * slots * count
    return pl.pallas_call(
        functools.partial(backward_kernel, query_len, parts),
        name="backward_tile",
        in_specs=[pl.BlockSpec(memory_space=pltpu.SMEM)]
        + [pl.BlockSpec(memory_space=pltpu.VMEM)] * 6,
        out_shape=[
            pltpu.HBM((count, slots + EXTRA, width), BF16),
            jax.ShapeDtypeStruct((2, parts // 4, q_rows, width), BF16),
            jax.ShapeDtypeStruct((2, parts // 4, q_rows, width), BF16),
        ],
        out_specs=[whole((count, slots + EXTRA, width))]
        + [whole((2, parts // 4, q_rows, width))] * 2,
        scratch_shapes=[
            pltpu.VMEM((width, rows), BF16),
            pltpu.VMEM((2, 2, parts // 4, q_rows, width), BF16),
        ],
        compiler_params=pltpu.CompilerParams(vmem_limit_bytes=16 * MIB),
        cost_estimate=pl.CostEstimate(
            flops=2 * work * width, transcendentals=0, bytes_accessed=3 * work
        ),
    )(core, own, spread, mixed, inverse, similar, stats)


def early_kernel(resid_ref, context_ref, proj_ref, normed_ref, inv_ref, context_t_ref):
    context = context_ref[...]
    hidden = resid_ref[...].astype(F32) + dot(context, proj_ref[...], ((1,), (0,)))
    centred = hidden - jnp.mean(hidden, axis=1, keepdims=True)
    variance = jnp.mean(centred * centred, axis=1, keepdims=True)
    inv_std = 1.0 / jnp.sqrt(variance + 1e-05)
    normed_ref[...] = centred * inv_std
    inv_ref[...] = jnp.broadcast_to(inv_std, inv_ref.shape)
    context_t_ref[...] = context.T


def early_rows(residual, context, out_proj, block=128):
    rows, width = residual.shape
    return pl.pallas_call(
        early_kernel,
        name="early_rows",
        grid=(rows // block,),
        in_specs=[
            pl.BlockSpec((block, width), lambda r: (r, 0)),
            pl.BlockSpec((block, width), lambda r: (r, 0)),
            whole(out_proj.shape),
        ],
        out_specs=[
            pl.BlockSpec((block, width), lambda r: (r, 0)),
            pl.BlockSpec((block, 128), lambda r: (r, 0)),
            pl.BlockSpec((width, block), lambda r: (0, r)),
        ],
        out_shape=[
            pltpu.HBM((rows, width), F32),
            pltpu.HBM((rows, 128), F32),
            pltpu.HBM((width, rows), BF16),
        ],
        compiler_params=pltpu.CompilerParams(vmem_limit_bytes=10 * MIB),
        cost_estimate=pl.CostEstimate(
            flops=2 * rows * width * width, transcendentals=0, bytes_accessed=10 * rows * width
        ),
    )(residual, context, out_proj)


def late_kernel(
    core_ref,
    parts_ref,
    normed_far,
    inv_far,
    gain_ref,
    colbert_ref,
    context_far,
    resid_ref,
    kept_ref,
    given_ref,
    loss_ref,
    normed_ref,
    inv_ref,
    context_t_ref,
    sums_ref,
    sems,
):
    loads = [
        pltpu.make_async_copy(far, near, sems.at[k])
        for k, (far, near) in enumerate(
            ((normed_far, normed_ref), (inv_far, inv_ref), (context_far, context_t_ref))
        )
    ]
    for load in loads:
        load.start()
    slots = parts_ref.shape[1] - EXTRA
    width = normed_ref.shape[1]
    total = parts_ref[0].astype(F32)
    for k in range(1, parts_ref.shape[0]):
        total = total + parts_ref[k].astype(F32)
    loss_ref[...] = jnp.broadcast_to(
        jnp.sum(total[slots:], axis=0, keepdims=True), loss_ref.shape
    )
    grad = total[:slots].astype(BF16)
    gain = gain_ref[...]
    gained = dot(grad, colbert_ref[...], ((1,), (1,))) * gain
    grad_t = grad.T
    for load in loads[:2]:
        load.wait()
    normed = normed_ref[...]
    inv_std = inv_ref[:, :1]
    resid = inv_std * (
        gained
        - jnp.mean(gained, axis=1, keepdims=True)
        - normed * jnp.mean(gained * normed, axis=1, keepdims=True)
    )
    resid = resid.astype(BF16)
    resid_ref[...] = resid
    scaled = (normed * gain).astype(BF16)
    blocks, lines = sums_ref.shape[1], sums_ref.shape[3]
    thin = grad.shape[1] // (2 * blocks)
    thick = lines - thin
    colbert = dot(grad_t, scaled, ((1,), (0,)))
    for k in range(2 * blocks):
        for j in range(width // 128):
            sums_ref[k // blocks, k % blocks, j, thick:, :] = colbert[
                k * thin : (k + 1) * thin, j * 128 : (j + 1) * 128
            ].astype(BF16)
    loads[2].wait()
    group = 4
    for first in range(0, 2 * blocks, group):
        part = dot(
            context_t_ref[first * thick : (first + group) * thick, :], resid, ((1,), (0,))
        ).astype(BF16)
        for k in range(first, first + group):
            at = (k - first) * thick
            for j in range(width // 128):
                sums_ref[k // blocks, k % blocks, j, :thick, :] = part[
                    at : at + thick, j * 128 : (j + 1) * 128
                ]
    kept_ref[...] = sums_ref[core_ref[0]]
    given_ref[...] = sums_ref[1 - core_ref[0]]


def far(array):
    return pltpu.with_memory_space_constraint(array, pltpu.HBM)


def late_rows(core, blocks, pieces, normed, inv_std, gain, colbert_proj, context_t):
    rows, width = normed.shape
    emb = colbert_proj.shape[1]
    shape = (blocks, width // 128, (width + emb) // (2 * blocks), 128)
    return pl.pallas_call(
        late_kernel,
        name="late_rows",
        in_specs=[
            pl.BlockSpec(memory_space=pltpu.SMEM),
            whole(pieces.shape),
            pl.BlockSpec(memory_space=pltpu.HBM),
            pl.BlockSpec(memory_space=pltpu.HBM),
            whole(gain.shape),
            whole(colbert_proj.shape),
            pl.BlockSpec(memory_space=pltpu.HBM),
        ],
        scratch_shapes=[
            pltpu.VMEM(normed.shape, F32),
            pltpu.VMEM(inv_std.shape, F32),
            pltpu.VMEM(context_t.shape, BF16),
            pltpu.VMEM((2, *shape), BF16),
            pltpu.SemaphoreType.DMA((3,)),
        ],
        out_shape=[
            jax.ShapeDtypeStruct((rows, width), BF16),
            jax.ShapeDtypeStruct(shape, BF16),
            jax.ShapeDtypeStruct(shape, BF16),
            jax.ShapeDtypeStruct((8, emb), F32),
        ],
        compiler_params=pltpu.CompilerParams(vmem_limit_bytes=24 * MIB),
        cost_estimate=pl.CostEstimate(
            flops=2 * rows * width * (width + 2 * emb),
            transcendentals=0,
            bytes_accessed=14 * rows * width,
        ),
    )(core, pieces, far(normed), far(inv_std), gain, colbert_proj, far(context_t))


def exchange(pieces, axis):
    return lax.all_to_all(pieces, axis, 0, 0, tiled=True)


def own_kernel(core_ref, half_ref, proj_ref):
    blocks, columns, _, block = half_ref.shape
    thick = proj_ref.shape[0] // blocks
    for k in range(blocks):
        for j in range(columns):
            proj_ref[k * thick : (k + 1) * thick, j * block : (j + 1) * block] = half_ref[
                k, j, :thick, :
            ].astype(F32)


def own_rows(core, half, width, group=4):
    blocks, columns, lines, block = half.shape
    return pl.pallas_call(
        own_kernel,
        name="own_rows",
        grid_spec=pltpu.PrefetchScalarGridSpec(
            num_scalar_prefetch=1,
            grid=(columns // group,),
            in_specs=[pl.BlockSpec((blocks, group, lines, block), lambda k, core: (0, k, 0, 0))],
            out_specs=pl.BlockSpec((width // 2, group * block), lambda k, core: (core[0], k)),
        ),
        out_shape=pltpu.HBM((width, width), F32),
        compiler_params=pltpu.CompilerParams(vmem_limit_bytes=12 * MIB),
        cost_estimate=pl.CostEstimate(
            flops=width * width, transcendentals=0, bytes_accessed=4 * width * width
        ),
    )(core, half)


def finish_kernel(
    core_ref, half_ref, other_ref, colbert_ref, gain_ref, _, proj_ref, grad_ref, gain_grad_ref
):
    blocks, columns, _, block = half_ref.shape
    thick = proj_ref.shape[0] // blocks
    even = core_ref[0] == 0
    for j in range(columns):
        at = slice(j * block, (j + 1) * block)
        own, others = [], []
        for k in range(blocks):
            piece = other_ref[k, j].astype(F32)
            proj_ref[k * thick : (k + 1) * thick, at] = piece[:thick]
            others.append(piece[thick:])
            own.append(half_ref[k, j].astype(F32)[thick:])
        own, others = jnp.concatenate(own, axis=0), jnp.concatenate(others, axis=0)
        colbert_grad = jnp.concatenate(
            [jnp.where(even, own, others), jnp.where(even, others, own)], axis=0
        )
        colbert_t = colbert_ref[at, :].astype(F32).T
        gain_grad_ref[:, at] = (
            jnp.sum(colbert_grad * colbert_t, axis=0, keepdims=True) / gain_ref[:, at]
        )
        grad_ref[at, :] = colbert_grad.T


def finish(core, half, other, colbert_proj, gain, proj, group=4):
    blocks, columns, lines, block = half.shape
    width, emb = colbert_proj.shape
    piece = pl.BlockSpec((blocks, group, lines, block), lambda k, core: (0, k, 0, 0))
    span = group * block
    return pl.pallas_call(
        finish_kernel,
        name="finish",
        grid_spec=pltpu.PrefetchScalarGridSpec(
            num_scalar_prefetch=1,
            grid=(columns // group,),
            in_specs=[
                piece,
                piece,
                pl.BlockSpec((span, emb), lambda k, core: (k, 0)),
                pl.BlockSpec((1, span), lambda k, core: (0, k)),
                pl.BlockSpec(memory_space=pl.ANY),
            ],
            out_specs=[
                pl.BlockSpec((width // 2, span), lambda k, core: (1 - core[0], k)),
                pl.BlockSpec((span, emb), lambda k, core: (k, 0)),
                pl.BlockSpec((1, span), lambda k, core: (0, k)),
            ],
        ),
        out_shape=[
            jax.ShapeDtypeStruct((width, width), F32),
            jax.ShapeDtypeStruct((width, emb), F32),
            jax.ShapeDtypeStruct((1, width), F32),
        ],
        input_output_aliases={5: 0},
        compiler_params=pltpu.CompilerParams(vmem_limit_bytes=12 * MIB),
        cost_estimate=pl.CostEstimate(
            flops=2 * width * width, transcendentals=0, bytes_accessed=4 * width * width
        ),
    )(core, half, other, colbert_proj, gain, proj)


SWAP = [(0, 1), (1, 0)]
FAR = [(k, k ^ 2) for k in range(4)]
NEAR = [(k, k ^ 1) for k in range(4)]


def pair_summed(kept, given, axis, pairs, out_type):
    taken = lax.ppermute(given, axis, pairs)
    return (kept.astype(F32) + taken.astype(F32)).astype(out_type)


def halves_summed(halves, axis, pairs, side, out_type):
    keep, give = side
    given = lax.dynamic_index_in_dim(halves, give, 0, False)
    kept = lax.dynamic_index_in_dim(halves, keep, 0, False)
    return pair_summed(kept, given, axis, pairs, out_type)


def query_gathered(own):
    held = own[None]
    for axis, pairs in ((CORE, SWAP), ("neg_0", NEAR), ("neg_0", FAR)):
        held = jnp.concatenate([held, lax.ppermute(held, axis, pairs)])
    return held, lax.ppermute(held, "neg_1", SWAP)


def sent_out(tile_ref, out_ref, sems):
    copies = [
        pltpu.make_async_copy(tile_ref, out_ref.at[k], sems.at[k]) for k in range(out_ref.shape[0])
    ]
    for copy in copies:
        copy.start()
    for copy in copies:
        copy.wait()


def pack_kernel(length_ref, p_ref, out_ref, tile_ref, sems):
    slots = p_ref.shape[1]
    tile_ref[:slots, :] = p_ref[0]
    tile_ref[slots:, :] = jnp.full(
        (EXTRA, p_ref.shape[2]), (length_ref[0] - LEAST).astype(F32)
    ).astype(BF16)
    sent_out(tile_ref, out_ref, sems)


def passage_copies(passage_emb, lengths, copies):
    _, slots, width = passage_emb.shape
    tile = (slots + EXTRA, width)
    return pl.pallas_call(
        pack_kernel,
        name="passage_copies",
        in_specs=[
            pl.BlockSpec(memory_space=pltpu.SMEM),
            pl.BlockSpec(memory_space=pltpu.VMEM),
        ],
        out_specs=pl.BlockSpec(memory_space=pltpu.HBM),
        out_shape=pltpu.HBM((copies, *tile), BF16),
        scratch_shapes=[pltpu.VMEM(tile, BF16), pltpu.SemaphoreType.DMA((copies,))],
    )(lengths, passage_emb)


def spread_kernel(parts_ref, out_ref):
    total = parts_ref[0].astype(F32)
    for k in range(1, parts_ref.shape[0]):
        total += parts_ref[k].astype(F32)
    out_ref[...] = jnp.broadcast_to(total.astype(BF16)[None], out_ref.shape)


def summed_copies(parts):
    return pl.pallas_call(
        spread_kernel,
        name="summed_copies",
        in_specs=[pl.BlockSpec(memory_space=pltpu.VMEM)],
        out_specs=pl.BlockSpec(memory_space=pltpu.VMEM),
        out_shape=pltpu.VMEM(parts.shape, BF16),
        compiler_params=pltpu.CompilerParams(vmem_limit_bytes=6 * MIB),
    )(parts)


def body(
    query_emb, positive, passage_emb, lengths, residual, context, out_proj, norm_gain, colbert_proj
):
    query_dev, query_len, emb = query_emb.shape
    neg_size, dp_size, cross_size = lax.axis_size(NEG), lax.axis_size(DP), lax.axis_size(CROSS)
    place, core = lax.axis_index(NEG), lax.axis_index(CORE)
    spot = jnp.arange(emb)[None] - place * query_dev
    wanted = jnp.sum(
        jnp.where(spot == jnp.arange(query_dev)[:, None], positive[:, None], 0), axis=0
    )
    query_own = jnp.concatenate(
        [
            query_emb.reshape(query_dev * query_len, emb),
            jnp.broadcast_to(wanted.astype(BF16)[None], (EXTRA, emb)),
        ]
    )
    copies, query_own = lax.optimization_barrier(
        (passage_copies(passage_emb, lengths, dp_size), query_own)
    )
    passage_pack = exchange(copies, DP)
    queries = query_gathered(query_own)
    ids = jnp.broadcast_to((jnp.arange(dp_size) * neg_size + place).astype(F32)[:, None], (dp_size, emb))
    row, column = lax.axis_index("neg_1"), lax.axis_index("neg_0")
    flip = (row * 8 + column * 2 + core)[None]
    sides = [
        (own.astype(jnp.uint32), (1 - own).astype(jnp.uint32))
        for own in (row, column // 2, column % 2)
    ]
    queries, sides = lax.optimization_barrier((queries, sides))
    row_side, far_side, near_side = sides
    spread, mixed, query_rows, inverse, similar, stats = forward_tile(
        flip, *queries, passage_pack, ids, query_len
    )
    stats = exchange(stats, NEG)
    passage_parts, kept, given = backward_tile(
        core[None], neg_size, query_rows, spread, mixed, inverse, similar, stats, query_len
    )
    residual, kept, given = lax.optimization_barrier((residual, kept, given))
    early = early_rows(residual, context, out_proj)
    query_part = pair_summed(kept, given, CORE, SWAP, BF16)
    query_part = halves_summed(query_part, "neg_1", SWAP, row_side, F32)
    passage_parts = exchange(passage_parts, DP)
    passage_parts, query_part, early = lax.optimization_barrier((passage_parts, query_part, early))
    normed, inv_std, context_t = early
    residual_grad, kept, given, loss_sum = late_rows(
        core[None], dp_size, passage_parts, normed, inv_std, norm_gain[None], colbert_proj, context_t
    )
    half = pair_summed(kept, given, CORE, SWAP, BF16)
    context_grad = jnp.dot(residual_grad, out_proj.T, preferred_element_type=F32).astype(BF16)
    query_part = query_part.reshape(2, 2, *query_part.shape[1:])
    query_part = halves_summed(query_part, "neg_0", FAR, far_side, F32)
    slabs = exchange(half.reshape(dp_size * cross_size, *half.shape[2:]), DP + CROSS)
    slabs, context_grad, query_part = lax.optimization_barrier((slabs, context_grad, query_part))
    half = exchange(summed_copies(slabs), DP + CROSS).reshape(half.shape)
    half, query_part = lax.optimization_barrier((half, query_part))
    query_grad = halves_summed(query_part, "neg_0", NEAR, near_side, F32)
    query_grad = query_grad.reshape(query_dev, query_len, emb)
    other = lax.ppermute(half, CORE, SWAP)
    proj = own_rows(core[None], half, out_proj.shape[0])
    out_proj_grad, colbert_grad, gain_grad = finish(
        core[None], half, other, colbert_proj, norm_gain[None], proj
    )
    loss = loss_sum[0, 0] / (query_dev * dp_size * neg_size)
    return (
        loss,
        query_grad,
        residual_grad,
        context_grad,
        out_proj_grad,
        colbert_grad,
        gain_grad[0],
    )


def solution(mesh):
    split = Mesh(mesh.devices.reshape(mesh.shape["dp"] // 2, 2, 4, 2, 2), DP_NEG)
    placed = (
        P(DP_NEG, None, None),
        P(DP_NEG),
        P(DP_NEG, None, None),
        P(DP_NEG),
        P(DP_NEG, None),
        P(DP_NEG, None),
        P(),
        P(),
        P(),
    )
    return jax.shard_map(
        body,
        mesh=split,
        in_specs=placed,
        out_specs=(P(), P(DP_NEG, None, None), P(DP_NEG, None), P(DP_NEG, None), P(), P(), P()),
        check_vma=False,
    )
```

```python
import functools

import jax
import jax.numpy as jnp
from jax import lax
from jax.experimental import pallas as pl
from jax.experimental.pallas import tpu as pltpu
from jax.sharding import Mesh
from jax.sharding import PartitionSpec as P

DP = ("dp_0", "dp_1")
NEG = ("neg_0", "neg_1", "neg_2")
CROSS = ("neg_0", "neg_1")
CORE = "neg_2"
DP_NEG = DP + NEG
BF16 = jnp.bfloat16
F32 = jnp.float32
EXTRA = 8
LEAST = 256
MIB = 1 << 20


def dot(a, b, dims, precision=None):
    return lax.dot_general(a, b, (dims, ((), ())), precision=precision, preferred_element_type=F32)


def token_query(rows, queries, query_len, transposed=False):
    shape = (queries, rows) if transposed else (rows, queries)
    row = lax.broadcasted_iota(jnp.int32, shape, 1 if transposed else 0)
    query = lax.broadcasted_iota(jnp.int32, shape, 0 if transposed else 1)
    first = query * query_len
    return ((row >= first) & (row < first + query_len)).astype(F32)


def whole(shape):
    return pl.BlockSpec(shape, lambda *_: (0,) * len(shape))


def stored(k):
    core, row, near, far = k % 2, k // 2 % 2, k // 4 % 2, k // 8
    return row * 8 + far * 4 + near * 2 + core


def forward_kernel(
    query_len,
    group,
    flip_ref,
    near_ref,
    far_ref,
    p_ref,
    ids_ref,
    exp_ref,
    mix_ref,
    own_ref,
    inv_ref,
    sim_ref,
    stats_ref,
    rows_ref,
    length_ref,
):
    passage = pl.program_id(0)
    half, q_rows, width = near_ref.shape[0], near_ref.shape[1] - EXTRA, near_ref.shape[2]
    parts = 2 * half
    slots = p_ref.shape[1] - EXTRA
    count, rows = inv_ref.shape
    queries = rows // query_len
    chunk = group * q_rows
    steps = parts // group
    tokens = p_ref[0, :slots, :]
    length = p_ref[0, slots : slots + 1, :].astype(F32) + float(LEAST)
    length_ref[pl.ds(passage, 1), :] = length
    wide = jnp.concatenate([length] * ((slots - LEAST) // width), axis=1)
    position = lax.broadcasted_iota(jnp.int32, wide.shape, 1).astype(F32) + float(LEAST)
    bias = jnp.where(position < wide, 0.0, -1e30)
    lane = lax.broadcasted_iota(jnp.int32, (chunk, width), 1)

    @pl.when(passage == 0)
    def _():
        rows_ref[...] = jnp.zeros_like(rows_ref)
        for k in range(parts):
            at = stored(k) ^ flip_ref[0]
            spot = at % half
            own_ref[k * q_rows : (k + 1) * q_rows, :] = jnp.where(
                at < half, near_ref[spot, :q_rows, :], far_ref[spot, :q_rows, :]
            )

    def scores(step):
        block = own_ref[step * chunk : (step + 1) * chunk, :]
        return dot(block, tokens, ((1,), (1,)))

    ahead = scores(0)
    late = None
    for step in range(steps):
        now = ahead
        if step + 1 < steps:
            ahead = scores(step + 1)
        if late is not None:
            mix_ref[passage, pl.ds((step - 1) * chunk, chunk), :] = dot(late, tokens, ((1,), (0,)))
        sure, rest = now[:, :LEAST], now[:, LEAST:] + bias
        highest = jnp.maximum(
            jnp.max(sure, axis=1, keepdims=True), jnp.max(rest, axis=1, keepdims=True)
        )
        sure = jnp.exp(sure - highest)
        rest = jnp.exp(rest - highest)
        total = jnp.sum(sure, axis=1, keepdims=True) + jnp.sum(rest, axis=1, keepdims=True)
        late = jnp.concatenate([sure.astype(BF16), rest.astype(BF16)], axis=1)
        at = pl.ds(step * chunk, chunk)
        exp_ref[passage, at, :] = late
        rows_ref[at, :] = jnp.where(
            lane == passage,
            highest + jnp.log(total),
            jnp.where(lane == passage + width // 2, total, rows_ref[at, :]),
        )
    mix_ref[passage, pl.ds((steps - 1) * chunk, chunk), :] = dot(late, tokens, ((1,), (0,)))

    @pl.when(passage == pl.num_programs(0) - 1)
    def _():
        turned = rows_ref[...].T
        inv_ref[...] = 1.0 / turned[width // 2 : width // 2 + count]
        similar = dot(
            turned[:count], token_query(rows, queries, query_len), ((1,), (0,)), lax.Precision.HIGHEST
        )
        similar = similar - float(query_len) * jnp.log(length_ref[...])[:, :queries]
        wanted = jnp.sum(
            near_ref[:, q_rows, :].astype(F32) + far_ref[:, q_rows, :].astype(F32),
            axis=0,
            keepdims=True,
        )[:, :queries]
        hit = (wanted == ids_ref[:, :queries]).astype(F32)
        highest = jnp.max(similar, axis=0, keepdims=True)
        total = jnp.sum(jnp.exp(similar - highest), axis=0, keepdims=True)
        positive = jnp.sum(jnp.where(hit > 0.0, similar, 0.0), axis=0, keepdims=True)
        sim_ref[0] = similar
        sim_ref[1] = hit
        stats = jnp.concatenate([highest, total, positive, jnp.zeros((5, queries), F32)], axis=0)
        stats = jnp.concatenate([stats, jnp.zeros((8, width - queries), F32)], axis=1)
        stats_ref[...] = jnp.broadcast_to(stats[None], stats_ref.shape)


def forward_tile(flip, near, far, passage_pack, ids, query_len, group=8):
    half, q_rows, width = near.shape
    parts, q_rows = 2 * half, q_rows - EXTRA
    count, slots = passage_pack.shape[0], passage_pack.shape[1] - EXTRA
    rows = parts * q_rows
    queries = rows // query_len
    work = rows * slots * count
    return pl.pallas_call(
        functools.partial(forward_kernel, query_len, group),
        name="forward_tile",
        grid=(count,),
        in_specs=[
            pl.BlockSpec(memory_space=pltpu.SMEM),
            whole(near.shape),
            whole(far.shape),
            pl.BlockSpec((1, slots + EXTRA, width), lambda p: (p, 0, 0)),
            whole(ids.shape),
        ],
        out_specs=[
            pl.BlockSpec(memory_space=pltpu.VMEM),
            pl.BlockSpec(memory_space=pltpu.VMEM),
            pl.BlockSpec(memory_space=pltpu.VMEM),
            whole((count, rows)),
            whole((2, count, queries)),
            whole((parts, 8, width)),
        ],
        out_shape=[
            pltpu.VMEM((count, rows, slots), BF16),
            pltpu.VMEM((count, rows, width), F32),
            pltpu.VMEM((rows, width), BF16),
            jax.ShapeDtypeStruct((count, rows), F32),
            jax.ShapeDtypeStruct((2, count, queries), F32),
            jax.ShapeDtypeStruct((parts, 8, width), F32),
        ],
        scratch_shapes=[pltpu.VMEM((rows, width), F32), pltpu.VMEM((count, width), F32)],
        compiler_params=pltpu.CompilerParams(vmem_limit_bytes=16 * MIB),
        cost_estimate=pl.CostEstimate(
            flops=4 * work * width, transcendentals=work, bytes_accessed=4 * work
        ),
    )(flip, near, far, passage_pack, ids)


def split_lines(value):
    high = value.astype(BF16).astype(F32)
    low = (value - high).astype(BF16).astype(F32)
    last = value - high - low
    row = lax.broadcasted_iota(jnp.int32, value.shape, 0)
    lines = jnp.where(row == 0, high, jnp.where(row == 1, low, jnp.where(row == 2, last, 0.0)))
    return lines.astype(BF16)


def backward_kernel(
    query_len,
    parts,
    core_ref,
    own_ref,
    exp_ref,
    mix_ref,
    inv_ref,
    sim_ref,
    stats_ref,
    pg_ref,
    kept_ref,
    given_ref,
    qt,
    halves,
):
    count, rows, slots = exp_ref.shape
    width, q_rows = own_ref.shape[1], rows // parts
    queries = rows // query_len
    for k in range(parts):
        qt[:, k * q_rows : (k + 1) * q_rows] = own_ref[k * q_rows : (k + 1) * q_rows, :].T
    highest_of = stats_ref[:, 0, :queries]
    highest = jnp.max(highest_of, axis=0, keepdims=True)
    total = jnp.sum(
        stats_ref[:, 1, :queries] * jnp.exp(highest_of - highest), axis=0, keepdims=True
    )
    positive = jnp.sum(stats_ref[:, 2, :queries], axis=0, keepdims=True)
    log_total = highest + jnp.log(total)
    coefficient = jnp.exp(sim_ref[0] - log_total) - sim_ref[1]
    scale = inv_ref[...] * dot(
        coefficient,
        token_query(rows, queries, query_len, True),
        ((1,), (0,)),
        lax.Precision.HIGHEST,
    )
    lines = split_lines(
        jnp.broadcast_to(jnp.sum(log_total - positive, axis=1, keepdims=True), (EXTRA, width))
    )
    for p in range(count):
        weighted = (qt[...].astype(F32) * scale[p : p + 1]).astype(BF16)
        pg_ref[p, :slots, :] = dot(weighted, exp_ref[p], ((1,), (0,))).T.astype(BF16)
        pg_ref[p, slots:, :] = lines
    turned = jnp.concatenate([scale, jnp.zeros((width - count, rows), F32)], axis=0).T
    for k in range(parts):
        at = slice(k * q_rows, (k + 1) * q_rows)
        sums = mix_ref[0, at, :] * turned[at, :1]
        for p in range(1, count):
            sums += mix_ref[p, at, :] * turned[at, p : p + 1]
        halves[k % 2, k // 2 % 2, k // 4] = sums.astype(BF16)
    kept_ref[...] = halves[core_ref[0]]
    given_ref[...] = halves[1 - core_ref[0]]


def backward_tile(core, parts, own, spread, mixed, inverse, similar, stats, query_len):
    count, rows, slots = spread.shape
    q_rows, width = rows // parts, own.shape[1]
    work = rows * slots * count
    return pl.pallas_call(
        functools.partial(backward_kernel, query_len, parts),
        name="backward_tile",
        in_specs=[pl.BlockSpec(memory_space=pltpu.SMEM)]
        + [pl.BlockSpec(memory_space=pltpu.VMEM)] * 6,
        out_shape=[
            pltpu.HBM((count, slots + EXTRA, width), BF16),
            jax.ShapeDtypeStruct((2, parts // 4, q_rows, width), BF16),
            jax.ShapeDtypeStruct((2, parts // 4, q_rows, width), BF16),
        ],
        out_specs=[whole((count, slots + EXTRA, width))]
        + [whole((2, parts // 4, q_rows, width))] * 2,
        scratch_shapes=[
            pltpu.VMEM((width, rows), BF16),
            pltpu.VMEM((2, 2, parts // 4, q_rows, width), BF16),
        ],
        compiler_params=pltpu.CompilerParams(vmem_limit_bytes=16 * MIB),
        cost_estimate=pl.CostEstimate(
            flops=2 * work * width, transcendentals=0, bytes_accessed=3 * work
        ),
    )(core, own, spread, mixed, inverse, similar, stats)


def early_kernel(resid_ref, context_ref, proj_ref, normed_ref, inv_ref, context_t_ref):
    context = context_ref[...]
    hidden = resid_ref[...].astype(F32) + dot(context, proj_ref[...], ((1,), (0,)))
    centred = hidden - jnp.mean(hidden, axis=1, keepdims=True)
    variance = jnp.mean(centred * centred, axis=1, keepdims=True)
    inv_std = 1.0 / jnp.sqrt(variance + 1e-05)
    normed_ref[...] = centred * inv_std
    inv_ref[...] = jnp.broadcast_to(inv_std, inv_ref.shape)
    context_t_ref[...] = context.T


def early_rows(residual, context, out_proj, block=128):
    rows, width = residual.shape
    return pl.pallas_call(
        early_kernel,
        name="early_rows",
        grid=(rows // block,),
        in_specs=[
            pl.BlockSpec((block, width), lambda r: (r, 0)),
            pl.BlockSpec((block, width), lambda r: (r, 0)),
            whole(out_proj.shape),
        ],
        out_specs=[
            pl.BlockSpec((block, width), lambda r: (r, 0)),
            pl.BlockSpec((block, 128), lambda r: (r, 0)),
            pl.BlockSpec((width, block), lambda r: (0, r)),
        ],
        out_shape=[
            pltpu.HBM((rows, width), F32),
            pltpu.HBM((rows, 128), F32),
            pltpu.HBM((width, rows), BF16),
        ],
        compiler_params=pltpu.CompilerParams(vmem_limit_bytes=10 * MIB),
        cost_estimate=pl.CostEstimate(
            flops=2 * rows * width * width, transcendentals=0, bytes_accessed=10 * rows * width
        ),
    )(residual, context, out_proj)


def late_kernel(
    core_ref,
    parts_ref,
    normed_far,
    inv_far,
    gain_ref,
    colbert_ref,
    context_far,
    resid_ref,
    kept_ref,
    given_ref,
    loss_ref,
    normed_ref,
    inv_ref,
    context_t_ref,
    sums_ref,
    sems,
):
    loads = [
        pltpu.make_async_copy(far, near, sems.at[k])
        for k, (far, near) in enumerate(
            ((normed_far, normed_ref), (inv_far, inv_ref), (context_far, context_t_ref))
        )
    ]
    for load in loads:
        load.start()
    slots = parts_ref.shape[1] - EXTRA
    width = normed_ref.shape[1]
    total = parts_ref[0].astype(F32)
    for k in range(1, parts_ref.shape[0]):
        total = total + parts_ref[k].astype(F32)
    loss_ref[...] = jnp.broadcast_to(
        jnp.sum(total[slots:], axis=0, keepdims=True), loss_ref.shape
    )
    grad = total[:slots].astype(BF16)
    gain = gain_ref[...]
    gained = dot(grad, colbert_ref[...], ((1,), (1,))) * gain
    grad_t = grad.T
    for load in loads[:2]:
        load.wait()
    normed = normed_ref[...]
    inv_std = inv_ref[:, :1]
    resid = inv_std * (
        gained
        - jnp.mean(gained, axis=1, keepdims=True)
        - normed * jnp.mean(gained * normed, axis=1, keepdims=True)
    )
    resid = resid.astype(BF16)
    resid_ref[...] = resid
    scaled = (normed * gain).astype(BF16)
    blocks, lines = sums_ref.shape[1], sums_ref.shape[3]
    thin = grad.shape[1] // (2 * blocks)
    thick = lines - thin
    colbert = dot(grad_t, scaled, ((1,), (0,)))
    for k in range(2 * blocks):
        for j in range(width // 128):
            sums_ref[k // blocks, k % blocks, j, thick:, :] = colbert[
                k * thin : (k + 1) * thin, j * 128 : (j + 1) * 128
            ].astype(BF16)
    loads[2].wait()
    group = 4
    for first in range(0, 2 * blocks, group):
        part = dot(
            context_t_ref[first * thick : (first + group) * thick, :], resid, ((1,), (0,))
        ).astype(BF16)
        for k in range(first, first + group):
            at = (k - first) * thick
            for j in range(width // 128):
                sums_ref[k // blocks, k % blocks, j, :thick, :] = part[
                    at : at + thick, j * 128 : (j + 1) * 128
                ]
    kept_ref[...] = sums_ref[core_ref[0]]
    given_ref[...] = sums_ref[1 - core_ref[0]]


def far(array):
    return pltpu.with_memory_space_constraint(array, pltpu.HBM)


def late_rows(core, blocks, pieces, normed, inv_std, gain, colbert_proj, context_t):
    rows, width = normed.shape
    emb = colbert_proj.shape[1]
    shape = (blocks, width // 128, (width + emb) // (2 * blocks), 128)
    return pl.pallas_call(
        late_kernel,
        name="late_rows",
        in_specs=[
            pl.BlockSpec(memory_space=pltpu.SMEM),
            whole(pieces.shape),
            pl.BlockSpec(memory_space=pltpu.HBM),
            pl.BlockSpec(memory_space=pltpu.HBM),
            whole(gain.shape),
            whole(colbert_proj.shape),
            pl.BlockSpec(memory_space=pltpu.HBM),
        ],
        scratch_shapes=[
            pltpu.VMEM(normed.shape, F32),
            pltpu.VMEM(inv_std.shape, F32),
            pltpu.VMEM(context_t.shape, BF16),
            pltpu.VMEM((2, *shape), BF16),
            pltpu.SemaphoreType.DMA((3,)),
        ],
        out_shape=[
            jax.ShapeDtypeStruct((rows, width), BF16),
            jax.ShapeDtypeStruct(shape, BF16),
            jax.ShapeDtypeStruct(shape, BF16),
            jax.ShapeDtypeStruct((8, emb), F32),
        ],
        compiler_params=pltpu.CompilerParams(vmem_limit_bytes=24 * MIB),
        cost_estimate=pl.CostEstimate(
            flops=2 * rows * width * (width + 2 * emb),
            transcendentals=0,
            bytes_accessed=14 * rows * width,
        ),
    )(core, pieces, far(normed), far(inv_std), gain, colbert_proj, far(context_t))


def exchange(pieces, axis):
    return lax.all_to_all(pieces, axis, 0, 0, tiled=True)


def own_kernel(core_ref, half_ref, proj_ref):
    blocks, columns, _, block = half_ref.shape
    thick = proj_ref.shape[0] // blocks
    for k in range(blocks):
        for j in range(columns):
            proj_ref[k * thick : (k + 1) * thick, j * block : (j + 1) * block] = half_ref[
                k, j, :thick, :
            ].astype(F32)


def own_rows(core, half, width, group=4):
    blocks, columns, lines, block = half.shape
    return pl.pallas_call(
        own_kernel,
        name="own_rows",
        grid_spec=pltpu.PrefetchScalarGridSpec(
            num_scalar_prefetch=1,
            grid=(columns // group,),
            in_specs=[pl.BlockSpec((blocks, group, lines, block), lambda k, core: (0, k, 0, 0))],
            out_specs=pl.BlockSpec((width // 2, group * block), lambda k, core: (core[0], k)),
        ),
        out_shape=pltpu.HBM((width, width), F32),
        compiler_params=pltpu.CompilerParams(vmem_limit_bytes=12 * MIB),
        cost_estimate=pl.CostEstimate(
            flops=width * width, transcendentals=0, bytes_accessed=4 * width * width
        ),
    )(core, half)


def finish_kernel(
    core_ref, half_ref, other_ref, colbert_ref, gain_ref, _, proj_ref, grad_ref, gain_grad_ref
):
    blocks, columns, _, block = half_ref.shape
    thick = proj_ref.shape[0] // blocks
    even = core_ref[0] == 0
    for j in range(columns):
        at = slice(j * block, (j + 1) * block)
        own, others = [], []
        for k in range(blocks):
            piece = other_ref[k, j].astype(F32)
            proj_ref[k * thick : (k + 1) * thick, at] = piece[:thick]
            others.append(piece[thick:])
            own.append(half_ref[k, j].astype(F32)[thick:])
        own, others = jnp.concatenate(own, axis=0), jnp.concatenate(others, axis=0)
        colbert_grad = jnp.concatenate(
            [jnp.where(even, own, others), jnp.where(even, others, own)], axis=0
        )
        colbert_t = colbert_ref[at, :].astype(F32).T
        gain_grad_ref[:, at] = (
            jnp.sum(colbert_grad * colbert_t, axis=0, keepdims=True) / gain_ref[:, at]
        )
        grad_ref[at, :] = colbert_grad.T


def finish(core, half, other, colbert_proj, gain, proj, group=4):
    blocks, columns, lines, block = half.shape
    width, emb = colbert_proj.shape
    piece = pl.BlockSpec((blocks, group, lines, block), lambda k, core: (0, k, 0, 0))
    span = group * block
    return pl.pallas_call(
        finish_kernel,
        name="finish",
        grid_spec=pltpu.PrefetchScalarGridSpec(
            num_scalar_prefetch=1,
            grid=(columns // group,),
            in_specs=[
                piece,
                piece,
                pl.BlockSpec((span, emb), lambda k, core: (k, 0)),
                pl.BlockSpec((1, span), lambda k, core: (0, k)),
                pl.BlockSpec(memory_space=pl.ANY),
            ],
            out_specs=[
                pl.BlockSpec((width // 2, span), lambda k, core: (1 - core[0], k)),
                pl.BlockSpec((span, emb), lambda k, core: (k, 0)),
                pl.BlockSpec((1, span), lambda k, core: (0, k)),
            ],
        ),
        out_shape=[
            jax.ShapeDtypeStruct((width, width), F32),
            jax.ShapeDtypeStruct((width, emb), F32),
            jax.ShapeDtypeStruct((1, width), F32),
        ],
        input_output_aliases={5: 0},
        compiler_params=pltpu.CompilerParams(vmem_limit_bytes=12 * MIB),
        cost_estimate=pl.CostEstimate(
            flops=2 * width * width, transcendentals=0, bytes_accessed=4 * width * width
        ),
    )(core, half, other, colbert_proj, gain, proj)


SWAP = [(0, 1), (1, 0)]
FAR = [(k, k ^ 2) for k in range(4)]
NEAR = [(k, k ^ 1) for k in range(4)]


def pair_summed(kept, given, axis, pairs, out_type):
    taken = lax.ppermute(given, axis, pairs)
    return (kept.astype(F32) + taken.astype(F32)).astype(out_type)


def halves_summed(halves, axis, pairs, side, out_type):
    keep, give = side
    given = lax.dynamic_index_in_dim(halves, give, 0, False)
    kept = lax.dynamic_index_in_dim(halves, keep, 0, False)
    return pair_summed(kept, given, axis, pairs, out_type)


def query_gathered(own):
    held = own[None]
    for axis, pairs in ((CORE, SWAP), ("neg_0", NEAR), ("neg_0", FAR)):
        held = jnp.concatenate([held, lax.ppermute(held, axis, pairs)])
    return held, lax.ppermute(held, "neg_1", SWAP)


def sent_out(tile_ref, out_ref, sems):
    copies = [
        pltpu.make_async_copy(tile_ref, out_ref.at[k], sems.at[k]) for k in range(out_ref.shape[0])
    ]
    for copy in copies:
        copy.start()
    for copy in copies:
        copy.wait()


def pack_kernel(length_ref, p_ref, out_ref, tile_ref, sems):
    slots = p_ref.shape[1]
    tile_ref[:slots, :] = p_ref[0]
    tile_ref[slots:, :] = jnp.full(
        (EXTRA, p_ref.shape[2]), (length_ref[0] - LEAST).astype(F32)
    ).astype(BF16)
    sent_out(tile_ref, out_ref, sems)


def passage_copies(passage_emb, lengths, copies):
    _, slots, width = passage_emb.shape
    tile = (slots + EXTRA, width)
    return pl.pallas_call(
        pack_kernel,
        name="passage_copies",
        in_specs=[
            pl.BlockSpec(memory_space=pltpu.SMEM),
            pl.BlockSpec(memory_space=pltpu.VMEM),
        ],
        out_specs=pl.BlockSpec(memory_space=pltpu.HBM),
        out_shape=pltpu.HBM((copies, *tile), BF16),
        scratch_shapes=[pltpu.VMEM(tile, BF16), pltpu.SemaphoreType.DMA((copies,))],
    )(lengths, passage_emb)


def spread_kernel(parts_ref, out_ref):
    total = parts_ref[0].astype(F32)
    for k in range(1, parts_ref.shape[0]):
        total += parts_ref[k].astype(F32)
    out_ref[...] = jnp.broadcast_to(total.astype(BF16)[None], out_ref.shape)


def summed_copies(parts):
    return pl.pallas_call(
        spread_kernel,
        name="summed_copies",
        in_specs=[pl.BlockSpec(memory_space=pltpu.VMEM)],
        out_specs=pl.BlockSpec(memory_space=pltpu.VMEM),
        out_shape=pltpu.VMEM(parts.shape, BF16),
        compiler_params=pltpu.CompilerParams(vmem_limit_bytes=6 * MIB),
    )(parts)


def body(
    query_emb, positive, passage_emb, lengths, residual, context, out_proj, norm_gain, colbert_proj
):
    query_dev, query_len, emb = query_emb.shape
    neg_size, dp_size, cross_size = lax.axis_size(NEG), lax.axis_size(DP), lax.axis_size(CROSS)
    place, core = lax.axis_index(NEG), lax.axis_index(CORE)
    spot = jnp.arange(emb)[None] - place * query_dev
    wanted = jnp.sum(
        jnp.where(spot == jnp.arange(query_dev)[:, None], positive[:, None], 0), axis=0
    )
    query_own = jnp.concatenate(
        [
            query_emb.reshape(query_dev * query_len, emb),
            jnp.broadcast_to(wanted.astype(BF16)[None], (EXTRA, emb)),
        ]
    )
    copies, query_own = lax.optimization_barrier(
        (passage_copies(passage_emb, lengths, dp_size), query_own)
    )
    passage_pack = exchange(copies, DP)
    queries = query_gathered(query_own)
    ids = jnp.broadcast_to((jnp.arange(dp_size) * neg_size + place).astype(F32)[:, None], (dp_size, emb))
    row, column = lax.axis_index("neg_1"), lax.axis_index("neg_0")
    flip = (row * 8 + column * 2 + core)[None]
    sides = [
        (own.astype(jnp.uint32), (1 - own).astype(jnp.uint32))
        for own in (row, column // 2, column % 2)
    ]
    queries, sides = lax.optimization_barrier((queries, sides))
    row_side, far_side, near_side = sides
    spread, mixed, query_rows, inverse, similar, stats = forward_tile(
        flip, *queries, passage_pack, ids, query_len
    )
    stats = exchange(stats, NEG)
    passage_parts, kept, given = backward_tile(
        core[None], neg_size, query_rows, spread, mixed, inverse, similar, stats, query_len
    )
    residual, kept, given = lax.optimization_barrier((residual, kept, given))
    early = early_rows(residual, context, out_proj)
    query_part = pair_summed(kept, given, CORE, SWAP, BF16)
    passage_parts = exchange(passage_parts, DP)
    passage_parts, query_part, early = lax.optimization_barrier((passage_parts, query_part, early))
    normed, inv_std, context_t = early
    residual_grad, kept, given, loss_sum = late_rows(
        core[None], dp_size, passage_parts, normed, inv_std, norm_gain[None], colbert_proj, context_t
    )
    half = pair_summed(kept, given, CORE, SWAP, BF16)
    context_grad = jnp.dot(residual_grad, out_proj.T, preferred_element_type=F32).astype(BF16)
    query_part = halves_summed(query_part, "neg_1", SWAP, row_side, F32)
    half, query_part = lax.optimization_barrier((half, query_part))
    slabs = exchange(half.reshape(dp_size * cross_size, *half.shape[2:]), DP + CROSS)
    slabs, context_grad = lax.optimization_barrier((slabs, context_grad))
    half = exchange(summed_copies(slabs), DP + CROSS).reshape(half.shape)
    half, query_part = lax.optimization_barrier((half, query_part))
    query_part = query_part.reshape(2, 2, *query_part.shape[1:])
    query_part = halves_summed(query_part, "neg_0", FAR, far_side, F32)
    query_grad = halves_summed(query_part, "neg_0", NEAR, near_side, F32)
    query_grad = query_grad.reshape(query_dev, query_len, emb)
    other = lax.ppermute(half, CORE, SWAP)
    proj = own_rows(core[None], half, out_proj.shape[0])
    out_proj_grad, colbert_grad, gain_grad = finish(
        core[None], half, other, colbert_proj, norm_gain[None], proj
    )
    loss = loss_sum[0, 0] / (query_dev * dp_size * neg_size)
    return (
        loss,
        query_grad,
        residual_grad,
        context_grad,
        out_proj_grad,
        colbert_grad,
        gain_grad[0],
    )


def solution(mesh):
    split = Mesh(mesh.devices.reshape(mesh.shape["dp"] // 2, 2, 4, 2, 2), DP_NEG)
    placed = (
        P(DP_NEG, None, None),
        P(DP_NEG),
        P(DP_NEG, None, None),
        P(DP_NEG),
        P(DP_NEG, None),
        P(DP_NEG, None),
        P(),
        P(),
        P(),
    )
    return jax.shard_map(
        body,
        mesh=split,
        in_specs=placed,
        out_specs=(P(), P(DP_NEG, None, None), P(DP_NEG, None), P(DP_NEG, None), P(), P(), P()),
        check_vma=False,
    )
```

```python
import functools

import jax
import jax.numpy as jnp
from jax import lax
from jax.experimental import pallas as pl
from jax.experimental.pallas import tpu as pltpu
from jax.sharding import Mesh
from jax.sharding import PartitionSpec as P

DP = ("dp_0", "dp_1")
NEG = ("neg_0", "neg_1", "neg_2")
CROSS = ("neg_0", "neg_1")
CORE = "neg_2"
DP_NEG = DP + NEG
BF16 = jnp.bfloat16
F32 = jnp.float32
EXTRA = 8
LEAST = 256
MIB = 1 << 20


def dot(a, b, dims, precision=None):
    return lax.dot_general(a, b, (dims, ((), ())), precision=precision, preferred_element_type=F32)


def token_query(rows, queries, query_len, transposed=False):
    shape = (queries, rows) if transposed else (rows, queries)
    row = lax.broadcasted_iota(jnp.int32, shape, 1 if transposed else 0)
    query = lax.broadcasted_iota(jnp.int32, shape, 0 if transposed else 1)
    first = query * query_len
    return ((row >= first) & (row < first + query_len)).astype(F32)


def whole(shape):
    return pl.BlockSpec(shape, lambda *_: (0,) * len(shape))


def stored(k):
    core, row, near, far = k % 2, k // 2 % 2, k // 4 % 2, k // 8
    return row * 8 + far * 4 + near * 2 + core


def forward_kernel(
    query_len,
    group,
    flip_ref,
    near_ref,
    far_ref,
    p_ref,
    ids_ref,
    exp_ref,
    mix_ref,
    own_ref,
    inv_ref,
    sim_ref,
    stats_ref,
    rows_ref,
    length_ref,
):
    passage = pl.program_id(0)
    half, q_rows, width = near_ref.shape[0], near_ref.shape[1] - EXTRA, near_ref.shape[2]
    parts = 2 * half
    slots = p_ref.shape[1] - EXTRA
    count, rows = inv_ref.shape
    queries = rows // query_len
    chunk = group * q_rows
    steps = parts // group
    tokens = p_ref[0, :slots, :]
    length = p_ref[0, slots : slots + 1, :].astype(F32) + float(LEAST)
    length_ref[pl.ds(passage, 1), :] = length
    wide = jnp.concatenate([length] * ((slots - LEAST) // width), axis=1)
    position = lax.broadcasted_iota(jnp.int32, wide.shape, 1).astype(F32) + float(LEAST)
    bias = jnp.where(position < wide, 0.0, -1e30)
    lane = lax.broadcasted_iota(jnp.int32, (chunk, width), 1)

    @pl.when(passage == 0)
    def _():
        rows_ref[...] = jnp.zeros_like(rows_ref)
        for k in range(parts):
            at = stored(k) ^ flip_ref[0]
            spot = at % half
            own_ref[k * q_rows : (k + 1) * q_rows, :] = jnp.where(
                at < half, near_ref[spot, :q_rows, :], far_ref[spot, :q_rows, :]
            )

    def scores(step):
        block = own_ref[step * chunk : (step + 1) * chunk, :]
        return dot(block, tokens, ((1,), (1,)))

    ahead = scores(0)
    late = None
    for step in range(steps):
        now = ahead
        if step + 1 < steps:
            ahead = scores(step + 1)
        if late is not None:
            mix_ref[passage, pl.ds((step - 1) * chunk, chunk), :] = dot(late, tokens, ((1,), (0,)))
        sure, rest = now[:, :LEAST], now[:, LEAST:] + bias
        highest = jnp.maximum(
            jnp.max(sure, axis=1, keepdims=True), jnp.max(rest, axis=1, keepdims=True)
        )
        sure = jnp.exp(sure - highest)
        rest = jnp.exp(rest - highest)
        total = jnp.sum(sure, axis=1, keepdims=True) + jnp.sum(rest, axis=1, keepdims=True)
        late = jnp.concatenate([sure.astype(BF16), rest.astype(BF16)], axis=1)
        at = pl.ds(step * chunk, chunk)
        exp_ref[passage, at, :] = late
        rows_ref[at, :] = jnp.where(
            lane == passage,
            highest + jnp.log(total),
            jnp.where(lane == passage + width // 2, total, rows_ref[at, :]),
        )
    mix_ref[passage, pl.ds((steps - 1) * chunk, chunk), :] = dot(late, tokens, ((1,), (0,)))

    @pl.when(passage == pl.num_programs(0) - 1)
    def _():
        turned = rows_ref[...].T
        inv_ref[...] = 1.0 / turned[width // 2 : width // 2 + count]
        similar = dot(
            turned[:count], token_query(rows, queries, query_len), ((1,), (0,)), lax.Precision.HIGHEST
        )
        similar = similar - float(query_len) * jnp.log(length_ref[...])[:, :queries]
        wanted = jnp.sum(
            near_ref[:, q_rows, :].astype(F32) + far_ref[:, q_rows, :].astype(F32),
            axis=0,
            keepdims=True,
        )[:, :queries]
        hit = (wanted == ids_ref[:, :queries]).astype(F32)
        highest = jnp.max(similar, axis=0, keepdims=True)
        total = jnp.sum(jnp.exp(similar - highest), axis=0, keepdims=True)
        positive = jnp.sum(jnp.where(hit > 0.0, similar, 0.0), axis=0, keepdims=True)
        sim_ref[0] = similar
        sim_ref[1] = hit
        stats = jnp.concatenate([highest, total, positive, jnp.zeros((5, queries), F32)], axis=0)
        stats = jnp.concatenate([stats, jnp.zeros((8, width - queries), F32)], axis=1)
        stats_ref[...] = jnp.broadcast_to(stats[None], stats_ref.shape)


def forward_tile(flip, near, far, passage_pack, ids, query_len, group=8):
    half, q_rows, width = near.shape
    parts, q_rows = 2 * half, q_rows - EXTRA
    count, slots = passage_pack.shape[0], passage_pack.shape[1] - EXTRA
    rows = parts * q_rows
    queries = rows // query_len
    work = rows * slots * count
    return pl.pallas_call(
        functools.partial(forward_kernel, query_len, group),
        name="forward_tile",
        grid=(count,),
        in_specs=[
            pl.BlockSpec(memory_space=pltpu.SMEM),
            whole(near.shape),
            whole(far.shape),
            pl.BlockSpec((1, slots + EXTRA, width), lambda p: (p, 0, 0)),
            whole(ids.shape),
        ],
        out_specs=[
            pl.BlockSpec(memory_space=pltpu.VMEM),
            pl.BlockSpec(memory_space=pltpu.VMEM),
            pl.BlockSpec(memory_space=pltpu.VMEM),
            whole((count, rows)),
            whole((2, count, queries)),
            whole((parts, 8, width)),
        ],
        out_shape=[
            pltpu.VMEM((count, rows, slots), BF16),
            pltpu.VMEM((count, rows, width), F32),
            pltpu.VMEM((rows, width), BF16),
            jax.ShapeDtypeStruct((count, rows), F32),
            jax.ShapeDtypeStruct((2, count, queries), F32),
            jax.ShapeDtypeStruct((parts, 8, width), F32),
        ],
        scratch_shapes=[pltpu.VMEM((rows, width), F32), pltpu.VMEM((count, width), F32)],
        compiler_params=pltpu.CompilerParams(vmem_limit_bytes=16 * MIB),
        cost_estimate=pl.CostEstimate(
            flops=4 * work * width, transcendentals=work, bytes_accessed=4 * work
        ),
    )(flip, near, far, passage_pack, ids)


def split_lines(value):
    high = value.astype(BF16).astype(F32)
    low = (value - high).astype(BF16).astype(F32)
    last = value - high - low
    row = lax.broadcasted_iota(jnp.int32, value.shape, 0)
    lines = jnp.where(row == 0, high, jnp.where(row == 1, low, jnp.where(row == 2, last, 0.0)))
    return lines.astype(BF16)


def backward_kernel(
    query_len,
    parts,
    core_ref,
    own_ref,
    exp_ref,
    mix_ref,
    inv_ref,
    sim_ref,
    stats_ref,
    pg_ref,
    kept_ref,
    given_ref,
    qt,
    halves,
):
    count, rows, slots = exp_ref.shape
    width, q_rows = own_ref.shape[1], rows // parts
    queries = rows // query_len
    for k in range(parts):
        qt[:, k * q_rows : (k + 1) * q_rows] = own_ref[k * q_rows : (k + 1) * q_rows, :].T
    highest_of = stats_ref[:, 0, :queries]
    highest = jnp.max(highest_of, axis=0, keepdims=True)
    total = jnp.sum(
        stats_ref[:, 1, :queries] * jnp.exp(highest_of - highest), axis=0, keepdims=True
    )
    positive = jnp.sum(stats_ref[:, 2, :queries], axis=0, keepdims=True)
    log_total = highest + jnp.log(total)
    coefficient = jnp.exp(sim_ref[0] - log_total) - sim_ref[1]
    scale = inv_ref[...] * dot(
        coefficient,
        token_query(rows, queries, query_len, True),
        ((1,), (0,)),
        lax.Precision.HIGHEST,
    )
    lines = split_lines(
        jnp.broadcast_to(jnp.sum(log_total - positive, axis=1, keepdims=True), (EXTRA, width))
    )
    for p in range(count):
        weighted = (qt[...].astype(F32) * scale[p : p + 1]).astype(BF16)
        pg_ref[p, :slots, :] = dot(weighted, exp_ref[p], ((1,), (0,))).T.astype(BF16)
        pg_ref[p, slots:, :] = lines
    turned = jnp.concatenate([scale, jnp.zeros((width - count, rows), F32)], axis=0).T
    for k in range(parts):
        at = slice(k * q_rows, (k + 1) * q_rows)
        sums = mix_ref[0, at, :] * turned[at, :1]
        for p in range(1, count):
            sums += mix_ref[p, at, :] * turned[at, p : p + 1]
        halves[k % 2, k // 2 % 2, k // 4] = sums.astype(BF16)
    kept_ref[...] = halves[core_ref[0]]
    given_ref[...] = halves[1 - core_ref[0]]


def backward_tile(core, parts, own, spread, mixed, inverse, similar, stats, query_len):
    count, rows, slots = spread.shape
    q_rows, width = rows // parts, own.shape[1]
    work = rows * slots * count
    return pl.pallas_call(
        functools.partial(backward_kernel, query_len, parts),
        name="backward_tile",
        in_specs=[pl.BlockSpec(memory_space=pltpu.SMEM)]
        + [pl.BlockSpec(memory_space=pltpu.VMEM)] * 6,
        out_shape=[
            pltpu.HBM((count, slots + EXTRA, width), BF16),
            jax.ShapeDtypeStruct((2, parts // 4, q_rows, width), BF16),
            jax.ShapeDtypeStruct((2, parts // 4, q_rows, width), BF16),
        ],
        out_specs=[whole((count, slots + EXTRA, width))]
        + [whole((2, parts // 4, q_rows, width))] * 2,
        scratch_shapes=[
            pltpu.VMEM((width, rows), BF16),
            pltpu.VMEM((2, 2, parts // 4, q_rows, width), BF16),
        ],
        compiler_params=pltpu.CompilerParams(vmem_limit_bytes=16 * MIB),
        cost_estimate=pl.CostEstimate(
            flops=2 * work * width, transcendentals=0, bytes_accessed=3 * work
        ),
    )(core, own, spread, mixed, inverse, similar, stats)


def early_kernel(resid_ref, context_ref, proj_ref, normed_ref, inv_ref, context_t_ref):
    context = context_ref[...]
    hidden = resid_ref[...].astype(F32) + dot(context, proj_ref[...], ((1,), (0,)))
    centred = hidden - jnp.mean(hidden, axis=1, keepdims=True)
    variance = jnp.mean(centred * centred, axis=1, keepdims=True)
    inv_std = 1.0 / jnp.sqrt(variance + 1e-05)
    normed_ref[...] = centred * inv_std
    inv_ref[...] = jnp.broadcast_to(inv_std, inv_ref.shape)
    context_t_ref[...] = context.T


def early_rows(residual, context, out_proj, block=128):
    rows, width = residual.shape
    return pl.pallas_call(
        early_kernel,
        name="early_rows",
        grid=(rows // block,),
        in_specs=[
            pl.BlockSpec((block, width), lambda r: (r, 0)),
            pl.BlockSpec((block, width), lambda r: (r, 0)),
            whole(out_proj.shape),
        ],
        out_specs=[
            pl.BlockSpec((block, width), lambda r: (r, 0)),
            pl.BlockSpec((block, 128), lambda r: (r, 0)),
            pl.BlockSpec((width, block), lambda r: (0, r)),
        ],
        out_shape=[
            pltpu.HBM((rows, width), F32),
            pltpu.HBM((rows, 128), F32),
            pltpu.HBM((width, rows), BF16),
        ],
        compiler_params=pltpu.CompilerParams(vmem_limit_bytes=10 * MIB),
        cost_estimate=pl.CostEstimate(
            flops=2 * rows * width * width, transcendentals=0, bytes_accessed=10 * rows * width
        ),
    )(residual, context, out_proj)


def late_kernel(
    core_ref,
    parts_ref,
    normed_far,
    inv_far,
    gain_ref,
    colbert_ref,
    context_far,
    resid_ref,
    kept_ref,
    given_ref,
    loss_ref,
    normed_ref,
    inv_ref,
    context_t_ref,
    sums_ref,
    sems,
):
    loads = [
        pltpu.make_async_copy(far, near, sems.at[k])
        for k, (far, near) in enumerate(
            ((normed_far, normed_ref), (inv_far, inv_ref), (context_far, context_t_ref))
        )
    ]
    for load in loads:
        load.start()
    slots = parts_ref.shape[1] - EXTRA
    width = normed_ref.shape[1]
    total = parts_ref[0].astype(F32)
    for k in range(1, parts_ref.shape[0]):
        total = total + parts_ref[k].astype(F32)
    loss_ref[...] = jnp.broadcast_to(
        jnp.sum(total[slots:], axis=0, keepdims=True), loss_ref.shape
    )
    grad = total[:slots].astype(BF16)
    gain = gain_ref[...]
    gained = dot(grad, colbert_ref[...], ((1,), (1,))) * gain
    grad_t = grad.T
    for load in loads[:2]:
        load.wait()
    normed = normed_ref[...]
    inv_std = inv_ref[:, :1]
    resid = inv_std * (
        gained
        - jnp.mean(gained, axis=1, keepdims=True)
        - normed * jnp.mean(gained * normed, axis=1, keepdims=True)
    )
    resid = resid.astype(BF16)
    resid_ref[...] = resid
    scaled = (normed * gain).astype(BF16)
    blocks, lines = sums_ref.shape[1], sums_ref.shape[3]
    thin = grad.shape[1] // (2 * blocks)
    thick = lines - thin
    colbert = dot(grad_t, scaled, ((1,), (0,)))
    for k in range(2 * blocks):
        for j in range(width // 128):
            sums_ref[k // blocks, k % blocks, j, thick:, :] = colbert[
                k * thin : (k + 1) * thin, j * 128 : (j + 1) * 128
            ].astype(BF16)
    loads[2].wait()
    group = 4
    for first in range(0, 2 * blocks, group):
        part = dot(
            context_t_ref[first * thick : (first + group) * thick, :], resid, ((1,), (0,))
        ).astype(BF16)
        for k in range(first, first + group):
            at = (k - first) * thick
            for j in range(width // 128):
                sums_ref[k // blocks, k % blocks, j, :thick, :] = part[
                    at : at + thick, j * 128 : (j + 1) * 128
                ]
    kept_ref[...] = sums_ref[core_ref[0]]
    given_ref[...] = sums_ref[1 - core_ref[0]]


def far(array):
    return pltpu.with_memory_space_constraint(array, pltpu.HBM)


def late_rows(core, blocks, pieces, normed, inv_std, gain, colbert_proj, context_t):
    rows, width = normed.shape
    emb = colbert_proj.shape[1]
    shape = (blocks, width // 128, (width + emb) // (2 * blocks), 128)
    return pl.pallas_call(
        late_kernel,
        name="late_rows",
        in_specs=[
            pl.BlockSpec(memory_space=pltpu.SMEM),
            whole(pieces.shape),
            pl.BlockSpec(memory_space=pltpu.HBM),
            pl.BlockSpec(memory_space=pltpu.HBM),
            whole(gain.shape),
            whole(colbert_proj.shape),
            pl.BlockSpec(memory_space=pltpu.HBM),
        ],
        scratch_shapes=[
            pltpu.VMEM(normed.shape, F32),
            pltpu.VMEM(inv_std.shape, F32),
            pltpu.VMEM(context_t.shape, BF16),
            pltpu.VMEM((2, *shape), BF16),
            pltpu.SemaphoreType.DMA((3,)),
        ],
        out_shape=[
            jax.ShapeDtypeStruct((rows, width), BF16),
            jax.ShapeDtypeStruct(shape, BF16),
            jax.ShapeDtypeStruct(shape, BF16),
            jax.ShapeDtypeStruct((8, emb), F32),
        ],
        compiler_params=pltpu.CompilerParams(vmem_limit_bytes=24 * MIB),
        cost_estimate=pl.CostEstimate(
            flops=2 * rows * width * (width + 2 * emb),
            transcendentals=0,
            bytes_accessed=14 * rows * width,
        ),
    )(core, pieces, far(normed), far(inv_std), gain, colbert_proj, far(context_t))


def exchange(pieces, axis):
    return lax.all_to_all(pieces, axis, 0, 0, tiled=True)


def own_kernel(core_ref, half_ref, proj_ref):
    blocks, columns, _, block = half_ref.shape
    thick = proj_ref.shape[0] // blocks
    for k in range(blocks):
        for j in range(columns):
            proj_ref[k * thick : (k + 1) * thick, j * block : (j + 1) * block] = half_ref[
                k, j, :thick, :
            ].astype(F32)


def own_rows(core, half, width, group=4):
    blocks, columns, lines, block = half.shape
    return pl.pallas_call(
        own_kernel,
        name="own_rows",
        grid_spec=pltpu.PrefetchScalarGridSpec(
            num_scalar_prefetch=1,
            grid=(columns // group,),
            in_specs=[pl.BlockSpec((blocks, group, lines, block), lambda k, core: (0, k, 0, 0))],
            out_specs=pl.BlockSpec((width // 2, group * block), lambda k, core: (core[0], k)),
        ),
        out_shape=pltpu.HBM((width, width), F32),
        compiler_params=pltpu.CompilerParams(vmem_limit_bytes=12 * MIB),
        cost_estimate=pl.CostEstimate(
            flops=width * width, transcendentals=0, bytes_accessed=4 * width * width
        ),
    )(core, half)


def finish_kernel(
    core_ref, half_ref, other_ref, colbert_ref, gain_ref, _, proj_ref, grad_ref, gain_grad_ref
):
    blocks, columns, _, block = half_ref.shape
    thick = proj_ref.shape[0] // blocks
    even = core_ref[0] == 0
    for j in range(columns):
        at = slice(j * block, (j + 1) * block)
        own, others = [], []
        for k in range(blocks):
            piece = other_ref[k, j].astype(F32)
            proj_ref[k * thick : (k + 1) * thick, at] = piece[:thick]
            others.append(piece[thick:])
            own.append(half_ref[k, j].astype(F32)[thick:])
        own, others = jnp.concatenate(own, axis=0), jnp.concatenate(others, axis=0)
        colbert_grad = jnp.concatenate(
            [jnp.where(even, own, others), jnp.where(even, others, own)], axis=0
        )
        colbert_t = colbert_ref[at, :].astype(F32).T
        gain_grad_ref[:, at] = (
            jnp.sum(colbert_grad * colbert_t, axis=0, keepdims=True) / gain_ref[:, at]
        )
        grad_ref[at, :] = colbert_grad.T


def finish(core, half, other, colbert_proj, gain, proj, group=4):
    blocks, columns, lines, block = half.shape
    width, emb = colbert_proj.shape
    piece = pl.BlockSpec((blocks, group, lines, block), lambda k, core: (0, k, 0, 0))
    span = group * block
    return pl.pallas_call(
        finish_kernel,
        name="finish",
        grid_spec=pltpu.PrefetchScalarGridSpec(
            num_scalar_prefetch=1,
            grid=(columns // group,),
            in_specs=[
                piece,
                piece,
                pl.BlockSpec((span, emb), lambda k, core: (k, 0)),
                pl.BlockSpec((1, span), lambda k, core: (0, k)),
                pl.BlockSpec(memory_space=pl.ANY),
            ],
            out_specs=[
                pl.BlockSpec((width // 2, span), lambda k, core: (1 - core[0], k)),
                pl.BlockSpec((span, emb), lambda k, core: (k, 0)),
                pl.BlockSpec((1, span), lambda k, core: (0, k)),
            ],
        ),
        out_shape=[
            jax.ShapeDtypeStruct((width, width), F32),
            jax.ShapeDtypeStruct((width, emb), F32),
            jax.ShapeDtypeStruct((1, width), F32),
        ],
        input_output_aliases={5: 0},
        compiler_params=pltpu.CompilerParams(vmem_limit_bytes=12 * MIB),
        cost_estimate=pl.CostEstimate(
            flops=2 * width * width, transcendentals=0, bytes_accessed=4 * width * width
        ),
    )(core, half, other, colbert_proj, gain, proj)


SWAP = [(0, 1), (1, 0)]
FAR = [(k, k ^ 2) for k in range(4)]
NEAR = [(k, k ^ 1) for k in range(4)]


def pair_summed(kept, given, axis, pairs, out_type):
    taken = lax.ppermute(given, axis, pairs)
    return (kept.astype(F32) + taken.astype(F32)).astype(out_type)


def halves_summed(halves, axis, pairs, side, out_type):
    keep, give = side
    given = lax.dynamic_index_in_dim(halves, give, 0, False)
    kept = lax.dynamic_index_in_dim(halves, keep, 0, False)
    return pair_summed(kept, given, axis, pairs, out_type)


def query_gathered(own):
    held = own[None]
    for axis, pairs in ((CORE, SWAP), ("neg_0", NEAR), ("neg_0", FAR)):
        held = jnp.concatenate([held, lax.ppermute(held, axis, pairs)])
    return held, lax.ppermute(held, "neg_1", SWAP)


def sent_out(tile_ref, out_ref, sems):
    copies = [
        pltpu.make_async_copy(tile_ref, out_ref.at[k], sems.at[k]) for k in range(out_ref.shape[0])
    ]
    for copy in copies:
        copy.start()
    for copy in copies:
        copy.wait()


def pack_kernel(length_ref, p_ref, out_ref, tile_ref, sems):
    slots = p_ref.shape[1]
    tile_ref[:slots, :] = p_ref[0]
    tile_ref[slots:, :] = jnp.full(
        (EXTRA, p_ref.shape[2]), (length_ref[0] - LEAST).astype(F32)
    ).astype(BF16)
    sent_out(tile_ref, out_ref, sems)


def passage_copies(passage_emb, lengths, copies):
    _, slots, width = passage_emb.shape
    tile = (slots + EXTRA, width)
    return pl.pallas_call(
        pack_kernel,
        name="passage_copies",
        in_specs=[
            pl.BlockSpec(memory_space=pltpu.SMEM),
            pl.BlockSpec(memory_space=pltpu.VMEM),
        ],
        out_specs=pl.BlockSpec(memory_space=pltpu.HBM),
        out_shape=pltpu.HBM((copies, *tile), BF16),
        scratch_shapes=[pltpu.VMEM(tile, BF16), pltpu.SemaphoreType.DMA((copies,))],
    )(lengths, passage_emb)


def spread_kernel(parts_ref, out_ref):
    total = parts_ref[0].astype(F32)
    for k in range(1, parts_ref.shape[0]):
        total += parts_ref[k].astype(F32)
    out_ref[...] = jnp.broadcast_to(total.astype(BF16)[None], out_ref.shape)


def summed_copies(parts):
    return pl.pallas_call(
        spread_kernel,
        name="summed_copies",
        in_specs=[pl.BlockSpec(memory_space=pltpu.VMEM)],
        out_specs=pl.BlockSpec(memory_space=pltpu.VMEM),
        out_shape=pltpu.VMEM(parts.shape, BF16),
        compiler_params=pltpu.CompilerParams(vmem_limit_bytes=6 * MIB),
    )(parts)


def body(
    query_emb, positive, passage_emb, lengths, residual, context, out_proj, norm_gain, colbert_proj
):
    query_dev, query_len, emb = query_emb.shape
    neg_size, dp_size, cross_size = lax.axis_size(NEG), lax.axis_size(DP), lax.axis_size(CROSS)
    place, core = lax.axis_index(NEG), lax.axis_index(CORE)
    spot = jnp.arange(emb)[None] - place * query_dev
    wanted = jnp.sum(
        jnp.where(spot == jnp.arange(query_dev)[:, None], positive[:, None], 0), axis=0
    )
    query_own = jnp.concatenate(
        [
            query_emb.reshape(query_dev * query_len, emb),
            jnp.broadcast_to(wanted.astype(BF16)[None], (EXTRA, emb)),
        ]
    )
    copies, query_own = lax.optimization_barrier(
        (passage_copies(passage_emb, lengths, dp_size), query_own)
    )
    passage_pack = exchange(copies, DP)
    queries = query_gathered(query_own)
    ids = jnp.broadcast_to((jnp.arange(dp_size) * neg_size + place).astype(F32)[:, None], (dp_size, emb))
    row, column = lax.axis_index("neg_1"), lax.axis_index("neg_0")
    flip = (row * 8 + column * 2 + core)[None]
    sides = [
        (own.astype(jnp.uint32), (1 - own).astype(jnp.uint32))
        for own in (row, column // 2, column % 2)
    ]
    queries, sides = lax.optimization_barrier((queries, sides))
    row_side, far_side, near_side = sides
    spread, mixed, query_rows, inverse, similar, stats = forward_tile(
        flip, *queries, passage_pack, ids, query_len
    )
    stats = exchange(stats, NEG)
    passage_parts, kept, given = backward_tile(
        core[None], neg_size, query_rows, spread, mixed, inverse, similar, stats, query_len
    )
    residual, kept, given = lax.optimization_barrier((residual, kept, given))
    early = early_rows(residual, context, out_proj)
    query_part = pair_summed(kept, given, CORE, SWAP, BF16)
    query_part = halves_summed(query_part, "neg_1", SWAP, row_side, BF16)
    passage_parts = exchange(passage_parts, DP)
    passage_parts, query_part, early = lax.optimization_barrier((passage_parts, query_part, early))
    normed, inv_std, context_t = early
    residual_grad, kept, given, loss_sum = late_rows(
        core[None], dp_size, passage_parts, normed, inv_std, norm_gain[None], colbert_proj, context_t
    )
    half = pair_summed(kept, given, CORE, SWAP, BF16)
    context_grad = jnp.dot(residual_grad, out_proj.T, preferred_element_type=F32).astype(BF16)
    query_part = query_part.reshape(2, 2, *query_part.shape[1:])
    query_part = halves_summed(query_part, "neg_0", FAR, far_side, F32)
    slabs = exchange(half.reshape(dp_size * cross_size, *half.shape[2:]), DP + CROSS)
    slabs, context_grad, query_part = lax.optimization_barrier((slabs, context_grad, query_part))
    half = exchange(summed_copies(slabs), DP + CROSS).reshape(half.shape)
    half, query_part = lax.optimization_barrier((half, query_part))
    query_grad = halves_summed(query_part, "neg_0", NEAR, near_side, F32)
    query_grad = query_grad.reshape(query_dev, query_len, emb)
    other = lax.ppermute(half, CORE, SWAP)
    proj = own_rows(core[None], half, out_proj.shape[0])
    out_proj_grad, colbert_grad, gain_grad = finish(
        core[None], half, other, colbert_proj, norm_gain[None], proj
    )
    loss = loss_sum[0, 0] / (query_dev * dp_size * neg_size)
    return (
        loss,
        query_grad,
        residual_grad,
        context_grad,
        out_proj_grad,
        colbert_grad,
        gain_grad[0],
    )


def solution(mesh):
    split = Mesh(mesh.devices.reshape(mesh.shape["dp"] // 2, 2, 4, 2, 2), DP_NEG)
    placed = (
        P(DP_NEG, None, None),
        P(DP_NEG),
        P(DP_NEG, None, None),
        P(DP_NEG),
        P(DP_NEG, None),
        P(DP_NEG, None),
        P(),
        P(),
        P(),
    )
    return jax.shard_map(
        body,
        mesh=split,
        in_specs=placed,
        out_specs=(P(), P(DP_NEG, None, None), P(DP_NEG, None), P(DP_NEG, None), P(), P(), P()),
        check_vma=False,
    )
```
